32 devices in a mesh: lat: 4 (over y, x), lon: 8 (over z, core).
Axes of the slice: x: 2, y: 2, z: 4, core: 2. Of those that a mesh axis runs over, the one named last changes fastest.
Arguments:
- control: float32 [548, 32, 1024], P(None, 'lat', 'lon'), may hold values from -6 to 6
- std_dev: float32 [548], replicated, may hold values from 0.3 to 3
- col_dev: int32 [3072, 1], P(('lat', 'lon')), may hold values from 0 to 31; in each aligned block of 96 rows (0 to 95, 96 to 191, ...) at most 6 rows name the same one
- col_cell: int32 [3072], P(('lat', 'lon')), may hold values from 0 to 1023
- jacobian: bfloat16 [3072, 150, 548], P(('lat', 'lon')), may hold values from -0.25 to 0.25
- innovation: float32 [3072, 150], P(('lat', 'lon')), may hold values from -6 to 6
- inv_error: float32 [150], replicated, may hold values from 0.3 to 3
Outputs:
- departures: float32 [3072, 150], P(('lat', 'lon'))
- increment: float32 [548, 32, 1024], P(None, 'lat', 'lon')
- adjoint: float32 [548, 32, 1024], P(None, 'lat', 'lon')
The draws below stay inside these ranges and needn't reach their ends.
Inputs may be any that keep to these rules, and one draw needn't show every extreme that they name: `col_dev`: among the soundings of one device (aligned blocks of 96 rows) at most 6 name the same device, and in every draw some device is named exactly 6 times by one block.
All inputs are finite; a program needn't handle non-finite values.
Results may differ from the reference program's by a relative error of at most 0.0025.
Values may be sent and summed in bfloat16 or wider, within the bound.
A program may use at most 128 MiB of HBM per device.

```python
import math
import jax
import jax.numpy as jnp
import numpy as np
from jax import lax

COL = 548
CH = 150
TLAT = 8
TLON = 128
LHALF = 8
S_DEV = 96
CAP = 6
NLAT = 32
NLON = 1024
SOUND = 3072
N_LAT = 4
N_LON = 8
DEVICES = 32


def place_ends(result, stream_key, low, top_value):
    shape = result.shape
    index_at = [jax.random.randint(jax.random.fold_in(stream_key, axis), (), 0, shape[axis]) for axis in range(len(shape))]
    result = result.at[tuple(index_at)].set(low)
    longest = shape.index(max(shape))
    index_at[longest] = (index_at[longest] + 1) % shape[longest]
    return result.at[tuple(index_at)].set(top_value)


def levels(stream_key, dims, pieces, low, largest):
    level, own = 1.0, jax.random.fold_in(stream_key, 6)
    for axis_at, shards_of in pieces:
        steps = jnp.exp(jax.random.uniform(jax.random.fold_in(own, axis_at), (shards_of,), jnp.float32, low / len(pieces), largest / len(pieces)))
        level = level * jnp.repeat(steps, dims[axis_at] // shards_of).reshape([-1 if axis == axis_at else 1 for axis in range(len(dims))])
    return level


def routed_block(rng, own, number, rows, amount, top, most, lean):
    ranking = jax.random.permutation(rng, amount)
    packed, ordinary = shares(amount, rows * top, most, lean, True), shares(amount, rows * top, most, lean, False)
    places = jnp.arange(amount)

    def named(tallies, rotation):
        used = int((tallies > 0).sum())
        fixed = max(1, used // 4)
        shifted = fixed + (places - fixed + rotation * (used - fixed)) % max(1, amount - fixed)
        return jnp.zeros((amount,), jnp.int32).at[ranking[jnp.where(places < fixed, places, shifted)]].set(jnp.asarray(tallies, jnp.int32))

    tallies = jnp.where(number % 4 == 0, named(packed, number // 4), named(ordinary, number - number // 4 - 1))
    mixed = jax.random.permutation(jax.random.fold_in(own, 3), amount)
    giver, receiver = mixed[0:amount // 2 * 2:2], mixed[1:amount // 2 * 2:2]
    margin = jnp.minimum(tallies[giver] - 1, most - tallies[receiver]) // 2
    margin = jnp.where((giver == ranking[0]) | (receiver == ranking[0]) | (tallies[receiver] == 0), 0, jnp.maximum(margin, 0))
    shifted = jax.random.randint(jax.random.fold_in(own, 4), (amount // 2,), 0, 1 << 20) % (margin + 1)
    tallies = tallies.at[giver].add(-shifted).at[receiver].add(shifted)
    items = jnp.searchsorted(jnp.cumsum(tallies), jnp.arange(rows * top), side="right").astype(jnp.int32)
    listing = items.reshape(top, rows).T
    listing = listing[jax.random.permutation(jax.random.fold_in(own, 1), rows)]
    rotation = jax.random.randint(jax.random.fold_in(own, 2), (rows, 1), 0, top)
    return jnp.take_along_axis(listing, (jnp.arange(top)[None, :] + rotation) % top, axis=1)


def shares(number_of, total, limit, skew, full):
    portions = [(1 << 20) // math.isqrt(standing ** skew) + 1 for standing in range(1, number_of + 1)]
    largest = limit if full else min(limit, max(-(-total // number_of), total * portions[0] // sum(portions)))
    least = 1 if total - largest >= number_of - 1 else 0
    holding, rest = [largest] + [least] * (number_of - 1), total - largest - least * (number_of - 1)
    while rest > 0:
        free = [i for i in range(1, number_of) if holding[i] < largest] or [i for i in range(1, number_of) if holding[i] < limit]
        pool, left = sum([portions[i] for i in free]), rest
        for i in free:
            more = min(limit - holding[i], max(1, left * portions[i] // pool), rest)
            holding[i] = holding[i] + more
            rest = rest - more
    return np.array(holding)


def noise(key, dims, scale, reach, pieces=(), kind=jnp.bfloat16):
    loudness = levels(key, dims, pieces, -0.22, 0.18) if pieces else 1.0
    array = jax.random.normal(key, dims, jnp.float32) * scale * loudness
    return jnp.minimum(jnp.maximum(array, -reach), reach).astype(kind)


def setup_inputs(seed: int = 0) -> dict:
    arg_keys = jax.random.split(jax.random.key(seed), 8)
    control = noise(arg_keys[0], (COL, NLAT, NLON), 1.0, 6.0, ((1, 4), (2, 8)), jnp.float32)
    std_dev = jnp.clip(jnp.exp(jax.random.uniform(arg_keys[1], (COL,), jnp.float32, math.log(0.3), math.log(3.0))), 0.3, 3.0)
    col_dev_keys = jax.random.split(jax.random.fold_in(arg_keys[2], 1), SOUND // S_DEV)
    col_dev_turns = jax.random.permutation(jax.random.fold_in(arg_keys[2], 3), SOUND // S_DEV)
    col_dev = jax.vmap(lambda own, number: routed_block(jax.random.fold_in(arg_keys[2], 2), own, number, S_DEV, DEVICES, 1, CAP, 2))(col_dev_keys, col_dev_turns).reshape((SOUND, 1))
    col_cell = place_ends(jax.random.randint(arg_keys[3], (SOUND,), 0, TLAT * TLON), jax.random.fold_in(arg_keys[3], 1), 0, (TLAT * TLON) - 1).astype(jnp.int32)
    jacobian = noise(arg_keys[4], (SOUND, CH, COL), COL ** -0.5, 0.25, ((0, 32),))
    innovation = noise(arg_keys[5], (SOUND, CH), 1.0, 6.0, ((0, 32),), jnp.float32)
    inv_error = jnp.clip(jnp.exp(jax.random.uniform(arg_keys[6], (CH,), jnp.float32, math.log(0.3), math.log(3.0))), 0.3, 3.0)
    return {"control": control, "std_dev": std_dev, "col_dev": col_dev, "col_cell": col_cell, "jacobian": jacobian, "innovation": innovation, "inv_error": inv_error}


def band(out_count, in_count, half_width):
    row_index = jnp.arange(out_count, dtype=jnp.int32)[:, None]
    col_index = jnp.arange(in_count, dtype=jnp.int32)[None, :]
    offset = (col_index - row_index - half_width).astype(jnp.float32)
    spread = 2.0 * half_width / 3.0
    taps = jnp.arange(-half_width, half_width + 1, dtype=jnp.int32).astype(jnp.float32)
    norm_total = jnp.sqrt(jnp.sum(jnp.exp(-taps * taps / (spread * spread))))
    weights = jnp.exp(-offset * offset / (2.0 * spread * spread)) / norm_total
    return jnp.where(jnp.abs(offset) <= half_width, weights, jnp.zeros_like(weights))

def along_lat(grid_field):
    half_width = LHALF
    extended = jnp.pad(grid_field, ((0, 0), (half_width, half_width), (0, 0)))
    lat_band = band(TLAT, TLAT + 2 * half_width, half_width)

    def one_block(block):
        window = lax.dynamic_slice_in_dim(extended, block * TLAT, TLAT + 2 * half_width, 1)
        return jnp.einsum('ij,cjk->cik', lat_band, window, precision=lax.Precision.HIGHEST)
    blocks = lax.map(one_block, jnp.arange(N_LAT, dtype=jnp.int32))
    return jnp.transpose(blocks, (1, 0, 2, 3)).reshape(grid_field.shape)

def along_lon(grid_field):
    half_width = TLON // 2
    extended = jnp.concatenate([grid_field[:, :, -half_width:], grid_field, grid_field[:, :, :half_width]], axis=2)
    lon_band = band(TLON, TLON + 2 * half_width, half_width)

    def one_block(block):
        window = lax.dynamic_slice_in_dim(extended, block * TLON, TLON + 2 * half_width, 2)
        return jnp.einsum('cik,jk->cij', window, lon_band, precision=lax.Precision.HIGHEST)
    blocks = lax.map(one_block, jnp.arange(N_LON, dtype=jnp.int32))
    return jnp.transpose(blocks, (1, 2, 0, 3)).reshape(grid_field.shape)

def reference(control, std_dev, col_dev, col_cell, jacobian, innovation, inv_error):
    width, lat_rows, lon_cols = control.shape
    increment = along_lon(along_lat(control)) * std_dev[:, None, None]
    target = col_dev[:, 0]
    row_of = target // N_LON * TLAT + col_cell // TLON
    column_of = target % N_LON * TLON + col_cell % TLON
    columns = increment[:, row_of, column_of].T.astype(jnp.bfloat16)

    def per_device(items):
        jac_block, col_block, innov_block = items
        jac_wide = jac_block.astype(jnp.float32)
        evolved = jnp.einsum('sqc,sc->sq', jac_wide, col_block.astype(jnp.float32))
        deps = evolved - innov_block
        weighted = (deps * inv_error[None, :]).astype(jnp.bfloat16)
        column_grad = jnp.einsum('sqc,sq->sc', jac_wide, weighted.astype(jnp.float32))
        return (deps, column_grad)
    departures, column_grad = lax.map(per_device, (jacobian.reshape(DEVICES, S_DEV, CH, width), columns.reshape(DEVICES, S_DEV, width), innovation.reshape(DEVICES, S_DEV, CH)))
    departures = departures.reshape(SOUND, CH)
    column_grad = column_grad.reshape(SOUND, width)
    flat_index = (row_of * lon_cols + column_of).astype(jnp.int32)
    gathered = jnp.zeros((width, lat_rows * lon_cols), jnp.float32).at[:, flat_index].add(column_grad.T)
    gathered = gathered.reshape(width, lat_rows, lon_cols) * std_dev[:, None, None]
    adjoint = along_lat(along_lon(gathered))
    return (departures, increment, adjoint)
```

```python
import functools
import math

import jax
import jax.numpy as jnp
from jax import lax
from jax.experimental import pallas as pl
from jax.experimental.pallas import tpu as pltpu
from jax.sharding import PartitionSpec as P

LHALF = 8
HIGHEST = lax.Precision.HIGHEST
MESH = pl.DeviceIdType.MESH


def tap_weights(offset, half_width):
    spread = 2.0 * half_width / 3.0
    taps = jnp.arange(-half_width, half_width + 1, dtype=jnp.int32).astype(jnp.float32)
    norm_total = jnp.sqrt(jnp.sum(jnp.exp(-taps * taps / (spread * spread))))
    weights = jnp.exp(-offset * offset / (2.0 * spread * spread)) / norm_total
    return jnp.where(jnp.abs(offset) <= half_width, weights, jnp.zeros_like(weights))


def shifts(axis, wrap):
    peers = lax.axis_size(axis)
    up = [(i, (i + 1) % peers) for i in range(peers if wrap else peers - 1)]
    return up, [(j, i) for i, j in up]


def around(array, axis, wrap):
    up, down = shifts(axis, wrap)
    return lax.ppermute(array, axis, up), lax.ppermute(array, axis, down)


def halves(weights):
    high = weights.astype(jnp.bfloat16)
    return high, (weights - high.astype(jnp.float32)).astype(jnp.bfloat16)


def tap_value(offset, half_width):
    spread = 2.0 * half_width / 3.0
    norm_total = math.sqrt(sum(math.exp(-e * e / (spread * spread)) for e in range(-half_width, half_width + 1)))
    weights = jnp.exp(-offset * offset / (2.0 * spread * spread)) / norm_total
    return jnp.where(jnp.abs(offset) <= half_width, weights, 0.0)


GROUP = 256
CHUNK = 2 * GROUP


def matmul(left, right):
    return jnp.dot(left, right, preferred_element_type=jnp.float32)


def across(left, right):
    return lax.dot_general(left, right, (((1,), (1,)), ((), ())), preferred_element_type=jnp.float32)


def dense_kernel(
    lat, lon, lat_rows, slots_each,
    ctrl_ref, wanted_ref, std_ref,
    inc_ref, table_ref, got_ref,
    own_ref, swap_ref, far_ref, g_ref, to_right_ref, to_left_ref, from_left_ref, from_right_ref,
    band_ref, mid_ref, edge_ref, std_row_ref, cell_ref, row_ref, pick_ref,
    swap_send, swap_recv, far_send, far_recv, lon_send, lon_recv,
    want_send, want_recv, col_send, col_recv,
):
    rows, lon_cols = ctrl_ref.shape
    width = rows // lat_rows
    full, rest = rows // CHUNK, rows % CHUNK
    log_lat, log_lon = lat_rows.bit_length() - 1, lon_cols.bit_length() - 1
    lon_half = lon_cols // 2
    row, column = lax.axis_index("lat"), lax.axis_index("lon")
    devices, me = lat * lon, row * lon + column
    odd = row % 2
    partner, step = row + 1 - 2 * odd, 2 - 4 * odd
    onward = jnp.logical_and(row + step >= 0, row + step < lat)
    comes = jnp.logical_and(row - step >= 0, row - step < lat)
    place = lambda other: (other // lon, other % lon)
    iota = lambda shape, axis: lax.broadcasted_iota(jnp.int32, shape, axis)

    barrier = pltpu.get_barrier_semaphore()

    def greet(d, carry):
        pl.semaphore_signal(barrier, inc=1, device_id=place((me + d) % devices), device_id_type=MESH)
        return carry

    lax.fori_loop(1, devices, greet, 0)

    def chunk_of(k):
        return pl.ds(pl.multiple_of(k * CHUNK, CHUNK), CHUNK)

    def half_of(k):
        return pl.ds(pl.multiple_of(k * GROUP, GROUP), GROUP)

    last, last_half = pl.ds(full * CHUNK, rest), pl.ds(full * GROUP, rest // 2)

    def remote(source, target, send, recv, device):
        return pltpu.make_async_remote_copy(
            src_ref=source, dst_ref=target, send_sem=send, recv_sem=recv, device_id=device, device_id_type=MESH
        )

    def request(dst, send, recv, other):
        return remote(wanted_ref.at[0], table_ref.at[dst], want_send.at[send], want_recv.at[recv], place(other))

    def swap(k, part):
        return remote(own_ref.at[part], swap_ref.at[part], swap_send.at[k], swap_recv.at[k], (partner, column))

    def forward(k, part):
        return remote(swap_ref.at[part], far_ref.at[part], far_send.at[k], far_recv.at[k], (row + step, column))

    def to_right(k, part):
        return remote(
            to_right_ref.at[part], from_left_ref.at[part], lon_send.at[0, k], lon_recv.at[0, k],
            (row, (column + 1) % lon),
        )

    def to_left(k, part):
        return remote(
            to_left_ref.at[part], from_right_ref.at[part], lon_send.at[1, k], lon_recv.at[1, k],
            (row, (column + lon - 1) % lon),
        )

    def back(d, group):
        part = pl.ds(pl.multiple_of(group * lon_cols, lon_cols), lon_cols)
        return remote(
            pick_ref.at[d, :, part], got_ref.at[me, :, part], col_send.at[d], col_recv.at[me], place(d)
        )

    def round_own(part):
        own_ref[part, :] = ctrl_ref[part, :].astype(jnp.bfloat16)

    round_own(pl.ds(0, CHUNK))
    pl.semaphore_wait(barrier, devices - 1)

    def ask(d, carry):
        request(me, (me + d) % devices, me, (me + d) % devices).start()
        return carry

    lax.fori_loop(1, devices, ask, 0)

    def send_own(k, carry):
        round_own(chunk_of(k + 1))
        swap(k, chunk_of(k)).start()
        return carry

    lax.fori_loop(0, full - 1, send_own, 0)
    round_own(last)
    swap(full - 1, chunk_of(full - 1)).start()
    table_ref[me] = wanted_ref[0]

    @pl.when(jnp.logical_not(comes))
    def _():
        far_ref[...] = jnp.zeros_like(far_ref)

    swap(full, last).start()

    square = (GROUP, GROUP)
    same = (iota(square, 0) >> log_lat) == (iota(square, 1) >> log_lat)
    apart = (iota(square, 1) & (lat_rows - 1)) - (iota(square, 0) & (lat_rows - 1))

    def lat_band(shift):
        return halves(jnp.where(same, tap_value((apart + shift).astype(jnp.float32), LHALF), 0.0))

    high, low = lat_band(0)
    swap_high, swap_low = lat_band(lat_rows - 2 * lat_rows * odd)
    far_high, far_low = lat_band(2 * lat_rows * odd - lat_rows)
    for at, block in enumerate((high, high, low, swap_high, swap_low, far_high, far_low)):
        band_ref[:, at * GROUP:(at + 1) * GROUP] = block
    along = iota((lon_cols, lon_cols), 0) - iota((lon_cols, lon_cols), 1)
    high, low = halves(tap_value(along.astype(jnp.float32), lon_half))
    mid_ref[:, :lon_cols] = high
    mid_ref[:, lon_cols:] = low
    wide = (2 * lon_cols, 2 * lon_cols)
    source, target = iota(wide, 0), iota(wide, 1)
    within, which = source & (lon_half - 1), (source >> (log_lon - 1)) & 1
    column_at = jnp.where(source < lon_cols, within - lon_half, within + lon_cols)
    apart = column_at - (target & (lon_cols - 1))
    value = jnp.where(which == (target >> log_lon), tap_value(apart.astype(jnp.float32), lon_half), 0.0)
    high, low = halves(value)
    edge_ref[0] = high
    edge_ref[1] = low

    def spread(c, carry):
        std_row_ref[pl.ds(pl.multiple_of(c * lat_rows, lat_rows), lat_rows), :] = jnp.full(
            (lat_rows, lon_cols), std_ref[0, c], jnp.float32
        )
        return carry

    lax.fori_loop(0, width, spread, 0)

    def hear(d, carry):
        other = (me + d) % devices
        asked = request(other, other, other, other)
        asked.wait_send()
        asked.wait_recv()
        return carry

    lax.fori_loop(1, devices, hear, 0)
    listed = jnp.broadcast_to(table_ref[...].astype(jnp.float32), (devices, 8, table_ref.shape[2]))
    wants = iota(listed.shape, 2) == iota(listed.shape, 1) + me * slots_each
    cell = jnp.sum(jnp.where(wants, listed, 0.0), axis=2, keepdims=True).astype(jnp.int32)
    cell = jnp.broadcast_to(cell, (devices, 8, lon_cols)).reshape(devices * 8, lon_cols)
    row_ref[...] = cell >> log_lon
    cell_ref[...] = jnp.where((cell & (lon_cols - 1)) == iota(cell.shape, 1), 1.0, 0.0).astype(jnp.bfloat16)

    def lat_product(first, second):
        def pair(ref):
            return jnp.concatenate([ref[first, :], ref[second, :]], axis=1)

        field = pair(ctrl_ref)
        field_high, field_low = halves(field)
        swapped, far = pair(swap_ref), pair(far_ref)
        stacked = jnp.concatenate([field_high, field_low, field_high, swapped, swapped, far, far], axis=0)
        return matmul(band_ref[...], stacked)

    lane = iota((1, lon_cols), 1)

    def pack(first, second, part):
        right = jnp.where(lane < lon_half, pltpu.roll(first, lon_half, 1), second)
        left = jnp.where(lane < lon_half, first, pltpu.roll(second, lon_half, 1))
        to_right_ref[part, :] = right.astype(jnp.bfloat16)
        to_left_ref[part, :] = left.astype(jnp.bfloat16)

    def smooth_lat(k):
        base = pl.multiple_of(k * CHUNK, CHUNK)
        first, second = pl.ds(base, GROUP), pl.ds(base + GROUP, GROUP)
        result = lat_product(first, second)
        top, bottom = result[:, :lon_cols], result[:, lon_cols:]
        g_ref[first, :] = top
        g_ref[second, :] = bottom
        pack(top, bottom, half_of(k))

    def smooth_lat_last():
        result = lat_product(pl.ds(rows - CHUNK, GROUP), pl.ds(rows - GROUP, GROUP))
        kept = jnp.concatenate([result[:, :lon_cols], result[:, lon_cols:]], axis=0)[CHUNK - rest:]
        g_ref[last, :] = kept
        pack(kept[: rest // 2], kept[rest // 2:], last_half)

    def smooth_lon(start, count, part):
        half = count // 2
        both = jnp.concatenate([from_left_ref[part, :], from_right_ref[part, :]], axis=1)
        sides = matmul(both, edge_ref[0]) + matmul(both, edge_ref[1])
        high, low = halves(g_ref[pl.ds(start, count), :])
        own = matmul(high, mid_ref[...])
        own = own[:, :lon_cols] + own[:, lon_cols:] + matmul(low, mid_ref[:, :lon_cols])
        first, second = pl.ds(start, half), pl.ds(start + half, half)
        inc_ref[first, :] = (own[:half] + sides[:, :lon_cols]) * std_row_ref[first, :]
        inc_ref[second, :] = (own[half:] + sides[:, lon_cols:]) * std_row_ref[second, :]

    def pick(start, count, group):
        values = inc_ref[pl.ds(start, count), :].astype(jnp.bfloat16)
        found = across(cell_ref[...], values)
        mine = (iota(row_ref.shape, 1) & (lat_rows - 1)) == row_ref[...]
        parts = []
        for at in range(0, count, lon_cols):
            piece = found[:, at:at + lon_cols]
            parts.append(jnp.where(mine[:, : piece.shape[1]], piece, 0.0).astype(jnp.bfloat16))
        masked = jnp.concatenate(parts, axis=1)
        gather = (iota((count, lon_cols), 0) >> log_lat) == iota((count, lon_cols), 1)
        result = matmul(masked, jnp.where(gather, 1.0, 0.0).astype(jnp.bfloat16))
        result = result.reshape(devices, 8, lon_cols)[:, :slots_each, :]
        pick_ref[:, :, pl.ds(pl.multiple_of(group * lon_cols, lon_cols), lon_cols)] = result.astype(jnp.bfloat16)

    def send_back(group):
        def give(d, carry):
            back((me + d) % devices, group).start()
            return carry

        lax.fori_loop(1, devices, give, 0)

    def stage(k, carry):
        def arrive(k, part):
            swap(k, part).wait_recv()

            @pl.when(onward)
            def _():
                forward(k, part).start()

        def await_far(k, part):
            @pl.when(comes)
            def _():
                forward(k, part).wait_recv()

        @pl.when(k < full)
        def _():
            arrive(k, chunk_of(k))

        @pl.when(k == full)
        def _():
            arrive(full, last)

        @pl.when(jnp.logical_and(k >= 1, k <= full))
        def _():
            await_far(k - 1, chunk_of(k - 1))
            smooth_lat(k - 1)

        @pl.when(k == full + 1)
        def _():
            await_far(full, last)
            smooth_lat_last()

        @pl.when(jnp.logical_and(k >= 2, k <= full + 1))
        def _():
            to_right(k - 2, half_of(k - 2)).wait_recv()
            to_left(k - 2, half_of(k - 2)).wait_recv()
            smooth_lon(pl.multiple_of((k - 2) * CHUNK, CHUNK), CHUNK, half_of(k - 2))

        @pl.when(jnp.logical_and(k >= 1, k <= full))
        def _():
            to_right(k - 1, half_of(k - 1)).start()
            to_left(k - 1, half_of(k - 1)).start()

        @pl.when(k == full + 1)
        def _():
            to_right(full, last_half).start()
            to_left(full, last_half).start()

        @pl.when(jnp.logical_and(jnp.logical_and(k >= 3, k <= full + 1), k % 2 == 1))
        def _():
            group = k // 2 - 1
            pick(pl.multiple_of(group * 2 * CHUNK, 2 * CHUNK), 2 * CHUNK, group)
            send_back(group)

        @pl.when(k == full + 2)
        def _():
            to_right(full, last_half).wait_recv()
            to_left(full, last_half).wait_recv()
            smooth_lon(full * CHUNK, rest, last_half)
            pick(full * CHUNK, rest, full // 2)
            send_back(full // 2)

        return carry

    lax.fori_loop(0, full + 3, stage, 0)
    got_ref[me] = pick_ref[me]

    def finish(k, part, half):
        swap(k, part).wait_send()

        @pl.when(onward)
        def _():
            forward(k, part).wait_send()

        to_right(k, half).wait_send()
        to_left(k, half).wait_send()

    def finish_full(k, carry):
        finish(k, chunk_of(k), half_of(k))
        return carry

    lax.fori_loop(0, full, finish_full, 0)
    finish(full, last, last_half)

    def collect(d, carry):
        other = (me + d) % devices
        whole = remote(
            pick_ref.at[other], got_ref.at[other], col_send.at[other], col_recv.at[other], place(other)
        )
        whole.wait_send()
        whole.wait_recv()
        return carry

    lax.fori_loop(1, devices, collect, 0)


def dense_step(control, wanted, std_dev, slots_each):
    lat, lon = lax.axis_size("lat"), lax.axis_size("lon")
    width, lat_rows, lon_cols = control.shape
    devices, rows = lat * lon, width * lat_rows
    pieces = rows // CHUNK + 1
    lanes = lane_tiles(width) * lon_cols
    wanted = jnp.pad(wanted, (0, -wanted.shape[0] % 128))[None, None, :]
    vmem = pl.BlockSpec(memory_space=pltpu.VMEM)
    dma = pltpu.SemaphoreType.DMA
    bf16, f32 = jnp.bfloat16, jnp.float32
    return pl.pallas_call(
        functools.partial(dense_kernel, lat, lon, lat_rows, slots_each),
        in_specs=[vmem, vmem, pl.BlockSpec(memory_space=pltpu.SMEM)],
        out_specs=[vmem, vmem, vmem],
        out_shape=[
            jax.ShapeDtypeStruct((rows, lon_cols), f32),
            jax.ShapeDtypeStruct((devices, *wanted.shape[1:]), wanted.dtype),
            jax.ShapeDtypeStruct((devices, slots_each, lanes), bf16),
        ],
        scratch_shapes=[
            pltpu.VMEM((rows, lon_cols), bf16),
            pltpu.VMEM((rows, lon_cols), bf16),
            pltpu.VMEM((rows, lon_cols), bf16),
            pltpu.VMEM((rows, lon_cols), f32),
            *[pltpu.VMEM((rows // 2, lon_cols), bf16)] * 4,
            pltpu.VMEM((GROUP, 7 * GROUP), bf16),
            pltpu.VMEM((lon_cols, 2 * lon_cols), bf16),
            pltpu.VMEM((2, 2 * lon_cols, 2 * lon_cols), bf16),
            pltpu.VMEM((rows, lon_cols), f32),
            pltpu.VMEM((devices * 8, lon_cols), bf16),
            pltpu.VMEM((devices * 8, lon_cols), jnp.int32),
            pltpu.VMEM((devices, slots_each, lanes), bf16),
            *[dma((pieces,))] * 4,
            *[dma((2, pieces))] * 2,
            *[dma((devices,))] * 4,
        ],
        compiler_params=pltpu.CompilerParams(collective_id=0, has_side_effects=True),
        name="dense",
    )(control.reshape(rows, lon_cols), wanted, std_dev[None, :])


def lane_tiles(count):
    return -(-count // 128)


def sounding_kernel(channels, step, jac_ref, col_ref, innov_ref, inv_ref, dep_ref, out_ref, grad_ref):
    rows, width = col_ref.shape
    padded = dep_ref.shape[1]
    lanes = lax.broadcasted_iota(jnp.int32, (rows, padded), 1)
    columns = col_ref[...].astype(jnp.float32)
    dep_ref[...] = jnp.zeros_like(dep_ref)
    grad_ref[...] = jnp.zeros_like(grad_ref)

    def some(index, carry):
        weighted = []
        found = jnp.zeros(dep_ref.shape, jnp.float32)
        for k in range(step):
            channel = index * step + k
            product = jac_ref[channel].astype(jnp.float32) * columns
            observed = jnp.where(lanes == channel, innov_ref[...], 0.0)
            product = jnp.concatenate([product[:, :padded] - observed, product[:, padded:]], axis=1)
            departure = jnp.sum(product, axis=1, keepdims=True)
            found = found + jnp.where(lanes == channel, departure, 0.0)
            weight = (departure * inv_ref[0, channel]).astype(jnp.bfloat16)
            weighted.append(weight.astype(jnp.float32))
        dep_ref[...] += found
        total = grad_ref[...]
        for k in range(step):
            total = total + jac_ref[index * step + k].astype(jnp.float32) * weighted[k]
        grad_ref[...] = total
        return carry

    lax.fori_loop(0, channels // step, some, 0)
    out_ref[...] = jnp.zeros_like(out_ref)
    out_ref[:, :width] = grad_ref[...].astype(out_ref.dtype)


def sounding_step(jacobian, columns, innovation, inv_error):
    count, channels, width = jacobian.shape
    rows = 16
    step = next(n for n in (10, 8, 6, 5, 4, 3, 2, 1) if channels % n == 0)
    padded = lane_tiles(channels) * 128
    innovation = jnp.pad(innovation, ((0, 0), (0, padded - channels)))
    departures, grad = pl.pallas_call(
        functools.partial(sounding_kernel, channels, step),
        grid=(count // rows,),
        in_specs=[
            pl.BlockSpec((channels, rows, width), lambda i: (0, i, 0)),
            pl.BlockSpec((rows, width), lambda i: (i, 0)),
            pl.BlockSpec((rows, padded), lambda i: (i, 0)),
            pl.BlockSpec(memory_space=pltpu.SMEM),
        ],
        out_specs=[
            pl.BlockSpec((rows, padded), lambda i: (i, 0)),
            pl.BlockSpec((rows, lane_tiles(width) * 128), lambda i: (i, 0)),
        ],
        out_shape=[
            jax.ShapeDtypeStruct((count, padded), jnp.float32),
            jax.ShapeDtypeStruct((count, lane_tiles(width) * 128), jnp.bfloat16),
        ],
        scratch_shapes=[pltpu.VMEM((rows, width), jnp.float32)],
        name="soundings",
    )(jnp.transpose(jacobian, (1, 0, 2)), columns, innovation, inv_error[None, :])
    return departures[:, :channels], grad


def adjoint_kernel(near_ref, before_ref, after_ref, col_ref, row_ref, std_ref, out_ref):
    lon_cols = col_ref.shape[1]
    total = jnp.zeros((2 * lon_cols, near_ref.shape[1]), jnp.float32)
    for at, grads in enumerate((near_ref, before_ref, after_ref)):
        high, low = halves(col_ref[at] * row_ref[0, at])
        both = jnp.concatenate([high, low], axis=0)
        total = total + jnp.dot(both, grads[...], preferred_element_type=jnp.float32)
    total = (total[:lon_cols] + total[lon_cols:]) * std_ref[...]
    out_ref[...] = total.T[: out_ref.shape[0]]


def adjoint_step(grads, rows, columns_at, std_dev, lat_rows, lon_cols):
    slots, wide = grads[0].shape
    width = std_dev.shape[0]
    std_dev = jnp.pad(std_dev, (0, wide - width))
    down = jnp.arange(lat_rows)[:, None, None, None]
    row_weight = tap_weights((rows[None, :, None, :] - down).astype(jnp.float32), LHALF)
    along = jnp.arange(lon_cols)[None, :, None]
    col_weight = tap_weights((columns_at[:, None, :] - along).astype(jnp.float32), lon_cols // 2)
    whole = pl.BlockSpec((slots, wide), lambda i: (0, 0))
    return pl.pallas_call(
        adjoint_kernel,
        grid=(lat_rows,),
        in_specs=[
            whole,
            whole,
            whole,
            pl.BlockSpec((3, lon_cols, slots), lambda i: (0, 0, 0)),
            pl.BlockSpec((1, 3, 1, slots), lambda i: (i, 0, 0, 0)),
            pl.BlockSpec((1, wide), lambda i: (0, 0)),
        ],
        out_specs=pl.BlockSpec((width, lon_cols), lambda i: (0, i)),
        out_shape=jax.ShapeDtypeStruct((width, lat_rows * lon_cols), jnp.float32),
        name="adjoint",
    )(*grads, col_weight, row_weight, std_dev[None, :])


def local(control, std_dev, col_dev, col_cell, jacobian, innovation, inv_error):
    width, lat_rows, lon_cols = control.shape
    devices = lax.axis_size("lat") * lax.axis_size("lon")
    sound_count = col_cell.shape[0]
    slots_each = max(2, 2 * sound_count // devices)
    slots = devices * slots_each

    target = col_dev[:, 0]
    onehot = (target[:, None] == jnp.arange(devices, dtype=jnp.int32)[None, :]).astype(jnp.int32)
    below = jnp.arange(sound_count)[:, None] > jnp.arange(sound_count)[None, :]
    earlier = jnp.dot(
        below.astype(jnp.bfloat16), onehot.astype(jnp.bfloat16), preferred_element_type=jnp.float32
    ).astype(jnp.int32)
    order_in = jnp.sum(earlier * onehot, axis=1)
    slot = target * slots_each + order_in
    wanted = jnp.zeros((slots,), jnp.int32).at[slot].set(col_cell)
    increment, table, got = dense_step(control, wanted, std_dev, slots_each)
    increment, table = increment.reshape(control.shape), table[:, 0, :slots]
    lat_at, lon_at = lax.axis_index("lat"), lax.axis_index("lon")
    lat_devices, lon_devices = lax.axis_size("lat"), lax.axis_size("lon")

    def asked_of(lat_shift, lon_shift):
        row = jnp.clip(lat_at + lat_shift, 0, lat_devices - 1)
        owner = row * lon_devices + (lon_at + lon_shift) % lon_devices
        return lax.dynamic_slice(table, (0, owner * slots_each), (devices, slots_each))

    columns = got[:, :, :width].reshape(slots, width)[slot]
    departures, column_grad = sounding_step(jacobian, columns, innovation, inv_error)
    wide = column_grad.shape[1]
    outgoing = jnp.zeros((slots, wide), jnp.bfloat16).at[slot].set(column_grad)
    arrived = lax.all_to_all(
        outgoing.reshape(devices, slots_each, wide), ("lat", "lon"), split_axis=0, concat_axis=0, tiled=True
    ).reshape(slots, wide)
    near = jnp.concatenate([arrived, *around(arrived, "lat", False)], axis=0)
    grads = (near, *around(near, "lon", True))
    order = (0, -1, 1)
    cells = jnp.stack([jnp.stack([asked_of(up, along) for up in order]) for along in order])
    cells = cells.reshape(3, 3, slots)
    shift = jnp.array(order, jnp.int32)
    rows = (cells // lon_cols + lat_rows * shift[None, :, None]).reshape(3, 3 * slots)
    columns_at = (cells % lon_cols + lon_cols * shift[:, None, None]).reshape(3, 3 * slots)
    adjoint = adjoint_step(grads, rows, columns_at, std_dev, lat_rows, lon_cols)
    return (departures, increment, adjoint.reshape(width, lat_rows, lon_cols))


def solution(mesh):
    placed = (
        P(None, "lat", "lon"),
        P(),
        P(("lat", "lon"), None),
        P(("lat", "lon")),
        P(("lat", "lon"), None, None),
        P(("lat", "lon"), None),
        P(),
    )
    return jax.shard_map(
        local,
        mesh=mesh,
        in_specs=placed,
        out_specs=(P(("lat", "lon"), None), P(None, "lat", "lon"), P(None, "lat", "lon")),
        check_vma=False,
    )
```

```python
import functools
import math

import jax
import jax.numpy as jnp
from jax import lax
from jax.experimental import pallas as pl
from jax.experimental.pallas import tpu as pltpu
from jax.sharding import PartitionSpec as P

LHALF = 8
MESH = pl.DeviceIdType.MESH


def tap_weights(offset, half_width):
    spread = 2.0 * half_width / 3.0
    taps = jnp.arange(-half_width, half_width + 1, dtype=jnp.int32).astype(jnp.float32)
    norm_total = jnp.sqrt(jnp.sum(jnp.exp(-taps * taps / (spread * spread))))
    weights = jnp.exp(-offset * offset / (2.0 * spread * spread)) / norm_total
    return jnp.where(jnp.abs(offset) <= half_width, weights, jnp.zeros_like(weights))


def halves(weights):
    high = weights.astype(jnp.bfloat16)
    return high, (weights - high.astype(jnp.float32)).astype(jnp.bfloat16)


def tap_value(offset, half_width):
    spread = 2.0 * half_width / 3.0
    norm_total = math.sqrt(sum(math.exp(-e * e / (spread * spread)) for e in range(-half_width, half_width + 1)))
    weights = jnp.exp(-offset * offset / (2.0 * spread * spread)) / norm_total
    return jnp.where(jnp.abs(offset) <= half_width, weights, 0.0)


GROUP = 256
CHUNK = 2 * GROUP


def matmul(left, right):
    return jnp.dot(left, right, preferred_element_type=jnp.float32)


def across(left, right):
    return lax.dot_general(left, right, (((1,), (1,)), ((), ())), preferred_element_type=jnp.float32)


def slots_of(dev_ref, cell_ref, slots_each, count):
    sound_count = dev_ref.shape[1]
    square = (sound_count, sound_count)
    iota = lambda shape, axis: lax.broadcasted_iota(jnp.int32, shape, axis)
    before = iota(square, 0) - iota(square, 1)
    across_lanes = jnp.broadcast_to(dev_ref[...].astype(jnp.float32), square)
    upright = lambda spread: jnp.sum(jnp.where(before == 0, spread, 0.0), axis=1, keepdims=True)
    down = upright(across_lanes)
    alike = across_lanes == down
    order = jnp.sum(jnp.where(jnp.logical_and(alike, before > 0), 1.0, 0.0), axis=1, keepdims=True)
    slot = down * slots_each + order
    onehot = slot.astype(jnp.int32) == iota((sound_count, count), 1)
    cell = upright(jnp.broadcast_to(cell_ref[...].astype(jnp.float32), square))
    order = jnp.sum(jnp.where(jnp.logical_and(alike, before < 0), 1.0, 0.0), axis=0, keepdims=True)
    return onehot, cell, (dev_ref[...].astype(jnp.float32) * slots_each + order).astype(jnp.int32)


def dense_kernel(
    lat, lon, lat_rows, slots_each,
    ctrl_hbm, dev_ref, ask_ref, std_ref,
    inc_hbm, table_ref, got_ref,
    ctrl_ref, inc_ref, wanted_ref, own_ref, swap_ref, far_ref, g_ref, to_right_ref, to_left_ref, from_left_ref, from_right_ref,
    band_ref, mid_ref, edge_ref, std_row_ref, cell_ref, row_ref, pick_ref,
    swap_send, swap_recv, far_send, far_recv, lon_send, lon_recv,
    want_send, want_recv, col_send, col_recv, load_sem, store_sem,
):
    rows, lon_cols = ctrl_ref.shape
    width = rows // lat_rows
    full, rest = rows // CHUNK, rows % CHUNK
    early = full // 4 * 2
    log_lat, log_lon = lat_rows.bit_length() - 1, lon_cols.bit_length() - 1
    lon_half = lon_cols // 2
    row, column = lax.axis_index("lat"), lax.axis_index("lon")
    devices, me = lat * lon, row * lon + column
    odd = row % 2
    partner, step = row + 1 - 2 * odd, 2 - 4 * odd
    onward = jnp.logical_and(row + step >= 0, row + step < lat)
    comes = jnp.logical_and(row - step >= 0, row - step < lat)
    place = lambda other: (other // lon, other % lon)
    iota = lambda shape, axis: lax.broadcasted_iota(jnp.int32, shape, axis)

    barrier = pltpu.get_barrier_semaphore()

    def greet(d, carry):
        pl.semaphore_signal(barrier, inc=1, device_id=place((me + d) % devices), device_id_type=MESH)
        return carry

    lax.fori_loop(1, devices, greet, 0)

    def chunk_of(k):
        return pl.ds(pl.multiple_of(k * CHUNK, CHUNK), CHUNK)

    def half_of(k):
        return pl.ds(pl.multiple_of(k * GROUP, GROUP), GROUP)

    last, last_half = pl.ds(full * CHUNK, rest), pl.ds(full * GROUP, rest // 2)

    def remote(source, target, send, recv, device):
        return pltpu.make_async_remote_copy(
            src_ref=source, dst_ref=target, send_sem=send, recv_sem=recv, device_id=device, device_id_type=MESH
        )

    def request(dst, send, recv, other):
        return remote(wanted_ref.at[0], table_ref.at[dst], want_send.at[send], want_recv.at[recv], place(other))

    def swap(k, part):
        return remote(own_ref.at[part], swap_ref.at[part], swap_send.at[k], swap_recv.at[k], (partner, column))

    def forward(k, part):
        return remote(swap_ref.at[part], far_ref.at[part], far_send.at[k], far_recv.at[k], (row + step, column))

    def to_right(k, part):
        return remote(
            to_right_ref.at[part], from_left_ref.at[part], lon_send.at[0, k], lon_recv.at[0, k],
            (row, (column + 1) % lon),
        )

    def to_left(k, part):
        return remote(
            to_left_ref.at[part], from_right_ref.at[part], lon_send.at[1, k], lon_recv.at[1, k],
            (row, (column + lon - 1) % lon),
        )

    def back(d, group):
        part = pl.ds(pl.multiple_of(group * lon_cols, lon_cols), lon_cols)
        return remote(
            pick_ref.at[d, :, part], got_ref.at[me, :, part], col_send.at[d], col_recv.at[me], place(d)
        )

    def round_own(part):
        own_ref[part, :] = ctrl_ref[part, :].astype(jnp.bfloat16)

    def load(k, part):
        return pltpu.make_async_copy(ctrl_hbm.at[part], ctrl_ref.at[part], load_sem.at[k])

    def store(k, part):
        return pltpu.make_async_copy(inc_ref.at[part], inc_hbm.at[part], store_sem.at[k])

    def begin(k, carry):
        load(k, chunk_of(k)).start()
        return carry

    lax.fori_loop(0, full, begin, 0)
    load(full, last).start()
    onehot, cell_at, _ = slots_of(dev_ref, ask_ref, slots_each, wanted_ref.shape[2])
    wanted_ref[0] = jnp.sum(jnp.where(onehot, cell_at, 0.0), axis=0, keepdims=True).astype(jnp.int32)

    @pl.when(jnp.logical_not(comes))
    def _():
        far_ref[...] = jnp.zeros_like(far_ref)

    load(0, chunk_of(0)).wait()
    round_own(chunk_of(0))
    pl.semaphore_wait(barrier, devices - 1)

    def ask(d, carry):
        request(me, (me + d) % devices, me, (me + d) % devices).start()
        return carry

    lax.fori_loop(1, devices, ask, 0)

    def send_own(k, carry):
        load(k + 1, chunk_of(k + 1)).wait()

        @pl.when(k + 1 < early)
        def _():
            round_own(chunk_of(k + 1))

        swap(k, chunk_of(k)).start()
        return carry

    lax.fori_loop(0, early, send_own, 0)
    lane = iota((1, lon_cols), 1)

    def pack(first, second, part):
        right = jnp.where(lane < lon_half, pltpu.roll(first, lon_half, 1), second)
        left = jnp.where(lane < lon_half, first, pltpu.roll(second, lon_half, 1))
        to_right_ref[part, :] = right.astype(jnp.bfloat16)
        to_left_ref[part, :] = left.astype(jnp.bfloat16)

    def send_lon(k, part):
        to_right(k, part).start()
        to_left(k, part).start()

    def pack_own(k, carry):
        base = pl.multiple_of(k * CHUNK, CHUNK)
        pack(ctrl_ref[pl.ds(base, GROUP), :], ctrl_ref[pl.ds(base + GROUP, GROUP), :], half_of(k))

        @pl.when(k + 1 < full)
        def _():
            load(k + 1, chunk_of(k + 1)).wait()

        send_lon(k, half_of(k))
        return carry

    lax.fori_loop(early, full, pack_own, 0)
    load(full, last).wait()
    middle = full * CHUNK + rest // 2
    pack(ctrl_ref[full * CHUNK:middle, :], ctrl_ref[middle:, :], last_half)
    table_ref[me] = wanted_ref[0]
    send_lon(full, last_half)

    square = (GROUP, GROUP)
    same = (iota(square, 0) >> log_lat) == (iota(square, 1) >> log_lat)
    apart = (iota(square, 1) & (lat_rows - 1)) - (iota(square, 0) & (lat_rows - 1))

    def lat_band(shift):
        return halves(jnp.where(same, tap_value((apart + shift).astype(jnp.float32), LHALF), 0.0))

    high, low = lat_band(0)
    swap_high, swap_low = lat_band(lat_rows - 2 * lat_rows * odd)
    far_high, far_low = lat_band(2 * lat_rows * odd - lat_rows)
    for at, block in enumerate((high, high, low, swap_high, swap_low, far_high, far_low)):
        band_ref[:, at * GROUP:(at + 1) * GROUP] = block
    along = iota((lon_cols, lon_cols), 0) - iota((lon_cols, lon_cols), 1)
    high, low = halves(tap_value(along.astype(jnp.float32), lon_half))
    mid_ref[:, :lon_cols] = high
    mid_ref[:, lon_cols:] = low
    wide = (2 * lon_cols, 2 * lon_cols)
    source, target = iota(wide, 0), iota(wide, 1)
    within, which = source & (lon_half - 1), (source >> (log_lon - 1)) & 1
    column_at = jnp.where(source < lon_cols, within - lon_half, within + lon_cols)
    apart = column_at - (target & (lon_cols - 1))
    value = jnp.where(which == (target >> log_lon), tap_value(apart.astype(jnp.float32), lon_half), 0.0)
    high, low = halves(value)
    edge_ref[0] = high
    edge_ref[1] = low

    def spread(c, carry):
        std_row_ref[pl.ds(pl.multiple_of(c * lat_rows, lat_rows), lat_rows), :] = jnp.full(
            (lat_rows, lon_cols), std_ref[0, c], jnp.float32
        )
        return carry

    lax.fori_loop(0, width, spread, 0)

    def hear(d, carry):
        other = (me + d) % devices
        asked = request(other, other, other, other)
        asked.wait_send()
        asked.wait_recv()
        return carry

    lax.fori_loop(1, devices, hear, 0)
    listed = jnp.broadcast_to(table_ref[...].astype(jnp.float32), (devices, 8, table_ref.shape[2]))
    wants = iota(listed.shape, 2) == iota(listed.shape, 1) + me * slots_each
    cell = jnp.sum(jnp.where(wants, listed, 0.0), axis=2, keepdims=True).astype(jnp.int32)
    cell = jnp.broadcast_to(cell, (devices, 8, lon_cols)).reshape(devices * 8, lon_cols)
    row_ref[...] = cell >> log_lon
    cell_ref[...] = jnp.where((cell & (lon_cols - 1)) == iota(cell.shape, 1), 1.0, 0.0).astype(jnp.bfloat16)

    def lat_product(ref, first, second):
        def pair(ref):
            return jnp.concatenate([ref[first, :], ref[second, :]], axis=1)

        field = pair(ref)
        field_high, field_low = halves(field)
        swapped, far = pair(swap_ref), pair(far_ref)
        stacked = jnp.concatenate([field_high, field_low, field_high, swapped, swapped, far, far], axis=0)
        return matmul(band_ref[...], stacked)

    def lat_then_send(k):
        base = pl.multiple_of(k * CHUNK, CHUNK)
        first, second = pl.ds(base, GROUP), pl.ds(base + GROUP, GROUP)
        result = lat_product(ctrl_ref, first, second)
        top, bottom = result[:, :lon_cols], result[:, lon_cols:]
        g_ref[first, :] = top
        g_ref[second, :] = bottom
        pack(top, bottom, half_of(k))

    def lat_last(k):
        base = pl.multiple_of(k * CHUNK, CHUNK)
        first, second = pl.ds(base, GROUP), pl.ds(base + GROUP, GROUP)
        result = lat_product(g_ref, first, second)
        inc_ref[first, :] = result[:, :lon_cols] * std_row_ref[first, :]
        inc_ref[second, :] = result[:, lon_cols:] * std_row_ref[second, :]

    def lat_rest():
        result = lat_product(g_ref, pl.ds(rows - CHUNK, GROUP), pl.ds(rows - GROUP, GROUP))
        kept = jnp.concatenate([result[:, :lon_cols], result[:, lon_cols:]], axis=0)[CHUNK - rest:]
        inc_ref[last, :] = kept * std_row_ref[last, :]

    def lon_product(ref, start, count, part):
        half = count // 2
        both = jnp.concatenate([from_left_ref[part, :], from_right_ref[part, :]], axis=1)
        sides = matmul(both, edge_ref[0]) + matmul(both, edge_ref[1])
        high, low = halves(ref[pl.ds(start, count), :])
        own = matmul(high, mid_ref[...])
        own = own[:, :lon_cols] + own[:, lon_cols:] + matmul(low, mid_ref[:, :lon_cols])
        return own[:half] + sides[:, :lon_cols], own[half:] + sides[:, lon_cols:]

    def lon_last(k):
        base = pl.multiple_of(k * CHUNK, CHUNK)
        first, second = pl.ds(base, GROUP), pl.ds(base + GROUP, GROUP)
        top, bottom = lon_product(g_ref, base, CHUNK, half_of(k))
        inc_ref[first, :] = top * std_row_ref[first, :]
        inc_ref[second, :] = bottom * std_row_ref[second, :]

    def lon_first(start, count, part):
        first, second = pl.ds(start, count // 2), pl.ds(start + count // 2, count // 2)
        top, bottom = lon_product(ctrl_ref, start, count, part)
        g_ref[first, :] = top
        g_ref[second, :] = bottom
        own_ref[first, :] = top.astype(jnp.bfloat16)
        own_ref[second, :] = bottom.astype(jnp.bfloat16)

    def pick(start, count, group):
        values = inc_ref[pl.ds(start, count), :].astype(jnp.bfloat16)
        found = across(cell_ref[...], values)
        mine = (iota(row_ref.shape, 1) & (lat_rows - 1)) == row_ref[...]
        parts = []
        for at in range(0, count, lon_cols):
            piece = found[:, at:at + lon_cols]
            parts.append(jnp.where(mine[:, : piece.shape[1]], piece, 0.0).astype(jnp.bfloat16))
        masked = jnp.concatenate(parts, axis=1)
        gather = (iota((count, lon_cols), 0) >> log_lat) == iota((count, lon_cols), 1)
        result = matmul(masked, jnp.where(gather, 1.0, 0.0).astype(jnp.bfloat16))
        result = result.reshape(devices, 8, lon_cols)[:, :slots_each, :]
        pick_ref[:, :, pl.ds(pl.multiple_of(group * lon_cols, lon_cols), lon_cols)] = result.astype(jnp.bfloat16)

    def send_back(group):
        def give(d, carry):
            back((me + d) % devices, group).start()
            return carry

        lax.fori_loop(1, devices, give, 0)

    def stage(k, carry):
        def arrive(k, part):
            swap(k, part).wait_recv()

            @pl.when(onward)
            def _():
                forward(k, part).start()

        def await_far(k, part):
            @pl.when(comes)
            def _():
                forward(k, part).wait_recv()

        @pl.when(k < full)
        def _():
            arrive(k, chunk_of(k))

        @pl.when(k == full)
        def _():
            arrive(full, last)

        def await_lon(k, part):
            to_right(k, part).wait_recv()
            to_left(k, part).wait_recv()

        ahead, behind, done = k + early, k - 2, k - 4

        @pl.when(ahead < full)
        def _():
            await_lon(ahead, half_of(ahead))
            lon_first(pl.multiple_of(ahead * CHUNK, CHUNK), CHUNK, half_of(ahead))
            swap(ahead, chunk_of(ahead)).start()

        @pl.when(ahead == full)
        def _():
            await_lon(full, last_half)
            lon_first(full * CHUNK, rest, last_half)
            swap(full, last).start()

        @pl.when(jnp.logical_and(behind >= 0, behind < early))
        def _():
            await_far(behind, chunk_of(behind))
            lat_then_send(behind)

        @pl.when(jnp.logical_and(done >= 0, done < early))
        def _():
            await_lon(done, half_of(done))
            lon_last(done)
            store(done, chunk_of(done)).start()

        @pl.when(jnp.logical_and(behind >= 0, behind < early))
        def _():
            send_lon(behind, half_of(behind))

        @pl.when(jnp.logical_and(behind >= early, behind < full))
        def _():
            await_far(behind, chunk_of(behind))
            lat_last(behind)
            store(behind, chunk_of(behind)).start()

        def give(group):
            pick(pl.multiple_of(group * 2 * CHUNK, 2 * CHUNK), 2 * CHUNK, group)
            send_back(group)

        @pl.when(jnp.logical_and(jnp.logical_and(done >= 0, done < early), done % 2 == 1))
        def _():
            give(done // 2)

        @pl.when(jnp.logical_and(jnp.logical_and(behind >= early, behind < full), behind % 2 == 1))
        def _():
            give(behind // 2)

        @pl.when(behind == full)
        def _():
            await_far(full, last)
            lat_rest()
            store(full, last).start()
            pick(full * CHUNK, rest, full // 2)
            send_back(full // 2)

        return carry

    lax.fori_loop(0, full + 3, stage, 0)
    got_ref[me] = pick_ref[me]

    def finish(k, part, half):
        swap(k, part).wait_send()

        @pl.when(onward)
        def _():
            forward(k, part).wait_send()

        store(k, part).wait()
        to_right(k, half).wait_send()
        to_left(k, half).wait_send()

    def finish_full(k, carry):
        finish(k, chunk_of(k), half_of(k))
        return carry

    lax.fori_loop(0, full, finish_full, 0)
    finish(full, last, last_half)

    def collect(d, carry):
        other = (me + d) % devices
        whole = remote(
            pick_ref.at[other], got_ref.at[other], col_send.at[other], col_recv.at[other], place(other)
        )
        whole.wait_send()
        whole.wait_recv()
        return carry

    lax.fori_loop(1, devices, collect, 0)


def dense_step(control, col_dev, col_cell, std_dev, slots_each):
    lat, lon = lax.axis_size("lat"), lax.axis_size("lon")
    width, lat_rows, lon_cols = control.shape
    devices, rows = lat * lon, width * lat_rows
    pieces = rows // CHUNK + 1
    lanes = lane_tiles(width) * lon_cols
    listed = (1, lane_tiles(devices * slots_each) * 128)
    vmem, hbm = pl.BlockSpec(memory_space=pltpu.VMEM), pl.BlockSpec(memory_space=pl.ANY)
    dma = pltpu.SemaphoreType.DMA
    bf16, f32 = jnp.bfloat16, jnp.float32
    return pl.pallas_call(
        functools.partial(dense_kernel, lat, lon, lat_rows, slots_each),
        in_specs=[hbm, vmem, vmem, pl.BlockSpec(memory_space=pltpu.SMEM)],
        out_specs=[hbm, vmem, vmem],
        out_shape=[
            jax.ShapeDtypeStruct((rows, lon_cols), f32),
            jax.ShapeDtypeStruct((devices, *listed), jnp.int32),
            jax.ShapeDtypeStruct((devices, slots_each, lanes), bf16),
        ],
        scratch_shapes=[
            pltpu.VMEM((rows, lon_cols), f32),
            pltpu.VMEM((rows, lon_cols), f32),
            pltpu.VMEM((1, *listed), jnp.int32),
            pltpu.VMEM((rows, lon_cols), bf16),
            pltpu.VMEM((rows, lon_cols), bf16),
            pltpu.VMEM((rows, lon_cols), bf16),
            pltpu.VMEM((rows, lon_cols), f32),
            *[pltpu.VMEM((rows // 2, lon_cols), bf16)] * 4,
            pltpu.VMEM((GROUP, 7 * GROUP), bf16),
            pltpu.VMEM((lon_cols, 2 * lon_cols), bf16),
            pltpu.VMEM((2, 2 * lon_cols, 2 * lon_cols), bf16),
            pltpu.VMEM((rows, lon_cols), f32),
            pltpu.VMEM((devices * 8, lon_cols), bf16),
            pltpu.VMEM((devices * 8, lon_cols), jnp.int32),
            pltpu.VMEM((devices, slots_each, lanes), bf16),
            *[dma((pieces,))] * 4,
            *[dma((2, pieces))] * 2,
            *[dma((devices,))] * 4,
            *[dma((pieces,))] * 2,
        ],
        compiler_params=pltpu.CompilerParams(collective_id=0, has_side_effects=True),
        name="dense",
    )(control.reshape(rows, lon_cols), col_dev.reshape(1, -1), col_cell[None, :], std_dev[None, :])


def lane_tiles(count):
    return -(-count // 128)


def sounding_kernel(
    slots_each, jac_ref, got_ref, dev_ref, innov_ref, inv_ref, field_ref,
    dep_ref, out_ref, copy_ref, apart_ref, col_ref, tail_ref, grad_ref,
):
    at, steps = pl.program_id(0), pl.num_programs(0)
    step, count, width = jac_ref.shape
    devices, lanes = got_ref.shape[0], got_ref.shape[2]
    most = width // 128 * 128
    iota = lambda shape, axis: lax.broadcasted_iota(jnp.int32, shape, axis)
    copy_ref[...] = field_ref[...]

    @pl.when(at == 0)
    def _():
        apart_ref[...] = jnp.zeros_like(apart_ref)
        apart_ref[:, :slots_each, :] = got_ref[...].astype(jnp.float32)
        onehot = slots_of(dev_ref, dev_ref, 8, devices * 8)[0]
        onehot = jnp.where(onehot, 1.0, 0.0).astype(jnp.bfloat16)
        columns = matmul(onehot, apart_ref[...].reshape(devices * 8, lanes).astype(jnp.bfloat16))
        col_ref[...] = jnp.zeros_like(col_ref)
        col_ref[:count, :] = columns.astype(jnp.bfloat16)
        tail_ref[...] = columns[:, most:]
        grad_ref[...] = jnp.zeros_like(grad_ref)

    found = across(jac_ref[:, :, :most].reshape(step * count, most), col_ref[:, :most])
    square = (count, 128)
    mine = iota(square, 0) == iota(square, 1)
    weighted = []
    for k in range(step):
        channel = at * step + k
        observed = innov_ref[0, pl.ds(k, 1), :]
        own = jnp.where(mine, found[k * count:(k + 1) * count] - observed, 0.0)
        if width > most:
            tail = jac_ref[k, :, most:].astype(jnp.float32) * tail_ref[:, : width - most]
            own = own + jnp.concatenate([tail, jnp.zeros((count, 128 - (width - most)), jnp.float32)], axis=1)
        departure = jnp.sum(own, axis=1, keepdims=True)
        dep_ref[pl.ds(channel, 1), :] = jnp.sum(jnp.where(mine, departure, 0.0), axis=0, keepdims=True)[:, :count]
        weight = (departure * inv_ref[0, channel]).astype(jnp.bfloat16)
        weighted.append(weight.astype(jnp.float32))
    for group in range(0, count, 16):
        part = slice(group, group + 16)
        total = grad_ref[part, :width]
        for k in range(step):
            total = total + jac_ref[k, part, :].astype(jnp.float32) * weighted[k][part]
        grad_ref[part, :width] = total

    @pl.when(at == steps - 1)
    def _():
        slot = slots_of(dev_ref, dev_ref, 8, devices * 8)[2]
        onehot = jnp.where(iota((devices * 8, count), 0) == slot, 1.0, 0.0).astype(jnp.bfloat16)
        outgoing = matmul(onehot, grad_ref[...].astype(jnp.bfloat16))
        outgoing = outgoing.reshape(devices, 8, lanes)[:, :slots_each, :]
        out_ref[...] = outgoing.astype(out_ref.dtype)


def sounding_step(jacobian, got, col_dev, innovation, inv_error, field):
    count, channels, width = jacobian.shape
    devices, slots_each, lanes = got.shape
    step = next(n for n in (10, 8, 6, 5, 4, 3, 2, 1) if channels % n == 0)
    steps = channels // step
    block = -(-field.shape[0] // (8 * steps)) * 8
    innovation = jnp.pad(innovation.T, ((0, 0), (0, 128 - count))).reshape(steps, step, 128)
    whole = lambda shape: pl.BlockSpec(shape, lambda i: (0,) * len(shape))
    departures, grad, field = pl.pallas_call(
        functools.partial(sounding_kernel, slots_each),
        grid=(steps,),
        in_specs=[
            pl.BlockSpec((step, count, width), lambda i: (i, 0, 0)),
            whole(got.shape),
            whole((1, count)),
            pl.BlockSpec((1, step, 128), lambda i: (i, 0, 0)),
            pl.BlockSpec(memory_space=pltpu.SMEM),
            pl.BlockSpec((block, field.shape[1]), lambda i: (i, 0)),
        ],
        out_specs=[
            whole((channels, count)),
            whole(got.shape),
            pl.BlockSpec((block, field.shape[1]), lambda i: (i, 0)),
        ],
        out_shape=[
            jax.ShapeDtypeStruct((channels, count), jnp.float32),
            jax.ShapeDtypeStruct(got.shape, jnp.bfloat16),
            jax.ShapeDtypeStruct(field.shape, jnp.float32),
        ],
        scratch_shapes=[
            pltpu.VMEM((devices, 8, lanes), jnp.float32),
            pltpu.VMEM((128, lanes), jnp.bfloat16),
            pltpu.VMEM((count, 128), jnp.float32),
            pltpu.VMEM((count, lanes), jnp.float32),
        ],
        name="soundings",
    )(jnp.transpose(jacobian, (1, 0, 2)), got, col_dev.reshape(1, -1), innovation, inv_error[None, :], field)
    return departures.T, grad, field


def adjoint_kernel(
    lat, lon, lat_rows, cuts,
    give_ref, table_ref, std_ref, out_ref,
    arrived_ref, apart_ref, grads_ref, weight_ref,
    give_send, give_recv, swap_send, swap_recv, far_send, far_recv, lon_send, lon_recv,
):
    devices, slots_each, lanes = give_ref.shape
    slots = devices * slots_each
    rows, lon_cols = out_ref.shape
    log_lon = lon_cols.bit_length() - 1
    row, column = lax.axis_index("lat"), lax.axis_index("lon")
    me = row * lon + column
    odd = row % 2
    near = 1 - 2 * odd
    partner, step = row + near, 2 * near
    onward = jnp.logical_and(row + step >= 0, row + step < lat)
    comes = jnp.logical_and(row - step >= 0, row - step < lat)
    place = lambda other: (other // lon, other % lon)
    iota = lambda shape, axis: lax.broadcasted_iota(jnp.int32, shape, axis)
    chunks = range(len(cuts) - 1)
    part = [pl.ds(cuts[j], cuts[j + 1] - cuts[j]) for j in chunks]

    @pl.when(jnp.logical_not(comes))
    def _():
        grads_ref[2] = jnp.zeros_like(grads_ref[2])

    barrier = pltpu.get_barrier_semaphore()

    def greet(d, carry):
        pl.semaphore_signal(barrier, inc=1, device_id=place((me + d) % devices), device_id_type=MESH)
        return carry

    lax.fori_loop(1, devices, greet, 0)
    arrived_ref[me] = give_ref[me]
    apart_ref[...] = jnp.zeros_like(apart_ref)
    pl.semaphore_wait(barrier, devices - 1)

    def remote(source, target, send, recv, device):
        return pltpu.make_async_remote_copy(
            src_ref=source, dst_ref=target, send_sem=send, recv_sem=recv, device_id=device, device_id_type=MESH
        )

    for j in chunks:

        def give(d, carry):
            other = (me + d) % devices
            remote(
                give_ref.at[other, :, part[j]], arrived_ref.at[me, :, part[j]],
                give_send.at[j, other], give_recv.at[j, me], place(other),
            ).start()
            return carry

        lax.fori_loop(1, devices, give, 0)

    total = 9 * slots
    flat = (1, total)
    at = iota(flat, 1).astype(jnp.float32)
    block = jnp.floor((at + 0.5) / slots)
    within = at - block * slots
    source = jnp.floor((within + 0.5) / slots_each)
    order = within - source * slots_each
    up = jnp.floor((block + 0.5) / 3.0)
    along = block - 3.0 * up
    lat_shift = jnp.where(up == 0.0, 0.0, jnp.where(up == 1.0, 1.0, -1.0)) * near.astype(jnp.float32)
    lon_shift = jnp.where(along == 0.0, 0.0, jnp.where(along == 1.0, -1.0, 1.0))
    owner_row = jnp.clip(row.astype(jnp.float32) + lat_shift, 0.0, lat - 1.0)
    owner_col = column.astype(jnp.float32) + lon_shift
    owner_col = jnp.where(owner_col < 0.0, owner_col + lon, jnp.where(owner_col >= lon, owner_col - lon, owner_col))
    wanted = ((owner_row * lon + owner_col) * slots_each + order).astype(jnp.int32)
    listed = table_ref[...].reshape(devices, table_ref.shape[2])
    chosen = jnp.where(iota((listed.shape[1], total), 0) == wanted, 1.0, 0.0).astype(jnp.bfloat16)
    mine = iota((devices, total), 0) == source.astype(jnp.int32)

    def position(values):
        found = matmul(values.astype(jnp.bfloat16), chosen)
        return jnp.sum(jnp.where(mine, found, 0.0), axis=0, keepdims=True)

    slot_row = position(listed >> log_lon) + lat_shift * lat_rows
    slot_col = position(listed & (lon_cols - 1)) + lon_shift * lon_cols
    down = iota((lon_cols, total), 0).astype(jnp.float32)
    col_weight = tap_value(slot_col - down, lon_cols // 2)
    for i in range(0, lat_rows, 2):
        for k in range(2):
            value = col_weight * tap_value(slot_row - (i + k), LHALF)
            high, low = halves(value)
            weight_ref[i // 2, k * lon_cols:(k + 1) * lon_cols, :] = high
            weight_ref[i // 2, (k + 2) * lon_cols:(k + 3) * lon_cols, :] = low

    padded = iota((slots, devices * 8), 1)
    compact = jnp.logical_and(
        iota((slots, devices * 8), 0) == (padded >> 3) * slots_each + (padded & 7), (padded & 7) < slots_each
    )
    compact = jnp.where(compact, 1.0, 0.0).astype(jnp.bfloat16)

    def receive(j):
        def wait(d, carry):
            other = (me + d) % devices
            copy = remote(
                give_ref.at[other, :, part[j]], arrived_ref.at[other, :, part[j]],
                give_send.at[j, other], give_recv.at[j, other], place(other),
            )
            copy.wait_send()
            copy.wait_recv()
            return carry

        lax.fori_loop(1, devices, wait, 0)
        apart_ref[:, :slots_each, part[j]] = arrived_ref[:, :, part[j]].astype(jnp.float32)
        wide = apart_ref[:, :, part[j]].reshape(devices * 8, cuts[j + 1] - cuts[j]).astype(jnp.bfloat16)
        grads_ref[0, 0, :, part[j]] = matmul(compact, wide).astype(jnp.bfloat16)

    def swap(j, b):
        return remote(
            grads_ref.at[0, b, :, part[j]], grads_ref.at[1, b, :, part[j]],
            swap_send.at[j, b], swap_recv.at[j, b], (partner, column),
        )

    def forward(j, b):
        return remote(
            grads_ref.at[1, b, :, part[j]], grads_ref.at[2, b, :, part[j]],
            far_send.at[j, b], far_recv.at[j, b], (row + step, column),
        )

    def to_right(j, a):
        return remote(
            grads_ref.at[a, 0, :, part[j]], grads_ref.at[a, 1, :, part[j]],
            lon_send.at[0, j, a], lon_recv.at[0, j, a], (row, (column + 1) % lon),
        )

    def to_left(j, a):
        return remote(
            grads_ref.at[a, 0, :, part[j]], grads_ref.at[a, 2, :, part[j]],
            lon_send.at[1, j, a], lon_recv.at[1, j, a], (row, (column + lon - 1) % lon),
        )

    def send_lon(j, a):
        to_right(j, a).start()
        to_left(j, a).start()

    def await_lon(j, a):
        to_right(j, a).wait_recv()
        to_left(j, a).wait_recv()

    def pass_on(j, b):
        swap(j, b).wait_recv()

        @pl.when(onward)
        def _():
            forward(j, b).start()

    def await_far(j, b):
        @pl.when(comes)
        def _():
            forward(j, b).wait_recv()

    def compute(j):
        count = cuts[j + 1] - cuts[j]
        kept = min(count, rows // lat_rows - cuts[j])
        grads = grads_ref[:, :, :, part[j]].reshape(total, count)

        def two(i, carry):
            result = matmul(weight_ref[i], grads)
            result = (result[: 2 * lon_cols] + result[2 * lon_cols:]) * std_ref[:, part[j]]
            for k in range(2):
                piece = result[k * lon_cols:(k + 1) * lon_cols].T
                out_ref[pl.ds(cuts[j] * lat_rows + 2 * i + k, kept, stride=lat_rows), :] = piece[:kept]
            return carry

        lax.fori_loop(0, lat_rows // 2, two, 0)

    lon_first, lat_first = chunks[:1], chunks[1:]
    for j in lon_first:
        receive(j)
        send_lon(j, 0)
    for j in lat_first:
        receive(j)
        swap(j, 0).start()
    for j in lon_first:
        swap(j, 0).start()
        await_lon(j, 0)
        swap(j, 1).start()
        swap(j, 2).start()
    for j in lat_first:
        pass_on(j, 0)
        send_lon(j, 0)
        send_lon(j, 1)
    for j in lon_first:
        pass_on(j, 0)
    for j in lat_first:
        await_far(j, 0)
        send_lon(j, 2)
    for b in (1, 2):
        for j in lon_first:
            pass_on(j, b)
    for b in range(3):
        for j in lon_first:
            await_far(j, b)
    for j in lon_first:
        compute(j)
    for j in lat_first:
        for a in range(3):
            await_lon(j, a)
        compute(j)
    for j in chunks:
        for b in range(3) if j in lon_first else (0,):
            swap(j, b).wait_send()

            @pl.when(onward)
            def _():
                forward(j, b).wait_send()

        for a in (0,) if j in lon_first else range(3):
            to_right(j, a).wait_send()
            to_left(j, a).wait_send()


def adjoint_step(outgoing, table, std_dev, lat_rows, lon_cols):
    lat, lon = lax.axis_size("lat"), lax.axis_size("lon")
    devices, slots_each, lanes = outgoing.shape
    slots, width = devices * slots_each, std_dev.shape[0]
    cuts = [*range(0, width // 256 * 256 + 1, 256), lanes]
    pieces = len(cuts) - 1
    std_dev = jnp.pad(std_dev, (0, lanes - width))[None, :]
    vmem = pl.BlockSpec(memory_space=pltpu.VMEM)
    dma = pltpu.SemaphoreType.DMA
    bf16, f32 = jnp.bfloat16, jnp.float32
    return pl.pallas_call(
        functools.partial(adjoint_kernel, lat, lon, lat_rows, cuts),
        in_specs=[vmem] * 3,
        out_specs=vmem,
        out_shape=jax.ShapeDtypeStruct((width * lat_rows, lon_cols), f32),
        scratch_shapes=[
            pltpu.VMEM((devices, slots_each, lanes), bf16),
            pltpu.VMEM((devices, 8, lanes), f32),
            pltpu.VMEM((3, 3, slots, lanes), bf16),
            pltpu.VMEM((lat_rows // 2, 4 * lon_cols, 9 * slots), bf16),
            *[dma((pieces, devices))] * 2,
            *[dma((pieces, 3))] * 4,
            *[dma((2, pieces, 3))] * 2,
        ],
        compiler_params=pltpu.CompilerParams(collective_id=1, has_side_effects=True),
        name="adjoint",
    )(outgoing, table, std_dev)


def local(control, std_dev, col_dev, col_cell, jacobian, innovation, inv_error):
    width, lat_rows, lon_cols = control.shape
    devices = lax.axis_size("lat") * lax.axis_size("lon")
    slots_each = max(2, 2 * col_cell.shape[0] // devices)
    increment, table, got = dense_step(control, col_dev, col_cell, std_dev, slots_each)
    departures, outgoing, increment = sounding_step(jacobian, got, col_dev, innovation, inv_error, increment)
    adjoint = adjoint_step(outgoing, table, std_dev, lat_rows, lon_cols)
    return departures, increment.reshape(control.shape), adjoint.reshape(control.shape)


def solution(mesh):
    placed = (
        P(None, "lat", "lon"),
        P(),
        P(("lat", "lon"), None),
        P(("lat", "lon")),
        P(("lat", "lon"), None, None),
        P(("lat", "lon"), None),
        P(),
    )
    return jax.shard_map(
        local,
        mesh=mesh,
        in_specs=placed,
        out_specs=(P(("lat", "lon"), None), P(None, "lat", "lon"), P(None, "lat", "lon")),
        check_vma=False,
    )
```

```python
import functools
import math

import jax
import jax.numpy as jnp
from jax import lax
from jax.experimental import pallas as pl
from jax.experimental.pallas import tpu as pltpu
from jax.sharding import PartitionSpec as P

LHALF = 8
MESH = pl.DeviceIdType.MESH


def tap_weights(offset, half_width):
    spread = 2.0 * half_width / 3.0
    taps = jnp.arange(-half_width, half_width + 1, dtype=jnp.int32).astype(jnp.float32)
    norm_total = jnp.sqrt(jnp.sum(jnp.exp(-taps * taps / (spread * spread))))
    weights = jnp.exp(-offset * offset / (2.0 * spread * spread)) / norm_total
    return jnp.where(jnp.abs(offset) <= half_width, weights, jnp.zeros_like(weights))


def halves(weights):
    high = weights.astype(jnp.bfloat16)
    return high, (weights - high.astype(jnp.float32)).astype(jnp.bfloat16)


def tap_value(offset, half_width):
    spread = 2.0 * half_width / 3.0
    norm_total = math.sqrt(sum(math.exp(-e * e / (spread * spread)) for e in range(-half_width, half_width + 1)))
    weights = jnp.exp(-offset * offset / (2.0 * spread * spread)) / norm_total
    return jnp.where(jnp.abs(offset) <= half_width, weights, 0.0)


GROUP = 256
CHUNK = 2 * GROUP


def matmul(left, right):
    return jnp.dot(left, right, preferred_element_type=jnp.float32)


def across(left, right):
    return lax.dot_general(left, right, (((1,), (1,)), ((), ())), preferred_element_type=jnp.float32)


def slots_of(dev_ref, cell_ref, slots_each, count):
    sound_count = dev_ref.shape[1]
    square = (sound_count, sound_count)
    iota = lambda shape, axis: lax.broadcasted_iota(jnp.int32, shape, axis)
    before = iota(square, 0) - iota(square, 1)
    across_lanes = jnp.broadcast_to(dev_ref[...].astype(jnp.float32), square)
    upright = lambda spread: jnp.sum(jnp.where(before == 0, spread, 0.0), axis=1, keepdims=True)
    down = upright(across_lanes)
    alike = across_lanes == down
    order = jnp.sum(jnp.where(jnp.logical_and(alike, before > 0), 1.0, 0.0), axis=1, keepdims=True)
    slot = down * slots_each + order
    onehot = slot.astype(jnp.int32) == iota((sound_count, count), 1)
    cell = upright(jnp.broadcast_to(cell_ref[...].astype(jnp.float32), square))
    order = jnp.sum(jnp.where(jnp.logical_and(alike, before < 0), 1.0, 0.0), axis=0, keepdims=True)
    return onehot, cell, (dev_ref[...].astype(jnp.float32) * slots_each + order).astype(jnp.int32)


def dense_kernel(
    lat, lon, lat_rows, slots_each,
    ctrl_hbm, dev_ref, ask_ref, std_ref,
    inc_hbm, table_ref, got_ref,
    ctrl_ref, inc_ref, wanted_ref, own_ref, swap_ref, far_ref, g_ref, to_right_ref, to_left_ref, from_left_ref, from_right_ref,
    band_ref, mid_ref, edge_ref, std_row_ref, cell_ref, row_ref, pick_ref,
    swap_send, swap_recv, far_send, far_recv, lon_send, lon_recv,
    want_send, want_recv, col_send, col_recv, load_sem, store_sem,
):
    rows, lon_cols = ctrl_ref.shape
    width = rows // lat_rows
    full, rest = rows // CHUNK, rows % CHUNK
    early = full // 4 * 2
    log_lat, log_lon = lat_rows.bit_length() - 1, lon_cols.bit_length() - 1
    lon_half = lon_cols // 2
    row, column = lax.axis_index("lat"), lax.axis_index("lon")
    devices, me = lat * lon, row * lon + column
    odd = row % 2
    partner, step = row + 1 - 2 * odd, 2 - 4 * odd
    onward = jnp.logical_and(row + step >= 0, row + step < lat)
    comes = jnp.logical_and(row - step >= 0, row - step < lat)
    place = lambda other: (other // lon, other % lon)
    iota = lambda shape, axis: lax.broadcasted_iota(jnp.int32, shape, axis)

    barrier = pltpu.get_barrier_semaphore()

    def greet(d, carry):
        pl.semaphore_signal(barrier, inc=1, device_id=place((me + d) % devices), device_id_type=MESH)
        return carry

    lax.fori_loop(1, devices, greet, 0)

    def chunk_of(k):
        return pl.ds(pl.multiple_of(k * CHUNK, CHUNK), CHUNK)

    def half_of(k):
        return pl.ds(pl.multiple_of(k * GROUP, GROUP), GROUP)

    last, last_half = pl.ds(full * CHUNK, rest), pl.ds(full * GROUP, rest // 2)

    def remote(source, target, send, recv, device):
        return pltpu.make_async_remote_copy(
            src_ref=source, dst_ref=target, send_sem=send, recv_sem=recv, device_id=device, device_id_type=MESH
        )

    def request(dst, send, recv, other):
        return remote(wanted_ref.at[0], table_ref.at[dst], want_send.at[send], want_recv.at[recv], place(other))

    def swap(k, part):
        return remote(own_ref.at[part], swap_ref.at[part], swap_send.at[k], swap_recv.at[k], (partner, column))

    def forward(k, part):
        return remote(swap_ref.at[part], far_ref.at[part], far_send.at[k], far_recv.at[k], (row + step, column))

    def to_right(k, part):
        return remote(
            to_right_ref.at[part], from_left_ref.at[part], lon_send.at[0, k], lon_recv.at[0, k],
            (row, (column + 1) % lon),
        )

    def to_left(k, part):
        return remote(
            to_left_ref.at[part], from_right_ref.at[part], lon_send.at[1, k], lon_recv.at[1, k],
            (row, (column + lon - 1) % lon),
        )

    def back(d, group):
        part = pl.ds(pl.multiple_of(group * lon_cols, lon_cols), lon_cols)
        return remote(
            pick_ref.at[d, :, part], got_ref.at[me, :, part], col_send.at[d], col_recv.at[me], place(d)
        )

    def round_own(part):
        own_ref[part, :] = ctrl_ref[part, :].astype(jnp.bfloat16)

    def load(k, part):
        return pltpu.make_async_copy(ctrl_hbm.at[part], ctrl_ref.at[part], load_sem.at[k])

    def store(k, part):
        return pltpu.make_async_copy(inc_ref.at[part], inc_hbm.at[part], store_sem.at[k])

    def begin(k, carry):
        load(k, chunk_of(k)).start()
        return carry

    lax.fori_loop(0, full, begin, 0)
    load(full, last).start()
    onehot, cell_at, _ = slots_of(dev_ref, ask_ref, slots_each, wanted_ref.shape[2])
    wanted_ref[0] = jnp.sum(jnp.where(onehot, cell_at, 0.0), axis=0, keepdims=True).astype(jnp.int32)

    @pl.when(jnp.logical_not(comes))
    def _():
        far_ref[...] = jnp.zeros_like(far_ref)

    load(0, chunk_of(0)).wait()
    round_own(chunk_of(0))
    pl.semaphore_wait(barrier, devices - 1)

    def ask(d, carry):
        request(me, (me + d) % devices, me, (me + d) % devices).start()
        return carry

    lax.fori_loop(1, devices, ask, 0)

    def send_own(k, carry):
        load(k + 1, chunk_of(k + 1)).wait()

        @pl.when(k + 1 < early)
        def _():
            round_own(chunk_of(k + 1))

        swap(k, chunk_of(k)).start()
        return carry

    lax.fori_loop(0, early, send_own, 0)
    lane = iota((1, lon_cols), 1)

    def pack(first, second, part):
        right = jnp.where(lane < lon_half, pltpu.roll(first, lon_half, 1), second)
        left = jnp.where(lane < lon_half, first, pltpu.roll(second, lon_half, 1))
        to_right_ref[part, :] = right.astype(jnp.bfloat16)
        to_left_ref[part, :] = left.astype(jnp.bfloat16)

    def send_lon(k, part):
        to_right(k, part).start()
        to_left(k, part).start()

    def pack_own(k, carry):
        base = pl.multiple_of(k * CHUNK, CHUNK)
        pack(ctrl_ref[pl.ds(base, GROUP), :], ctrl_ref[pl.ds(base + GROUP, GROUP), :], half_of(k))

        @pl.when(k + 1 < full)
        def _():
            load(k + 1, chunk_of(k + 1)).wait()

        send_lon(k, half_of(k))
        return carry

    lax.fori_loop(early, full, pack_own, 0)
    load(full, last).wait()
    middle = full * CHUNK + rest // 2
    pack(ctrl_ref[full * CHUNK:middle, :], ctrl_ref[middle:, :], last_half)
    table_ref[me] = wanted_ref[0]
    send_lon(full, last_half)

    square = (GROUP, GROUP)
    same = (iota(square, 0) >> log_lat) == (iota(square, 1) >> log_lat)
    apart = (iota(square, 1) & (lat_rows - 1)) - (iota(square, 0) & (lat_rows - 1))

    def lat_band(shift):
        return halves(jnp.where(same, tap_value((apart + shift).astype(jnp.float32), LHALF), 0.0))

    high, low = lat_band(0)
    swap_high, swap_low = lat_band(lat_rows - 2 * lat_rows * odd)
    far_high, far_low = lat_band(2 * lat_rows * odd - lat_rows)
    for at, block in enumerate((high, high, low, swap_high, swap_low, far_high, far_low)):
        band_ref[:, at * GROUP:(at + 1) * GROUP] = block
    along = iota((lon_cols, lon_cols), 0) - iota((lon_cols, lon_cols), 1)
    high, low = halves(tap_value(along.astype(jnp.float32), lon_half))
    mid_ref[:, :lon_cols] = high
    mid_ref[:, lon_cols:] = low
    wide = (2 * lon_cols, 2 * lon_cols)
    source, target = iota(wide, 0), iota(wide, 1)
    within, which = source & (lon_half - 1), (source >> (log_lon - 1)) & 1
    column_at = jnp.where(source < lon_cols, within - lon_half, within + lon_cols)
    apart = column_at - (target & (lon_cols - 1))
    value = jnp.where(which == (target >> log_lon), tap_value(apart.astype(jnp.float32), lon_half), 0.0)
    high, low = halves(value)
    edge_ref[0] = high
    edge_ref[1] = low

    def spread(c, carry):
        std_row_ref[pl.ds(pl.multiple_of(c * lat_rows, lat_rows), lat_rows), :] = jnp.full(
            (lat_rows, lon_cols), std_ref[c], jnp.float32
        )
        return carry

    lax.fori_loop(0, width, spread, 0)

    def hear(d, carry):
        other = (me + d) % devices
        asked = request(other, other, other, other)
        asked.wait_send()
        asked.wait_recv()
        return carry

    lax.fori_loop(1, devices, hear, 0)
    listed = jnp.broadcast_to(table_ref[...].astype(jnp.float32), (devices, 8, table_ref.shape[2]))
    wants = iota(listed.shape, 2) == iota(listed.shape, 1) + me * slots_each
    cell = jnp.sum(jnp.where(wants, listed, 0.0), axis=2, keepdims=True).astype(jnp.int32)
    cell = jnp.broadcast_to(cell, (devices, 8, lon_cols)).reshape(devices * 8, lon_cols)
    row_ref[...] = cell >> log_lon
    cell_ref[...] = jnp.where((cell & (lon_cols - 1)) == iota(cell.shape, 1), 1.0, 0.0).astype(jnp.bfloat16)

    def lat_product(ref, first, second):
        def pair(ref):
            return jnp.concatenate([ref[first, :], ref[second, :]], axis=1)

        field = pair(ref)
        field_high, field_low = halves(field)
        swapped, far = pair(swap_ref), pair(far_ref)
        stacked = jnp.concatenate([field_high, field_low, field_high, swapped, swapped, far, far], axis=0)
        return matmul(band_ref[...], stacked)

    def lat_then_send(k):
        base = pl.multiple_of(k * CHUNK, CHUNK)
        first, second = pl.ds(base, GROUP), pl.ds(base + GROUP, GROUP)
        result = lat_product(ctrl_ref, first, second)
        top, bottom = result[:, :lon_cols], result[:, lon_cols:]
        g_ref[first, :] = top
        g_ref[second, :] = bottom
        pack(top, bottom, half_of(k))

    def lat_last(k):
        base = pl.multiple_of(k * CHUNK, CHUNK)
        first, second = pl.ds(base, GROUP), pl.ds(base + GROUP, GROUP)
        result = lat_product(g_ref, first, second)
        inc_ref[first, :] = result[:, :lon_cols] * std_row_ref[first, :]
        inc_ref[second, :] = result[:, lon_cols:] * std_row_ref[second, :]

    def lat_rest():
        result = lat_product(g_ref, pl.ds(rows - CHUNK, GROUP), pl.ds(rows - GROUP, GROUP))
        kept = jnp.concatenate([result[:, :lon_cols], result[:, lon_cols:]], axis=0)[CHUNK - rest:]
        inc_ref[last, :] = kept * std_row_ref[last, :]

    def lon_product(ref, start, count, part):
        half = count // 2
        both = jnp.concatenate([from_left_ref[part, :], from_right_ref[part, :]], axis=1)
        sides = matmul(both, edge_ref[0]) + matmul(both, edge_ref[1])
        high, low = halves(ref[pl.ds(start, count), :])
        own = matmul(high, mid_ref[...])
        own = own[:, :lon_cols] + own[:, lon_cols:] + matmul(low, mid_ref[:, :lon_cols])
        return own[:half] + sides[:, :lon_cols], own[half:] + sides[:, lon_cols:]

    def lon_last(k):
        base = pl.multiple_of(k * CHUNK, CHUNK)
        first, second = pl.ds(base, GROUP), pl.ds(base + GROUP, GROUP)
        top, bottom = lon_product(g_ref, base, CHUNK, half_of(k))
        inc_ref[first, :] = top * std_row_ref[first, :]
        inc_ref[second, :] = bottom * std_row_ref[second, :]

    def lon_first(start, count, part):
        first, second = pl.ds(start, count // 2), pl.ds(start + count // 2, count // 2)
        top, bottom = lon_product(ctrl_ref, start, count, part)
        g_ref[first, :] = top
        g_ref[second, :] = bottom
        own_ref[first, :] = top.astype(jnp.bfloat16)
        own_ref[second, :] = bottom.astype(jnp.bfloat16)

    def pick(start, count, group):
        values = inc_ref[pl.ds(start, count), :].astype(jnp.bfloat16)
        found = across(cell_ref[...], values)
        mine = (iota(row_ref.shape, 1) & (lat_rows - 1)) == row_ref[...]
        parts = []
        for at in range(0, count, lon_cols):
            piece = found[:, at:at + lon_cols]
            parts.append(jnp.where(mine[:, : piece.shape[1]], piece, 0.0).astype(jnp.bfloat16))
        masked = jnp.concatenate(parts, axis=1)
        gather = (iota((count, lon_cols), 0) >> log_lat) == iota((count, lon_cols), 1)
        result = matmul(masked, jnp.where(gather, 1.0, 0.0).astype(jnp.bfloat16))
        result = result.reshape(devices, 8, lon_cols)[:, :slots_each, :]
        pick_ref[:, :, pl.ds(pl.multiple_of(group * lon_cols, lon_cols), lon_cols)] = result.astype(jnp.bfloat16)

    def send_back(group):
        def give(d, carry):
            back((me + d) % devices, group).start()
            return carry

        lax.fori_loop(1, devices, give, 0)

    def stage(k, carry):
        def arrive(k, part):
            swap(k, part).wait_recv()

            @pl.when(onward)
            def _():
                forward(k, part).start()

        def await_far(k, part):
            @pl.when(comes)
            def _():
                forward(k, part).wait_recv()

        @pl.when(k < full)
        def _():
            arrive(k, chunk_of(k))

        @pl.when(k == full)
        def _():
            arrive(full, last)

        def await_lon(k, part):
            to_right(k, part).wait_recv()
            to_left(k, part).wait_recv()

        ahead, behind, done = k + early, k - 2, k - 4

        @pl.when(ahead < full)
        def _():
            await_lon(ahead, half_of(ahead))
            lon_first(pl.multiple_of(ahead * CHUNK, CHUNK), CHUNK, half_of(ahead))
            swap(ahead, chunk_of(ahead)).start()

        @pl.when(ahead == full)
        def _():
            await_lon(full, last_half)
            lon_first(full * CHUNK, rest, last_half)
            swap(full, last).start()

        @pl.when(jnp.logical_and(behind >= 0, behind < early))
        def _():
            await_far(behind, chunk_of(behind))
            lat_then_send(behind)

        @pl.when(jnp.logical_and(done >= 0, done < early))
        def _():
            await_lon(done, half_of(done))
            lon_last(done)
            store(done, chunk_of(done)).start()

        @pl.when(jnp.logical_and(behind >= 0, behind < early))
        def _():
            send_lon(behind, half_of(behind))

        @pl.when(jnp.logical_and(behind >= early, behind < full))
        def _():
            await_far(behind, chunk_of(behind))
            lat_last(behind)
            store(behind, chunk_of(behind)).start()

        def give(group):
            pick(pl.multiple_of(group * 2 * CHUNK, 2 * CHUNK), 2 * CHUNK, group)
            send_back(group)

        @pl.when(jnp.logical_and(jnp.logical_and(done >= 0, done < early), done % 2 == 1))
        def _():
            give(done // 2)

        @pl.when(jnp.logical_and(jnp.logical_and(behind >= early, behind < full), behind % 2 == 1))
        def _():
            give(behind // 2)

        @pl.when(behind == full)
        def _():
            await_far(full, last)
            lat_rest()
            store(full, last).start()
            pick(full * CHUNK, rest, full // 2)
            send_back(full // 2)

        return carry

    lax.fori_loop(0, full + 3, stage, 0)
    got_ref[me] = pick_ref[me]

    def finish(k, part, half):
        swap(k, part).wait_send()

        @pl.when(onward)
        def _():
            forward(k, part).wait_send()

        store(k, part).wait()
        to_right(k, half).wait_send()
        to_left(k, half).wait_send()

    def finish_full(k, carry):
        finish(k, chunk_of(k), half_of(k))
        return carry

    lax.fori_loop(0, full, finish_full, 0)
    finish(full, last, last_half)

    def collect(d, carry):
        other = (me + d) % devices
        whole = remote(
            pick_ref.at[other], got_ref.at[other], col_send.at[other], col_recv.at[other], place(other)
        )
        whole.wait_send()
        whole.wait_recv()
        return carry

    lax.fori_loop(1, devices, collect, 0)


def dense_step(control, col_dev, col_cell, std_dev, slots_each):
    lat, lon = lax.axis_size("lat"), lax.axis_size("lon")
    width, lat_rows, lon_cols = control.shape
    devices, rows = lat * lon, width * lat_rows
    pieces = rows // CHUNK + 1
    lanes = lane_tiles(width) * lon_cols
    listed = (1, lane_tiles(devices * slots_each) * 128)
    vmem, hbm = pl.BlockSpec(memory_space=pltpu.VMEM), pl.BlockSpec(memory_space=pl.ANY)
    dma = pltpu.SemaphoreType.DMA
    bf16, f32 = jnp.bfloat16, jnp.float32
    return pl.pallas_call(
        functools.partial(dense_kernel, lat, lon, lat_rows, slots_each),
        in_specs=[hbm, vmem, vmem, pl.BlockSpec(memory_space=pltpu.SMEM)],
        out_specs=[hbm, vmem, vmem],
        out_shape=[
            jax.ShapeDtypeStruct((rows, lon_cols), f32),
            jax.ShapeDtypeStruct((devices, *listed), jnp.int32),
            jax.ShapeDtypeStruct((devices, slots_each, lanes), bf16),
        ],
        scratch_shapes=[
            pltpu.VMEM((rows, lon_cols), f32),
            pltpu.VMEM((rows, lon_cols), f32),
            pltpu.VMEM((1, *listed), jnp.int32),
            pltpu.VMEM((rows, lon_cols), bf16),
            pltpu.VMEM((rows, lon_cols), bf16),
            pltpu.VMEM((rows, lon_cols), bf16),
            pltpu.VMEM((rows, lon_cols), f32),
            *[pltpu.VMEM((rows // 2, lon_cols), bf16)] * 4,
            pltpu.VMEM((GROUP, 7 * GROUP), bf16),
            pltpu.VMEM((lon_cols, 2 * lon_cols), bf16),
            pltpu.VMEM((2, 2 * lon_cols, 2 * lon_cols), bf16),
            pltpu.VMEM((rows, lon_cols), f32),
            pltpu.VMEM((devices * 8, lon_cols), bf16),
            pltpu.VMEM((devices * 8, lon_cols), jnp.int32),
            pltpu.VMEM((devices, slots_each, lanes), bf16),
            *[dma((pieces,))] * 4,
            *[dma((2, pieces))] * 2,
            *[dma((devices,))] * 4,
            *[dma((pieces,))] * 2,
        ],
        compiler_params=pltpu.CompilerParams(collective_id=0, has_side_effects=True),
        name="dense",
    )(control.reshape(rows, lon_cols), col_dev.reshape(1, -1), col_cell[None, :], std_dev)


def lane_tiles(count):
    return -(-count // 128)


PIECE = 16


def piece_slot(index, slots_each, piece, kind):
    device, row = index >> 4, index & (PIECE - 1)
    spare = PIECE - 2 * slots_each
    if kind < 2:
        number = row - kind * slots_each
        valid = jnp.logical_and(number >= 0, number < slots_each)
    else:
        number = row - 2 * slots_each + piece * spare
        valid = jnp.logical_and(row >= 2 * slots_each, number < slots_each)
    return jnp.where(valid, device * 8 + number, -1)


def sounding_kernel(
    slots_each, step,
    jac_hbm, got_ref, dev_ref, innov_ref, inv_ref, field_hbm,
    dep_ref, out_ref, copy_hbm,
    jac_ref, field_ref, apart_ref, col_ref, tail_ref, weight_ref, grad_ref, jac_sem, field_sem,
):
    channels, count, width = jac_ref.shape
    steps = channels // step
    devices, lanes = got_ref.shape[0], got_ref.shape[2]
    most = width // 128 * 128
    iota = lambda shape, axis: lax.broadcasted_iota(jnp.int32, shape, axis)

    def load(b):
        part = pl.ds(b * step, step)
        return pltpu.make_async_copy(jac_hbm.at[part], jac_ref.at[part], jac_sem.at[b])

    take = pltpu.make_async_copy(field_hbm, field_ref, field_sem.at[0])
    leave = pltpu.make_async_copy(field_ref, copy_hbm, field_sem.at[1])
    load(0).start()
    take.start()

    def begin(b, carry):
        load(b).start()
        return carry

    lax.fori_loop(1, steps, begin, 0)
    apart_ref[...] = jnp.zeros_like(apart_ref)
    apart_ref[:, :slots_each, :] = got_ref[...].astype(jnp.float32)
    onehot, _, slot = slots_of(dev_ref, dev_ref, 8, devices * 8)
    onehot = jnp.where(onehot, 1.0, 0.0).astype(jnp.bfloat16)
    columns = matmul(onehot, apart_ref[...].reshape(devices * 8, lanes).astype(jnp.bfloat16))
    col_ref[...] = columns.astype(jnp.bfloat16)
    tail_ref[...] = columns[:, most:]
    grad_ref[...] = jnp.zeros_like(grad_ref)
    square = (count, count)

    def product(b):
        block = jac_ref[pl.ds(b * step, step), :, :most]
        return across(block.reshape(step * count, most), col_ref[:, :most])

    def depart(b, found):
        mine = iota(square, 0) == iota(square, 1)
        for k in range(step):
            channel = b * step + k
            own = jnp.where(mine, found[k * count:(k + 1) * count] - innov_ref[pl.ds(channel, 1), :], 0.0)
            if width > most:
                tail = jac_ref[channel, :, most:].astype(jnp.float32) * tail_ref[:, : width - most]
                own = own + jnp.concatenate([tail, jnp.zeros((count, count - (width - most)), jnp.float32)], axis=1)
            departure = jnp.sum(own, axis=1, keepdims=True)
            dep_ref[pl.ds(channel, 1), :] = jnp.sum(jnp.where(mine, departure, 0.0), axis=0, keepdims=True)
            weight = (departure * inv_ref[channel]).astype(jnp.bfloat16).astype(jnp.float32)
            weight_ref[k] = jnp.broadcast_to(weight, (count, 128))

    def gradient(b):
        for group in range(0, count, 16):
            part = slice(group, group + 16)
            for lane in range(0, width, 128):
                end = min(lane + 128, width)
                total = grad_ref[part, lane:end]
                for k in range(step):
                    values = jac_ref[b * step + k, part, lane:end].astype(jnp.float32)
                    total = total + values * weight_ref[k, part, : end - lane]
                grad_ref[part, lane:end] = total

    load(0).wait()
    depart(0, product(0))
    take.wait()
    leave.start()

    def body(b, carry):
        load(b).wait()
        found = product(b)
        gradient(b - 1)
        depart(b, found)
        return carry

    lax.fori_loop(1, steps, body, 0)
    gradient(steps - 1)
    grads = grad_ref[...].astype(jnp.bfloat16)
    for piece in range(2):
        packed = jnp.zeros((devices * PIECE, 128), jnp.float32)
        for kind in range(3):
            held = piece_slot(iota((devices * PIECE, count), 0), slots_each, piece, kind)
            onehot = jnp.where(held == slot, 1.0, 0.0).astype(jnp.bfloat16)
            tile = (2 * piece + kind if kind < 2 else 4) * 128
            packed = packed + matmul(onehot, grads[:, tile:tile + 128])
        out_ref[piece] = packed.astype(out_ref.dtype)
    leave.wait()


def sounding_step(jacobian, got, col_dev, innovation, inv_error, field):
    count, channels, width = jacobian.shape
    devices, slots_each, lanes = got.shape
    step = next(n for n in (10, 8, 6, 5, 4, 3, 2, 1) if channels % n == 0)
    vmem, hbm = pl.BlockSpec(memory_space=pltpu.VMEM), pl.BlockSpec(memory_space=pl.ANY)
    departures, grad, field = pl.pallas_call(
        functools.partial(sounding_kernel, slots_each, step),
        in_specs=[hbm, vmem, vmem, vmem, pl.BlockSpec(memory_space=pltpu.SMEM), hbm],
        out_specs=[vmem, vmem, hbm],
        out_shape=[
            jax.ShapeDtypeStruct((channels, count), jnp.float32),
            jax.ShapeDtypeStruct((2, devices * PIECE, 128), jnp.bfloat16),
            jax.ShapeDtypeStruct(field.shape, jnp.float32),
        ],
        scratch_shapes=[
            pltpu.VMEM((channels, count, width), jnp.bfloat16),
            pltpu.VMEM(field.shape, jnp.float32),
            pltpu.VMEM((devices, 8, lanes), jnp.float32),
            pltpu.VMEM((count, lanes), jnp.bfloat16),
            pltpu.VMEM((count, 128), jnp.float32),
            pltpu.VMEM((step, count, 128), jnp.float32),
            pltpu.VMEM((count, lanes), jnp.float32),
            pltpu.SemaphoreType.DMA((channels // step,)),
            pltpu.SemaphoreType.DMA((2,)),
        ],
        name="soundings",
    )(jnp.transpose(jacobian, (1, 0, 2)), got, col_dev.reshape(1, -1), innovation.T, inv_error, field)
    return departures.T, grad, field


def adjoint_kernel(
    lat, lon, lat_rows, slots_each, cuts,
    give_ref, table_ref, std_ref, out_ref,
    arrived_ref, compact_ref, grads_ref, weight_ref,
    give_send, give_recv, swap_send, swap_recv, far_send, far_recv, lon_send, lon_recv,
):
    devices = lat * lon
    slots = devices * slots_each
    rows, lon_cols = out_ref.shape
    log_lon = lon_cols.bit_length() - 1
    row, column = lax.axis_index("lat"), lax.axis_index("lon")
    me = row * lon + column
    odd = row % 2
    near = 1 - 2 * odd
    partner, step = row + near, 2 * near
    onward = jnp.logical_and(row + step >= 0, row + step < lat)
    comes = jnp.logical_and(row - step >= 0, row - step < lat)
    place = lambda other: (other // lon, other % lon)
    iota = lambda shape, axis: lax.broadcasted_iota(jnp.int32, shape, axis)
    chunks = range(len(cuts) - 1)
    part = [pl.ds(cuts[j], cuts[j + 1] - cuts[j]) for j in chunks]

    @pl.when(jnp.logical_not(comes))
    def _():
        grads_ref[2] = jnp.zeros_like(grads_ref[2])

    barrier = pltpu.get_barrier_semaphore()

    def greet(d, carry):
        pl.semaphore_signal(barrier, inc=1, device_id=place((me + d) % devices), device_id_type=MESH)
        return carry

    lax.fori_loop(1, devices, greet, 0)

    def piece_of(d):
        return pl.ds(pl.multiple_of(d * PIECE, PIECE), PIECE)

    arrived_ref[:, piece_of(me), :] = give_ref[:, piece_of(me), :]
    pl.semaphore_wait(barrier, devices - 1)

    def remote(source, target, send, recv, device):
        return pltpu.make_async_remote_copy(
            src_ref=source, dst_ref=target, send_sem=send, recv_sem=recv, device_id=device, device_id_type=MESH
        )

    def hand(j, other, source):
        return remote(
            give_ref.at[j, piece_of(other)], arrived_ref.at[j, piece_of(source)],
            give_send.at[j, other], give_recv.at[j, source], place(other),
        )

    for j in range(2):

        def give(d, carry):
            hand(j, (me + d) % devices, me).start()
            return carry

        lax.fori_loop(1, devices, give, 0)

    total = 9 * slots
    flat = (1, total)
    at = iota(flat, 1).astype(jnp.float32)
    block = jnp.floor((at + 0.5) / slots)
    within = at - block * slots
    source = jnp.floor((within + 0.5) / slots_each)
    order = within - source * slots_each
    up = jnp.floor((block + 0.5) / 3.0)
    along = block - 3.0 * up
    lat_shift = jnp.where(up == 0.0, 0.0, jnp.where(up == 1.0, 1.0, -1.0)) * near.astype(jnp.float32)
    lon_shift = jnp.where(along == 0.0, 0.0, jnp.where(along == 1.0, -1.0, 1.0))
    owner_row = jnp.clip(row.astype(jnp.float32) + lat_shift, 0.0, lat - 1.0)
    owner_col = column.astype(jnp.float32) + lon_shift
    owner_col = jnp.where(owner_col < 0.0, owner_col + lon, jnp.where(owner_col >= lon, owner_col - lon, owner_col))
    wanted = ((owner_row * lon + owner_col) * slots_each + order).astype(jnp.int32)
    listed = table_ref[...].reshape(devices, table_ref.shape[2])
    chosen = jnp.where(iota((listed.shape[1], total), 0) == wanted, 1.0, 0.0).astype(jnp.bfloat16)
    mine = iota((devices, total), 0) == source.astype(jnp.int32)

    def position(values):
        found = matmul(values.astype(jnp.bfloat16), chosen)
        return jnp.sum(jnp.where(mine, found, 0.0), axis=0, keepdims=True)

    slot_row = position(listed >> log_lon) + lat_shift * lat_rows
    slot_col = position(listed & (lon_cols - 1)) + lon_shift * lon_cols
    down = iota((lon_cols, total), 0).astype(jnp.float32)
    col_weight = tap_value(slot_col - down, lon_cols // 2)
    for i in range(0, lat_rows, 2):
        for k in range(2):
            value = col_weight * tap_value(slot_row - (i + k), LHALF)
            high, low = halves(value)
            weight_ref[i // 2, k * lon_cols:(k + 1) * lon_cols, :] = high
            weight_ref[i // 2, (k + 2) * lon_cols:(k + 3) * lon_cols, :] = low

    spread = (slots, devices * PIECE)
    for at, (piece, kind) in enumerate(((0, 0), (0, 1), (0, 2), (1, 2))):
        held = piece_slot(iota(spread, 1), slots_each, piece, kind)
        wanted = jnp.where(held < 0, -1, (held >> 3) * slots_each + (held & 7))
        compact_ref[at] = jnp.where(wanted == iota(spread, 0), 1.0, 0.0).astype(jnp.bfloat16)

    def receive(j):
        def wait(d, carry):
            other = (me + d) % devices
            hand(j, other, other).wait_send()
            hand(j, other, other).wait_recv()
            return carry

        lax.fori_loop(1, devices, wait, 0)
        for kind in range(2):
            tile = (2 * j + kind) * 128
            grads_ref[0, 0, :, tile:tile + 128] = matmul(compact_ref[kind], arrived_ref[j]).astype(jnp.bfloat16)

    def receive_rest():
        rest = matmul(compact_ref[2], arrived_ref[0]) + matmul(compact_ref[3], arrived_ref[1])
        grads_ref[0, 0, :, part[2]] = rest.astype(jnp.bfloat16)

    def swap(j, b):
        return remote(
            grads_ref.at[0, b, :, part[j]], grads_ref.at[1, b, :, part[j]],
            swap_send.at[j, b], swap_recv.at[j, b], (partner, column),
        )

    def forward(j, b):
        return remote(
            grads_ref.at[1, b, :, part[j]], grads_ref.at[2, b, :, part[j]],
            far_send.at[j, b], far_recv.at[j, b], (row + step, column),
        )

    def to_right(j, a):
        return remote(
            grads_ref.at[a, 0, :, part[j]], grads_ref.at[a, 1, :, part[j]],
            lon_send.at[0, j, a], lon_recv.at[0, j, a], (row, (column + 1) % lon),
        )

    def to_left(j, a):
        return remote(
            grads_ref.at[a, 0, :, part[j]], grads_ref.at[a, 2, :, part[j]],
            lon_send.at[1, j, a], lon_recv.at[1, j, a], (row, (column + lon - 1) % lon),
        )

    def send_lon(j, a):
        to_right(j, a).start()
        to_left(j, a).start()

    def await_lon(j, a):
        to_right(j, a).wait_recv()
        to_left(j, a).wait_recv()

    def pass_on(j, b):
        swap(j, b).wait_recv()

        @pl.when(onward)
        def _():
            forward(j, b).start()

    def await_far(j, b):
        @pl.when(comes)
        def _():
            forward(j, b).wait_recv()

    def compute(j):
        count = cuts[j + 1] - cuts[j]
        kept = min(count, rows // lat_rows - cuts[j])
        grads = grads_ref[:, :, :, part[j]].reshape(total, count)

        def two(i, carry):
            result = matmul(weight_ref[i], grads)
            result = (result[: 2 * lon_cols] + result[2 * lon_cols:]) * std_ref[:, part[j]]
            for k in range(2):
                piece = result[k * lon_cols:(k + 1) * lon_cols].T
                out_ref[pl.ds(cuts[j] * lat_rows + 2 * i + k, kept, stride=lat_rows), :] = piece[:kept]
            return carry

        lax.fori_loop(0, lat_rows // 2, two, 0)

    lon_first = (0, 2)
    receive(0)
    send_lon(0, 0)
    swap(0, 0).start()
    receive(1)
    swap(1, 0).start()
    receive_rest()
    send_lon(2, 0)
    swap(2, 0).start()
    pass_on(0, 0)
    await_lon(0, 0)
    swap(0, 1).start()
    swap(0, 2).start()
    pass_on(1, 0)
    send_lon(1, 0)
    send_lon(1, 1)
    pass_on(2, 0)
    await_lon(2, 0)
    swap(2, 1).start()
    swap(2, 2).start()
    await_far(1, 0)
    send_lon(1, 2)
    for j in lon_first:
        pass_on(j, 1)
        pass_on(j, 2)
    for j in chunks:
        if j in lon_first:
            for b in range(3):
                await_far(j, b)
        else:
            for a in range(3):
                await_lon(j, a)
        compute(j)
    for j in chunks:
        for b in range(3) if j in lon_first else (0,):
            swap(j, b).wait_send()

            @pl.when(onward)
            def _():
                forward(j, b).wait_send()

        for a in (0,) if j in lon_first else range(3):
            to_right(j, a).wait_send()
            to_left(j, a).wait_send()


def adjoint_step(outgoing, table, std_dev, slots_each, lat_rows, lon_cols):
    lat, lon = lax.axis_size("lat"), lax.axis_size("lon")
    devices = lat * lon
    slots, width = devices * slots_each, std_dev.shape[0]
    lanes = lane_tiles(width) * 128
    cuts = [0, 256, 512, lanes]
    pieces = len(cuts) - 1
    std_dev = jnp.pad(std_dev, (0, lanes - width))[None, :]
    vmem = pl.BlockSpec(memory_space=pltpu.VMEM)
    dma = pltpu.SemaphoreType.DMA
    bf16, f32 = jnp.bfloat16, jnp.float32
    return pl.pallas_call(
        functools.partial(adjoint_kernel, lat, lon, lat_rows, slots_each, cuts),
        in_specs=[vmem] * 3,
        out_specs=vmem,
        out_shape=jax.ShapeDtypeStruct((width * lat_rows, lon_cols), f32),
        scratch_shapes=[
            pltpu.VMEM((2, devices * PIECE, 128), bf16),
            pltpu.VMEM((4, slots, devices * PIECE), bf16),
            pltpu.VMEM((3, 3, slots, lanes), bf16),
            pltpu.VMEM((lat_rows // 2, 4 * lon_cols, 9 * slots), bf16),
            *[dma((2, devices))] * 2,
            *[dma((pieces, 3))] * 4,
            *[dma((2, pieces, 3))] * 2,
        ],
        compiler_params=pltpu.CompilerParams(collective_id=1, has_side_effects=True),
        name="adjoint",
    )(outgoing, table, std_dev)


def local(control, std_dev, col_dev, col_cell, jacobian, innovation, inv_error):
    width, lat_rows, lon_cols = control.shape
    devices = lax.axis_size("lat") * lax.axis_size("lon")
    slots_each = max(2, 2 * col_cell.shape[0] // devices)
    increment, table, got = dense_step(control, col_dev, col_cell, std_dev, slots_each)
    departures, outgoing, increment = sounding_step(jacobian, got, col_dev, innovation, inv_error, increment)
    adjoint = adjoint_step(outgoing, table, std_dev, slots_each, lat_rows, lon_cols)
    return departures, increment.reshape(control.shape), adjoint.reshape(control.shape)


def solution(mesh):
    placed = (
        P(None, "lat", "lon"),
        P(),
        P(("lat", "lon"), None),
        P(("lat", "lon")),
        P(("lat", "lon"), None, None),
        P(("lat", "lon"), None),
        P(),
    )
    return jax.shard_map(
        local,
        mesh=mesh,
        in_specs=placed,
        out_specs=(P(("lat", "lon"), None), P(None, "lat", "lon"), P(None, "lat", "lon")),
        check_vma=False,
    )
```

```python
import functools
import math

import jax
import jax.numpy as jnp
from jax import lax
from jax.experimental import pallas as pl
from jax.experimental.pallas import tpu as pltpu
from jax.sharding import PartitionSpec as P

LHALF = 8
MESH = pl.DeviceIdType.MESH
VMEM = 48 << 20
DENSE_VMEM = 64300000


def tap_weights(offset, half_width):
    spread = 2.0 * half_width / 3.0
    taps = jnp.arange(-half_width, half_width + 1, dtype=jnp.int32).astype(jnp.float32)
    norm_total = jnp.sqrt(jnp.sum(jnp.exp(-taps * taps / (spread * spread))))
    weights = jnp.exp(-offset * offset / (2.0 * spread * spread)) / norm_total
    return jnp.where(jnp.abs(offset) <= half_width, weights, jnp.zeros_like(weights))


def halves(weights):
    high = weights.astype(jnp.bfloat16)
    return high, (weights - high.astype(jnp.float32)).astype(jnp.bfloat16)


def tap_value(offset, half_width):
    spread = 2.0 * half_width / 3.0
    norm_total = math.sqrt(sum(math.exp(-e * e / (spread * spread)) for e in range(-half_width, half_width + 1)))
    weights = jnp.exp(-offset * offset / (2.0 * spread * spread)) / norm_total
    return jnp.where(jnp.abs(offset) <= half_width, weights, 0.0)


GROUP = 256
CHUNK = 2 * GROUP


def matmul(left, right):
    return jnp.dot(left, right, preferred_element_type=jnp.float32)


def across(left, right):
    return lax.dot_general(left, right, (((1,), (1,)), ((), ())), preferred_element_type=jnp.float32)


def slots_of(dev_ref, cell_ref, slots_each, count):
    sound_count = dev_ref.shape[1]
    square = (sound_count, sound_count)
    iota = lambda shape, axis: lax.broadcasted_iota(jnp.int32, shape, axis)
    before = iota(square, 0) - iota(square, 1)
    across_lanes = jnp.broadcast_to(dev_ref[...].astype(jnp.float32), square)
    upright = lambda spread: jnp.sum(jnp.where(before == 0, spread, 0.0), axis=1, keepdims=True)
    down = upright(across_lanes)
    alike = across_lanes == down
    order = jnp.sum(jnp.where(jnp.logical_and(alike, before > 0), 1.0, 0.0), axis=1, keepdims=True)
    slot = down * slots_each + order
    onehot = slot.astype(jnp.int32) == iota((sound_count, count), 1)
    cell = upright(jnp.broadcast_to(cell_ref[...].astype(jnp.float32), square))
    order = jnp.sum(jnp.where(jnp.logical_and(alike, before < 0), 1.0, 0.0), axis=0, keepdims=True)
    return onehot, cell, (dev_ref[...].astype(jnp.float32) * slots_each + order).astype(jnp.int32)


def dense_kernel(
    lat, lon, lat_rows, slots_each,
    ctrl_hbm, dev_hbm, ask_hbm, std_hbm,
    inc_ref, table_ref, got_ref,
    ctrl_ref, dev_ref, ask_ref, std_ref, wanted_ref, own_ref, swap_ref, far_ref, g_ref, to_right_ref, to_left_ref, from_left_ref, from_right_ref,
    band_ref, mid_ref, edge_ref, std_row_ref, cell_ref, row_ref, pick_ref,
    swap_send, swap_recv, far_send, far_recv, lon_send, lon_recv,
    want_send, want_recv, col_send, col_recv, load_sem, small_sem,
):
    rows, lon_cols = ctrl_ref.shape
    width = rows // lat_rows
    full, rest = rows // CHUNK, rows % CHUNK
    early = full // 4 * 2
    log_lat, log_lon = lat_rows.bit_length() - 1, lon_cols.bit_length() - 1
    lon_half = lon_cols // 2
    row, column = lax.axis_index("lat"), lax.axis_index("lon")
    devices, me = lat * lon, row * lon + column
    odd = row % 2
    partner, step = row + 1 - 2 * odd, 2 - 4 * odd
    onward = jnp.logical_and(row + step >= 0, row + step < lat)
    comes = jnp.logical_and(row - step >= 0, row - step < lat)
    place = lambda other: (other // lon, other % lon)
    iota = lambda shape, axis: lax.broadcasted_iota(jnp.int32, shape, axis)

    barrier = pltpu.get_barrier_semaphore()

    def greet(d, carry):
        pl.semaphore_signal(barrier, inc=1, device_id=place((me + d) % devices), device_id_type=MESH)
        return carry

    lax.fori_loop(1, devices, greet, 0)

    def chunk_of(k):
        return pl.ds(pl.multiple_of(k * CHUNK, CHUNK), CHUNK)

    def half_of(k):
        return pl.ds(pl.multiple_of(k * GROUP, GROUP), GROUP)

    last, last_half = pl.ds(full * CHUNK, rest), pl.ds(full * GROUP, rest // 2)

    def remote(source, target, send, recv, device):
        return pltpu.make_async_remote_copy(
            src_ref=source, dst_ref=target, send_sem=send, recv_sem=recv, device_id=device, device_id_type=MESH
        )

    def request(dst, send, recv, other):
        return remote(wanted_ref.at[0], table_ref.at[dst], want_send.at[send], want_recv.at[recv], place(other))

    def swap(k, part):
        return remote(own_ref.at[part], swap_ref.at[part], swap_send.at[k], swap_recv.at[k], (partner, column))

    def forward(k, part):
        return remote(swap_ref.at[part], far_ref.at[part], far_send.at[k], far_recv.at[k], (row + step, column))

    def to_right(k, part):
        return remote(
            to_right_ref.at[part], from_left_ref.at[part], lon_send.at[0, k], lon_recv.at[0, k],
            (row, (column + 1) % lon),
        )

    def to_left(k, part):
        return remote(
            to_left_ref.at[part], from_right_ref.at[part], lon_send.at[1, k], lon_recv.at[1, k],
            (row, (column + lon - 1) % lon),
        )

    def back(d, group):
        part = pl.ds(pl.multiple_of(group * lon_cols, lon_cols), lon_cols)
        return remote(
            pick_ref.at[d, :, part], got_ref.at[me, :, part], col_send.at[d], col_recv.at[me], place(d)
        )

    def round_own(part):
        own_ref[part, :] = ctrl_ref[part, :].astype(jnp.bfloat16)

    def load(k, part):
        return pltpu.make_async_copy(ctrl_hbm.at[part], ctrl_ref.at[part], load_sem.at[k])

    def begin(k, carry):
        load(k, chunk_of(k)).start()
        return carry

    small = [
        pltpu.make_async_copy(source, target, small_sem.at[at])
        for at, (source, target) in enumerate(((dev_hbm, dev_ref), (ask_hbm, ask_ref), (std_hbm, std_ref)))
    ]
    for copy in small:
        copy.start()
    lax.fori_loop(0, full, begin, 0)
    load(full, last).start()
    for copy in small:
        copy.wait()
    onehot, cell_at, _ = slots_of(dev_ref, ask_ref, slots_each, wanted_ref.shape[2])
    wanted_ref[0] = jnp.sum(jnp.where(onehot, cell_at, 0.0), axis=0, keepdims=True).astype(jnp.int32)

    @pl.when(jnp.logical_not(comes))
    def _():
        far_ref[...] = jnp.zeros_like(far_ref)

    load(0, chunk_of(0)).wait()
    round_own(chunk_of(0))
    pl.semaphore_wait(barrier, devices - 1)

    def ask(d, carry):
        request(me, (me + d) % devices, me, (me + d) % devices).start()
        return carry

    lax.fori_loop(1, devices, ask, 0)

    def send_own(k, carry):
        load(k + 1, chunk_of(k + 1)).wait()

        @pl.when(k + 1 < early)
        def _():
            round_own(chunk_of(k + 1))

        swap(k, chunk_of(k)).start()
        return carry

    lax.fori_loop(0, early, send_own, 0)
    lane = iota((1, lon_cols), 1)

    def pack(first, second, part):
        right = jnp.where(lane < lon_half, pltpu.roll(first, lon_half, 1), second)
        left = jnp.where(lane < lon_half, first, pltpu.roll(second, lon_half, 1))
        to_right_ref[part, :] = right.astype(jnp.bfloat16)
        to_left_ref[part, :] = left.astype(jnp.bfloat16)

    def send_lon(k, part):
        to_right(k, part).start()
        to_left(k, part).start()

    def pack_own(k, carry):
        base = pl.multiple_of(k * CHUNK, CHUNK)
        pack(ctrl_ref[pl.ds(base, GROUP), :], ctrl_ref[pl.ds(base + GROUP, GROUP), :], half_of(k))

        @pl.when(k + 1 < full)
        def _():
            load(k + 1, chunk_of(k + 1)).wait()

        send_lon(k, half_of(k))
        return carry

    lax.fori_loop(early, full, pack_own, 0)
    load(full, last).wait()
    middle = full * CHUNK + rest // 2
    pack(ctrl_ref[full * CHUNK:middle, :], ctrl_ref[middle:, :], last_half)
    table_ref[me] = wanted_ref[0]
    send_lon(full, last_half)

    square = (GROUP, GROUP)
    same = (iota(square, 0) >> log_lat) == (iota(square, 1) >> log_lat)
    apart = (iota(square, 1) & (lat_rows - 1)) - (iota(square, 0) & (lat_rows - 1))

    def lat_band(shift):
        return halves(jnp.where(same, tap_value((apart + shift).astype(jnp.float32), LHALF), 0.0))

    high, low = lat_band(0)
    swap_high, swap_low = lat_band(lat_rows - 2 * lat_rows * odd)
    far_high, far_low = lat_band(2 * lat_rows * odd - lat_rows)
    for at, block in enumerate((high, high, low, swap_high, swap_low, far_high, far_low)):
        band_ref[:, at * GROUP:(at + 1) * GROUP] = block
    along = iota((lon_cols, lon_cols), 0) - iota((lon_cols, lon_cols), 1)
    high, low = halves(tap_value(along.astype(jnp.float32), lon_half))
    mid_ref[:, :lon_cols] = high
    mid_ref[:, lon_cols:] = low
    wide = (2 * lon_cols, 2 * lon_cols)
    source, target = iota(wide, 0), iota(wide, 1)
    within, which = source & (lon_half - 1), (source >> (log_lon - 1)) & 1
    column_at = jnp.where(source < lon_cols, within - lon_half, within + lon_cols)
    apart = column_at - (target & (lon_cols - 1))
    value = jnp.where(which == (target >> log_lon), tap_value(apart.astype(jnp.float32), lon_half), 0.0)
    high, low = halves(value)
    edge_ref[0] = high
    edge_ref[1] = low

    def spread(c, carry):
        std_row_ref[pl.ds(pl.multiple_of(c * lat_rows, lat_rows), lat_rows), :] = jnp.full(
            (lat_rows, lon_cols), std_ref[c], jnp.float32
        )
        return carry

    lax.fori_loop(0, width, spread, 0)

    def hear(d, carry):
        other = (me + d) % devices
        asked = request(other, other, other, other)
        asked.wait_send()
        asked.wait_recv()
        return carry

    lax.fori_loop(1, devices, hear, 0)
    listed = jnp.broadcast_to(table_ref[...].astype(jnp.float32), (devices, 8, table_ref.shape[2]))
    wants = iota(listed.shape, 2) == iota(listed.shape, 1) + me * slots_each
    cell = jnp.sum(jnp.where(wants, listed, 0.0), axis=2, keepdims=True).astype(jnp.int32)
    cell = jnp.broadcast_to(cell, (devices, 8, lon_cols)).reshape(devices * 8, lon_cols)
    row_ref[...] = cell >> log_lon
    cell_ref[...] = jnp.where((cell & (lon_cols - 1)) == iota(cell.shape, 1), 1.0, 0.0).astype(jnp.bfloat16)

    def lat_product(ref, first, second):
        def pair(ref):
            return jnp.concatenate([ref[first, :], ref[second, :]], axis=1)

        field = pair(ref)
        field_high, field_low = halves(field)
        swapped, far = pair(swap_ref), pair(far_ref)
        stacked = jnp.concatenate([field_high, field_low, field_high, swapped, swapped, far, far], axis=0)
        return matmul(band_ref[...], stacked)

    def lat_then_send(k):
        base = pl.multiple_of(k * CHUNK, CHUNK)
        first, second = pl.ds(base, GROUP), pl.ds(base + GROUP, GROUP)
        result = lat_product(ctrl_ref, first, second)
        top, bottom = result[:, :lon_cols], result[:, lon_cols:]
        g_ref[first, :] = top
        g_ref[second, :] = bottom
        pack(top, bottom, half_of(k))

    def lat_last(k):
        base = pl.multiple_of(k * CHUNK, CHUNK)
        first, second = pl.ds(base, GROUP), pl.ds(base + GROUP, GROUP)
        result = lat_product(g_ref, first, second)
        inc_ref[first, :] = result[:, :lon_cols] * std_row_ref[first, :]
        inc_ref[second, :] = result[:, lon_cols:] * std_row_ref[second, :]

    def lat_rest():
        result = lat_product(g_ref, pl.ds(rows - CHUNK, GROUP), pl.ds(rows - GROUP, GROUP))
        kept = jnp.concatenate([result[:, :lon_cols], result[:, lon_cols:]], axis=0)[CHUNK - rest:]
        inc_ref[last, :] = kept * std_row_ref[last, :]

    def lon_product(ref, start, count, part):
        half = count // 2
        both = jnp.concatenate([from_left_ref[part, :], from_right_ref[part, :]], axis=1)
        sides = matmul(both, edge_ref[0]) + matmul(both, edge_ref[1])
        high, low = halves(ref[pl.ds(start, count), :])
        own = matmul(high, mid_ref[...])
        own = own[:, :lon_cols] + own[:, lon_cols:] + matmul(low, mid_ref[:, :lon_cols])
        return own[:half] + sides[:, :lon_cols], own[half:] + sides[:, lon_cols:]

    def lon_last(k):
        base = pl.multiple_of(k * CHUNK, CHUNK)
        first, second = pl.ds(base, GROUP), pl.ds(base + GROUP, GROUP)
        top, bottom = lon_product(g_ref, base, CHUNK, half_of(k))
        inc_ref[first, :] = top * std_row_ref[first, :]
        inc_ref[second, :] = bottom * std_row_ref[second, :]

    def lon_first(start, count, part):
        first, second = pl.ds(start, count // 2), pl.ds(start + count // 2, count // 2)
        top, bottom = lon_product(ctrl_ref, start, count, part)
        g_ref[first, :] = top
        g_ref[second, :] = bottom
        own_ref[first, :] = top.astype(jnp.bfloat16)
        own_ref[second, :] = bottom.astype(jnp.bfloat16)

    def pick(start, count, group):
        values = inc_ref[pl.ds(start, count), :].astype(jnp.bfloat16)
        found = across(cell_ref[...], values)
        mine = (iota(row_ref.shape, 1) & (lat_rows - 1)) == row_ref[...]
        parts = []
        for at in range(0, count, lon_cols):
            piece = found[:, at:at + lon_cols]
            parts.append(jnp.where(mine[:, : piece.shape[1]], piece, 0.0).astype(jnp.bfloat16))
        masked = jnp.concatenate(parts, axis=1)
        gather = (iota((count, lon_cols), 0) >> log_lat) == iota((count, lon_cols), 1)
        result = matmul(masked, jnp.where(gather, 1.0, 0.0).astype(jnp.bfloat16))
        result = result.reshape(devices, 8, lon_cols)[:, :slots_each, :]
        pick_ref[:, :, pl.ds(pl.multiple_of(group * lon_cols, lon_cols), lon_cols)] = result.astype(jnp.bfloat16)

    def send_back(group):
        def give(d, carry):
            back((me + d) % devices, group).start()
            return carry

        lax.fori_loop(1, devices, give, 0)

    def stage(k, carry):
        def arrive(k, part):
            swap(k, part).wait_recv()

            @pl.when(onward)
            def _():
                forward(k, part).start()

        def await_far(k, part):
            @pl.when(comes)
            def _():
                forward(k, part).wait_recv()

        @pl.when(k < full)
        def _():
            arrive(k, chunk_of(k))

        @pl.when(k == full)
        def _():
            arrive(full, last)

        def await_lon(k, part):
            to_right(k, part).wait_recv()
            to_left(k, part).wait_recv()

        ahead, behind, done = k + early, k - 2, k - 4

        @pl.when(ahead < full)
        def _():
            await_lon(ahead, half_of(ahead))
            lon_first(pl.multiple_of(ahead * CHUNK, CHUNK), CHUNK, half_of(ahead))
            swap(ahead, chunk_of(ahead)).start()

        @pl.when(ahead == full)
        def _():
            await_lon(full, last_half)
            lon_first(full * CHUNK, rest, last_half)
            swap(full, last).start()

        @pl.when(jnp.logical_and(behind >= 0, behind < early))
        def _():
            await_far(behind, chunk_of(behind))
            lat_then_send(behind)

        @pl.when(jnp.logical_and(done >= 0, done < early))
        def _():
            await_lon(done, half_of(done))
            lon_last(done)

        @pl.when(jnp.logical_and(behind >= 0, behind < early))
        def _():
            send_lon(behind, half_of(behind))

        @pl.when(jnp.logical_and(behind >= early, behind < full))
        def _():
            await_far(behind, chunk_of(behind))
            lat_last(behind)

        def give(group):
            pick(pl.multiple_of(group * 2 * CHUNK, 2 * CHUNK), 2 * CHUNK, group)
            send_back(group)

        @pl.when(jnp.logical_and(jnp.logical_and(done >= 0, done < early), done % 2 == 1))
        def _():
            give(done // 2)

        @pl.when(jnp.logical_and(jnp.logical_and(behind >= early, behind < full), behind % 2 == 1))
        def _():
            give(behind // 2)

        @pl.when(behind == full)
        def _():
            await_far(full, last)
            lat_rest()
            pick(full * CHUNK, rest, full // 2)
            send_back(full // 2)

        return carry

    lax.fori_loop(0, full + 3, stage, 0)
    got_ref[me] = pick_ref[me]

    def finish(k, part, half):
        swap(k, part).wait_send()

        @pl.when(onward)
        def _():
            forward(k, part).wait_send()

        to_right(k, half).wait_send()
        to_left(k, half).wait_send()

    def finish_full(k, carry):
        finish(k, chunk_of(k), half_of(k))
        return carry

    lax.fori_loop(0, full, finish_full, 0)
    finish(full, last, last_half)

    def collect(d, carry):
        other = (me + d) % devices
        whole = remote(
            pick_ref.at[other], got_ref.at[other], col_send.at[other], col_recv.at[other], place(other)
        )
        whole.wait_send()
        whole.wait_recv()
        return carry

    lax.fori_loop(1, devices, collect, 0)


def dense_step(control, col_dev, col_cell, std_dev, slots_each):
    lat, lon = lax.axis_size("lat"), lax.axis_size("lon")
    width, lat_rows, lon_cols = control.shape
    devices, rows = lat * lon, width * lat_rows
    pieces = rows // CHUNK + 1
    lanes = lane_tiles(width) * lon_cols
    listed = (1, lane_tiles(devices * slots_each) * 128)
    vmem, hbm = pl.BlockSpec(memory_space=pltpu.VMEM), pl.BlockSpec(memory_space=pltpu.HBM)
    dma = pltpu.SemaphoreType.DMA
    bf16, f32 = jnp.bfloat16, jnp.float32
    return pl.pallas_call(
        functools.partial(dense_kernel, lat, lon, lat_rows, slots_each),
        in_specs=[hbm] * 4,
        out_specs=[vmem, vmem, vmem],
        out_shape=[
            jax.ShapeDtypeStruct((rows, lon_cols), f32),
            jax.ShapeDtypeStruct((devices, *listed), jnp.int32),
            jax.ShapeDtypeStruct((devices, slots_each, lanes), bf16),
        ],
        scratch_shapes=[
            pltpu.VMEM((rows, lon_cols), f32),
            pltpu.VMEM((1, col_cell.shape[0]), jnp.int32),
            pltpu.VMEM((1, col_cell.shape[0]), jnp.int32),
            pltpu.SMEM(std_dev.shape, f32),
            pltpu.VMEM((1, *listed), jnp.int32),
            pltpu.VMEM((rows, lon_cols), bf16),
            pltpu.VMEM((rows, lon_cols), bf16),
            pltpu.VMEM((rows, lon_cols), bf16),
            pltpu.VMEM((rows, lon_cols), f32),
            *[pltpu.VMEM((rows // 2, lon_cols), bf16)] * 4,
            pltpu.VMEM((GROUP, 7 * GROUP), bf16),
            pltpu.VMEM((lon_cols, 2 * lon_cols), bf16),
            pltpu.VMEM((2, 2 * lon_cols, 2 * lon_cols), bf16),
            pltpu.VMEM((rows, lon_cols), f32),
            pltpu.VMEM((devices * 8, lon_cols), bf16),
            pltpu.VMEM((devices * 8, lon_cols), jnp.int32),
            pltpu.VMEM((devices, slots_each, lanes), bf16),
            *[dma((pieces,))] * 4,
            *[dma((2, pieces))] * 2,
            *[dma((devices,))] * 4,
            dma((pieces,)),
            dma((3,)),
        ],
        compiler_params=pltpu.CompilerParams(collective_id=0, has_side_effects=True, vmem_limit_bytes=DENSE_VMEM),
        name="dense",
    )(control.reshape(rows, lon_cols), col_dev.reshape(1, -1), col_cell[None, :], std_dev)


def lane_tiles(count):
    return -(-count // 128)


PIECE = 16


def piece_slot(index, slots_each, piece, kind):
    device, row = index >> 4, index & (PIECE - 1)
    spare = PIECE - 2 * slots_each
    if kind < 2:
        number = row - kind * slots_each
        valid = jnp.logical_and(number >= 0, number < slots_each)
    else:
        number = row - 2 * slots_each + piece * spare
        valid = jnp.logical_and(row >= 2 * slots_each, number < slots_each)
    return jnp.where(valid, device * 8 + number, -1)


def sounding_part(
    slots_each, step,
    jac_hbm, got_ref, dev_ref, innov_ref, inv_ref, dep_ref, out_ref,
    jac_ref, apart_ref, col_ref, tail_ref, weight_ref, grad_ref, jac_sem,
):
    channels, count, width = jac_ref.shape
    steps = channels // step
    devices, lanes = got_ref.shape[0], got_ref.shape[2]
    most = width // 128 * 128
    iota = lambda shape, axis: lax.broadcasted_iota(jnp.int32, shape, axis)

    def load(b):
        part = pl.ds(b * step, step)
        return pltpu.make_async_copy(jac_hbm.at[part], jac_ref.at[part], jac_sem.at[b])

    def begin(b, carry):
        load(b).start()
        return carry

    lax.fori_loop(0, steps, begin, 0)
    apart_ref[...] = jnp.zeros_like(apart_ref)
    apart_ref[:, :slots_each, :] = got_ref[...].astype(jnp.float32)
    onehot, _, slot = slots_of(dev_ref, dev_ref, 8, devices * 8)
    onehot = jnp.where(onehot, 1.0, 0.0).astype(jnp.bfloat16)
    columns = matmul(onehot, apart_ref[...].reshape(devices * 8, lanes).astype(jnp.bfloat16))
    col_ref[...] = columns.astype(jnp.bfloat16)
    tail_ref[...] = columns[:, most:]
    grad_ref[...] = jnp.zeros_like(grad_ref)
    square = (count, count)

    def product(b):
        block = jac_ref[pl.ds(b * step, step), :, :most]
        return across(block.reshape(step * count, most), col_ref[:, :most])

    def depart(b, found):
        mine = iota(square, 0) == iota(square, 1)
        for k in range(step):
            channel = b * step + k
            own = jnp.where(mine, found[k * count:(k + 1) * count] - innov_ref[pl.ds(channel, 1), :], 0.0)
            if width > most:
                tail = jac_ref[channel, :, most:].astype(jnp.float32) * tail_ref[:, : width - most]
                own = own + jnp.concatenate([tail, jnp.zeros((count, count - (width - most)), jnp.float32)], axis=1)
            departure = jnp.sum(own, axis=1, keepdims=True)
            dep_ref[pl.ds(channel, 1), :] = jnp.sum(jnp.where(mine, departure, 0.0), axis=0, keepdims=True)
            weight = (departure * inv_ref[channel]).astype(jnp.bfloat16).astype(jnp.float32)
            weight_ref[k] = jnp.broadcast_to(weight, (count, 128))

    def gradient(b):
        for group in range(0, count, 16):
            part = slice(group, group + 16)
            for lane in range(0, width, 128):
                end = min(lane + 128, width)
                total = grad_ref[part, lane:end]
                for k in range(step):
                    values = jac_ref[b * step + k, part, lane:end].astype(jnp.float32)
                    total = total + values * weight_ref[k, part, : end - lane]
                grad_ref[part, lane:end] = total

    load(0).wait()
    depart(0, product(0))

    def body(b, carry):
        load(b).wait()
        found = product(b)
        gradient(b - 1)
        depart(b, found)
        return carry

    lax.fori_loop(1, steps, body, 0)
    gradient(steps - 1)
    grads = grad_ref[...].astype(jnp.bfloat16)
    for piece in range(2):
        packed = jnp.zeros((devices * PIECE, 128), jnp.float32)
        for kind in range(3):
            held = piece_slot(iota((devices * PIECE, count), 0), slots_each, piece, kind)
            onehot = jnp.where(held == slot, 1.0, 0.0).astype(jnp.bfloat16)
            tile = (2 * piece + kind if kind < 2 else 4) * 128
            packed = packed + matmul(onehot, grads[:, tile:tile + 128])
        out_ref[piece] = packed.astype(out_ref.dtype)


def adjoint_kernel(
    lat, lon, lat_rows, slots_each, cuts, step,
    jac_hbm, got_ref, dev_ref, innov_ref, inv_ref, table_ref, std_ref,
    dep_ref, out_ref,
    jac_ref, apart_ref, col_ref, tail_ref, scale_ref, grad_ref, jac_sem,
    give_ref, arrived_ref, compact_ref, grads_ref, weight_ref, std_row_ref,
    give_send, give_recv, swap_send, swap_recv, far_send, far_recv, lon_send, lon_recv,
):
    devices = lat * lon
    slots = devices * slots_each
    rows, lon_cols = out_ref.shape
    log_lon = lon_cols.bit_length() - 1
    row, column = lax.axis_index("lat"), lax.axis_index("lon")
    me = row * lon + column
    odd = row % 2
    near = 1 - 2 * odd
    partner, stride = row + near, 2 * near
    onward = jnp.logical_and(row + stride >= 0, row + stride < lat)
    comes = jnp.logical_and(row - stride >= 0, row - stride < lat)
    place = lambda other: (other // lon, other % lon)
    iota = lambda shape, axis: lax.broadcasted_iota(jnp.int32, shape, axis)
    chunks = range(len(cuts) - 1)
    part = [pl.ds(cuts[j], cuts[j + 1] - cuts[j]) for j in chunks]

    @pl.when(jnp.logical_not(comes))
    def _():
        grads_ref[2] = jnp.zeros_like(grads_ref[2])

    barrier = pltpu.get_barrier_semaphore()

    def greet(d, carry):
        pl.semaphore_signal(barrier, inc=1, device_id=place((me + d) % devices), device_id_type=MESH)
        return carry

    lax.fori_loop(1, devices, greet, 0)
    sounding_part(
        slots_each, step, jac_hbm, got_ref, dev_ref, innov_ref, inv_ref, dep_ref, give_ref,
        jac_ref, apart_ref, col_ref, tail_ref, scale_ref, grad_ref, jac_sem,
    )
    std_row_ref[...] = jnp.zeros_like(std_row_ref)
    std_row_ref[:, : std_ref.shape[0]] = std_ref[...].reshape(1, -1)

    def piece_of(d):
        return pl.ds(pl.multiple_of(d * PIECE, PIECE), PIECE)

    arrived_ref[:, piece_of(me), :] = give_ref[:, piece_of(me), :]
    pl.semaphore_wait(barrier, devices - 1)

    def remote(source, target, send, recv, device):
        return pltpu.make_async_remote_copy(
            src_ref=source, dst_ref=target, send_sem=send, recv_sem=recv, device_id=device, device_id_type=MESH
        )

    def hand(j, other, source):
        return remote(
            give_ref.at[j, piece_of(other)], arrived_ref.at[j, piece_of(source)],
            give_send.at[j, other], give_recv.at[j, source], place(other),
        )

    for j in range(2):

        def give(d, carry):
            hand(j, (me + d) % devices, me).start()
            return carry

        lax.fori_loop(1, devices, give, 0)

    total = 9 * slots
    flat = (1, total)
    at = iota(flat, 1).astype(jnp.float32)
    block = jnp.floor((at + 0.5) / slots)
    within = at - block * slots
    source = jnp.floor((within + 0.5) / slots_each)
    order = within - source * slots_each
    up = jnp.floor((block + 0.5) / 3.0)
    along = block - 3.0 * up
    lat_shift = jnp.where(up == 0.0, 0.0, jnp.where(up == 1.0, 1.0, -1.0)) * near.astype(jnp.float32)
    lon_shift = jnp.where(along == 0.0, 0.0, jnp.where(along == 1.0, -1.0, 1.0))
    owner_row = jnp.clip(row.astype(jnp.float32) + lat_shift, 0.0, lat - 1.0)
    owner_col = column.astype(jnp.float32) + lon_shift
    owner_col = jnp.where(owner_col < 0.0, owner_col + lon, jnp.where(owner_col >= lon, owner_col - lon, owner_col))
    wanted = ((owner_row * lon + owner_col) * slots_each + order).astype(jnp.int32)
    listed = table_ref[...].reshape(devices, table_ref.shape[2])
    chosen = jnp.where(iota((listed.shape[1], total), 0) == wanted, 1.0, 0.0).astype(jnp.bfloat16)
    mine = iota((devices, total), 0) == source.astype(jnp.int32)

    def position(values):
        found = matmul(values.astype(jnp.bfloat16), chosen)
        return jnp.sum(jnp.where(mine, found, 0.0), axis=0, keepdims=True)

    slot_row = position(listed >> log_lon) + lat_shift * lat_rows
    slot_col = position(listed & (lon_cols - 1)) + lon_shift * lon_cols
    down = iota((lon_cols, total), 0).astype(jnp.float32)
    col_weight = tap_value(slot_col - down, lon_cols // 2)
    for i in range(0, lat_rows, 2):
        for k in range(2):
            value = col_weight * tap_value(slot_row - (i + k), LHALF)
            high, low = halves(value)
            weight_ref[i // 2, k * lon_cols:(k + 1) * lon_cols, :] = high
            weight_ref[i // 2, (k + 2) * lon_cols:(k + 3) * lon_cols, :] = low

    spread = (slots, devices * PIECE)
    for at, (piece, kind) in enumerate(((0, 0), (0, 1), (0, 2), (1, 2))):
        held = piece_slot(iota(spread, 1), slots_each, piece, kind)
        wanted = jnp.where(held < 0, -1, (held >> 3) * slots_each + (held & 7))
        compact_ref[at] = jnp.where(wanted == iota(spread, 0), 1.0, 0.0).astype(jnp.bfloat16)

    def receive(j):
        def wait(d, carry):
            other = (me + d) % devices
            hand(j, other, other).wait_send()
            hand(j, other, other).wait_recv()
            return carry

        lax.fori_loop(1, devices, wait, 0)
        for kind in range(2):
            tile = (2 * j + kind) * 128
            grads_ref[0, 0, :, tile:tile + 128] = matmul(compact_ref[kind], arrived_ref[j]).astype(jnp.bfloat16)

    def receive_rest():
        rest = matmul(compact_ref[2], arrived_ref[0]) + matmul(compact_ref[3], arrived_ref[1])
        grads_ref[0, 0, :, part[2]] = rest.astype(jnp.bfloat16)

    def swap(j, b):
        return remote(
            grads_ref.at[0, b, :, part[j]], grads_ref.at[1, b, :, part[j]],
            swap_send.at[j, b], swap_recv.at[j, b], (partner, column),
        )

    def forward(j, b):
        return remote(
            grads_ref.at[1, b, :, part[j]], grads_ref.at[2, b, :, part[j]],
            far_send.at[j, b], far_recv.at[j, b], (row + stride, column),
        )

    def to_right(j, a):
        return remote(
            grads_ref.at[a, 0, :, part[j]], grads_ref.at[a, 1, :, part[j]],
            lon_send.at[0, j, a], lon_recv.at[0, j, a], (row, (column + 1) % lon),
        )

    def to_left(j, a):
        return remote(
            grads_ref.at[a, 0, :, part[j]], grads_ref.at[a, 2, :, part[j]],
            lon_send.at[1, j, a], lon_recv.at[1, j, a], (row, (column + lon - 1) % lon),
        )

    def send_lon(j, a):
        to_right(j, a).start()
        to_left(j, a).start()

    def await_lon(j, a):
        to_right(j, a).wait_recv()
        to_left(j, a).wait_recv()

    def pass_on(j, b):
        swap(j, b).wait_recv()

        @pl.when(onward)
        def _():
            forward(j, b).start()

    def await_far(j, b):
        @pl.when(comes)
        def _():
            forward(j, b).wait_recv()

    def compute(j):
        count = cuts[j + 1] - cuts[j]
        kept = min(count, rows // lat_rows - cuts[j])
        grads = grads_ref[:, :, :, part[j]].reshape(total, count)

        def two(i, carry):
            result = matmul(weight_ref[i], grads)
            result = (result[: 2 * lon_cols] + result[2 * lon_cols:]) * std_row_ref[:, part[j]]
            for k in range(2):
                piece = result[k * lon_cols:(k + 1) * lon_cols].T
                out_ref[pl.ds(cuts[j] * lat_rows + 2 * i + k, kept, stride=lat_rows), :] = piece[:kept]
            return carry

        lax.fori_loop(0, lat_rows // 2, two, 0)

    lon_first = (0, 2)
    receive(0)
    send_lon(0, 0)
    swap(0, 0).start()
    receive(1)
    swap(1, 0).start()
    receive_rest()
    send_lon(2, 0)
    swap(2, 0).start()
    pass_on(0, 0)
    await_lon(0, 0)
    swap(0, 1).start()
    swap(0, 2).start()
    pass_on(1, 0)
    send_lon(1, 0)
    send_lon(1, 1)
    pass_on(2, 0)
    await_lon(2, 0)
    swap(2, 1).start()
    swap(2, 2).start()
    await_far(1, 0)
    send_lon(1, 2)
    for j in lon_first:
        pass_on(j, 1)
        pass_on(j, 2)
    for j in chunks:
        if j in lon_first:
            for b in range(3):
                await_far(j, b)
        else:
            for a in range(3):
                await_lon(j, a)
        compute(j)
    for j in chunks:
        for b in range(3) if j in lon_first else (0,):
            swap(j, b).wait_send()

            @pl.when(onward)
            def _():
                forward(j, b).wait_send()

        for a in (0,) if j in lon_first else range(3):
            to_right(j, a).wait_send()
            to_left(j, a).wait_send()


def analysis_step(jacobian, got, table, col_dev, innovation, inv_error, std_dev, lat_rows, lon_cols):
    lat, lon = lax.axis_size("lat"), lax.axis_size("lon")
    count, channels, width = jacobian.shape
    devices, slots_each, lanes = got.shape
    slots, rows = devices * slots_each, width * lat_rows
    cuts = [0, 256, 512, lanes]
    pieces = len(cuts) - 1
    step = next(n for n in (10, 8, 6, 5, 4, 3, 2, 1) if channels % n == 0)
    vmem, hbm = pl.BlockSpec(memory_space=pltpu.VMEM), pl.BlockSpec(memory_space=pl.ANY)
    dma = pltpu.SemaphoreType.DMA
    bf16, f32 = jnp.bfloat16, jnp.float32
    departures, adjoint = pl.pallas_call(
        functools.partial(adjoint_kernel, lat, lon, lat_rows, slots_each, cuts, step),
        in_specs=[hbm, vmem, vmem, vmem, pl.BlockSpec(memory_space=pltpu.SMEM), vmem, vmem],
        out_specs=[vmem, vmem],
        out_shape=[
            jax.ShapeDtypeStruct((channels, count), f32),
            jax.ShapeDtypeStruct((rows, lon_cols), f32),
        ],
        scratch_shapes=[
            pltpu.VMEM((channels, count, width), bf16),
            pltpu.VMEM((devices, 8, lanes), f32),
            pltpu.VMEM((count, lanes), bf16),
            pltpu.VMEM((count, 128), f32),
            pltpu.VMEM((step, count, 128), f32),
            pltpu.VMEM((count, lanes), f32),
            dma((channels // step,)),
            pltpu.VMEM((2, devices * PIECE, 128), bf16),
            pltpu.VMEM((2, devices * PIECE, 128), bf16),
            pltpu.VMEM((4, slots, devices * PIECE), bf16),
            pltpu.VMEM((3, 3, slots, lanes), bf16),
            pltpu.VMEM((lat_rows // 2, 4 * lon_cols, 9 * slots), bf16),
            pltpu.VMEM((1, lanes), f32),
            *[dma((2, devices))] * 2,
            *[dma((pieces, 3))] * 4,
            *[dma((2, pieces, 3))] * 2,
        ],
        compiler_params=pltpu.CompilerParams(collective_id=1, has_side_effects=True, vmem_limit_bytes=VMEM),
        name="analysis",
    )(jnp.transpose(jacobian, (1, 0, 2)), got, col_dev.reshape(1, -1), innovation.T, inv_error, table, std_dev)
    return departures, adjoint


def local(control, std_dev, col_dev, col_cell, jacobian, innovation, inv_error):
    width, lat_rows, lon_cols = control.shape
    devices = lax.axis_size("lat") * lax.axis_size("lon")
    slots_each = max(2, 2 * col_cell.shape[0] // devices)
    increment, table, got = dense_step(control, col_dev, col_cell, std_dev, slots_each)
    departures, adjoint = analysis_step(
        jacobian, got, table, col_dev, innovation, inv_error, std_dev, lat_rows, lon_cols
    )
    return departures.T, increment.reshape(control.shape), adjoint.reshape(control.shape)


def solution(mesh):
    placed = (
        P(None, "lat", "lon"),
        P(),
        P(("lat", "lon"), None),
        P(("lat", "lon")),
        P(("lat", "lon"), None, None),
        P(("lat", "lon"), None),
        P(),
    )
    return jax.shard_map(
        local,
        mesh=mesh,
        in_specs=placed,
        out_specs=(P(("lat", "lon"), None), P(None, "lat", "lon"), P(None, "lat", "lon")),
        check_vma=False,
    )
```

```python
import functools
import math

import jax
import jax.numpy as jnp
from jax import lax
from jax.experimental import pallas as pl
from jax.experimental.pallas import tpu as pltpu
from jax.sharding import PartitionSpec as P

LHALF = 8
MESH = pl.DeviceIdType.MESH
VMEM = 48 << 20
DENSE_VMEM = 64300000


def tap_weights(offset, half_width):
    spread = 2.0 * half_width / 3.0
    taps = jnp.arange(-half_width, half_width + 1, dtype=jnp.int32).astype(jnp.float32)
    norm_total = jnp.sqrt(jnp.sum(jnp.exp(-taps * taps / (spread * spread))))
    weights = jnp.exp(-offset * offset / (2.0 * spread * spread)) / norm_total
    return jnp.where(jnp.abs(offset) <= half_width, weights, jnp.zeros_like(weights))


def halves(weights):
    high = weights.astype(jnp.bfloat16)
    return high, (weights - high.astype(jnp.float32)).astype(jnp.bfloat16)


def tap_value(offset, half_width):
    spread = 2.0 * half_width / 3.0
    norm_total = math.sqrt(sum(math.exp(-e * e / (spread * spread)) for e in range(-half_width, half_width + 1)))
    weights = jnp.exp(-offset * offset / (2.0 * spread * spread)) / norm_total
    return jnp.where(jnp.abs(offset) <= half_width, weights, 0.0)


GROUP = 256
CHUNK = 2 * GROUP


def matmul(left, right):
    return jnp.dot(left, right, preferred_element_type=jnp.float32)


def across(left, right):
    return lax.dot_general(left, right, (((1,), (1,)), ((), ())), preferred_element_type=jnp.float32)


def slots_of(dev_ref, cell_ref, slots_each, count):
    sound_count = dev_ref.shape[1]
    square = (sound_count, sound_count)
    iota = lambda shape, axis: lax.broadcasted_iota(jnp.int32, shape, axis)
    before = iota(square, 0) - iota(square, 1)
    across_lanes = jnp.broadcast_to(dev_ref[...].astype(jnp.float32), square)
    upright = lambda spread: jnp.sum(jnp.where(before == 0, spread, 0.0), axis=1, keepdims=True)
    down = upright(across_lanes)
    alike = across_lanes == down
    order = jnp.sum(jnp.where(jnp.logical_and(alike, before > 0), 1.0, 0.0), axis=1, keepdims=True)
    slot = down * slots_each + order
    onehot = slot.astype(jnp.int32) == iota((sound_count, count), 1)
    cell = upright(jnp.broadcast_to(cell_ref[...].astype(jnp.float32), square))
    order = jnp.sum(jnp.where(jnp.logical_and(alike, before < 0), 1.0, 0.0), axis=0, keepdims=True)
    return onehot, cell, (dev_ref[...].astype(jnp.float32) * slots_each + order).astype(jnp.int32)


def dense_kernel(
    lat, lon, lat_rows, slots_each,
    ctrl_hbm, dev_hbm, ask_hbm, std_hbm,
    inc_ref, table_ref, got_ref,
    ctrl_ref, dev_ref, ask_ref, std_ref, wanted_ref, own_ref, swap_ref, far_ref, g_ref, to_right_ref, to_left_ref, from_left_ref, from_right_ref,
    band_ref, mid_ref, edge_ref, std_row_ref, cell_ref, row_ref, pick_ref,
    swap_send, swap_recv, far_send, far_recv, lon_send, lon_recv,
    want_send, want_recv, col_send, col_recv, load_sem, small_sem, token_sem,
):
    rows, lon_cols = ctrl_ref.shape
    width = rows // lat_rows
    full, rest = rows // CHUNK, rows % CHUNK
    early = full // 4 * 2
    log_lat, log_lon = lat_rows.bit_length() - 1, lon_cols.bit_length() - 1
    lon_half = lon_cols // 2
    row, column = lax.axis_index("lat"), lax.axis_index("lon")
    devices, me = lat * lon, row * lon + column
    odd = row % 2
    partner, step = row + 1 - 2 * odd, 2 - 4 * odd
    onward = jnp.logical_and(row + step >= 0, row + step < lat)
    comes = jnp.logical_and(row - step >= 0, row - step < lat)
    place = lambda other: (other // lon, other % lon)
    iota = lambda shape, axis: lax.broadcasted_iota(jnp.int32, shape, axis)

    barrier = pltpu.get_barrier_semaphore()

    right, left = (row, (column + 1) % lon), (row, (column + lon - 1) % lon)

    def tell(semaphore, device):
        pl.semaphore_signal(semaphore, inc=1, device_id=device, device_id_type=MESH)

    for d in range(1, lat):
        tell(barrier, ((row + d) % lat, column))
    tell(barrier, right)
    tell(barrier, left)

    def chunk_of(k):
        return pl.ds(pl.multiple_of(k * CHUNK, CHUNK), CHUNK)

    def half_of(k):
        return pl.ds(pl.multiple_of(k * GROUP, GROUP), GROUP)

    last, last_half = pl.ds(full * CHUNK, rest), pl.ds(full * GROUP, rest // 2)

    def remote(source, target, send, recv, device):
        return pltpu.make_async_remote_copy(
            src_ref=source, dst_ref=target, send_sem=send, recv_sem=recv, device_id=device, device_id_type=MESH
        )

    def request(dst, send, recv, other):
        return remote(wanted_ref.at[0], table_ref.at[dst], want_send.at[send], want_recv.at[recv], place(other))

    def swap(k, part):
        return remote(own_ref.at[part], swap_ref.at[part], swap_send.at[k], swap_recv.at[k], (partner, column))

    def forward(k, part):
        return remote(swap_ref.at[part], far_ref.at[part], far_send.at[k], far_recv.at[k], (row + step, column))

    def to_right(k, part):
        return remote(
            to_right_ref.at[part], from_left_ref.at[part], lon_send.at[0, k], lon_recv.at[0, k],
            (row, (column + 1) % lon),
        )

    def to_left(k, part):
        return remote(
            to_left_ref.at[part], from_right_ref.at[part], lon_send.at[1, k], lon_recv.at[1, k],
            (row, (column + lon - 1) % lon),
        )

    def back(d, group):
        part = pl.ds(pl.multiple_of(group * lon_cols, lon_cols), lon_cols)
        return remote(
            pick_ref.at[d, :, part], got_ref.at[me, :, part], col_send.at[d], col_recv.at[me], place(d)
        )

    def round_own(part):
        own_ref[part, :] = ctrl_ref[part, :].astype(jnp.bfloat16)

    def load(k, part):
        return pltpu.make_async_copy(ctrl_hbm.at[part], ctrl_ref.at[part], load_sem.at[k])

    def begin(k, carry):
        load(k, chunk_of(k)).start()
        return carry

    small = [
        pltpu.make_async_copy(source, target, small_sem.at[at])
        for at, (source, target) in enumerate(((dev_hbm, dev_ref), (ask_hbm, ask_ref), (std_hbm, std_ref)))
    ]
    for copy in small:
        copy.start()
    lax.fori_loop(0, full, begin, 0)
    load(full, last).start()
    for copy in small:
        copy.wait()
    onehot, cell_at, _ = slots_of(dev_ref, ask_ref, slots_each, wanted_ref.shape[2])
    wanted_ref[0] = jnp.sum(jnp.where(onehot, cell_at, 0.0), axis=0, keepdims=True).astype(jnp.int32)

    @pl.when(jnp.logical_not(comes))
    def _():
        far_ref[...] = jnp.zeros_like(far_ref)

    load(0, chunk_of(0)).wait()
    round_own(chunk_of(0))
    pl.semaphore_wait(barrier, lat + 1)

    def pass_tokens():
        tell(token_sem.at[0], right)
        tell(token_sem.at[1], left)

    pass_tokens()

    def ask(d, carry):
        request(me, (me + d) % devices, me, (me + d) % devices).start()
        return carry


    def send_own(k, carry):
        load(k + 1, chunk_of(k + 1)).wait()

        @pl.when(k + 1 < early)
        def _():
            round_own(chunk_of(k + 1))

        swap(k, chunk_of(k)).start()
        return carry

    lax.fori_loop(0, early, send_own, 0)
    lane = iota((1, lon_cols), 1)

    def pack(first, second, part):
        right = jnp.where(lane < lon_half, pltpu.roll(first, lon_half, 1), second)
        left = jnp.where(lane < lon_half, first, pltpu.roll(second, lon_half, 1))
        to_right_ref[part, :] = right.astype(jnp.bfloat16)
        to_left_ref[part, :] = left.astype(jnp.bfloat16)

    def send_lon(k, part):
        to_right(k, part).start()
        to_left(k, part).start()

    def pack_own(k, carry):
        base = pl.multiple_of(k * CHUNK, CHUNK)
        pack(ctrl_ref[pl.ds(base, GROUP), :], ctrl_ref[pl.ds(base + GROUP, GROUP), :], half_of(k))

        @pl.when(k + 1 < full)
        def _():
            load(k + 1, chunk_of(k + 1)).wait()

        send_lon(k, half_of(k))
        return carry

    lax.fori_loop(early, full, pack_own, 0)
    load(full, last).wait()
    middle = full * CHUNK + rest // 2
    pack(ctrl_ref[full * CHUNK:middle, :], ctrl_ref[middle:, :], last_half)
    table_ref[me] = wanted_ref[0]
    send_lon(full, last_half)

    square = (GROUP, GROUP)
    same = (iota(square, 0) >> log_lat) == (iota(square, 1) >> log_lat)
    apart = (iota(square, 1) & (lat_rows - 1)) - (iota(square, 0) & (lat_rows - 1))

    def lat_band(shift):
        return halves(jnp.where(same, tap_value((apart + shift).astype(jnp.float32), LHALF), 0.0))

    high, low = lat_band(0)
    swap_high, swap_low = lat_band(lat_rows - 2 * lat_rows * odd)
    far_high, far_low = lat_band(2 * lat_rows * odd - lat_rows)
    for at, block in enumerate((high, high, low, swap_high, swap_low, far_high, far_low)):
        band_ref[:, at * GROUP:(at + 1) * GROUP] = block
    along = iota((lon_cols, lon_cols), 0) - iota((lon_cols, lon_cols), 1)
    high, low = halves(tap_value(along.astype(jnp.float32), lon_half))
    mid_ref[:, :lon_cols] = high
    mid_ref[:, lon_cols:] = low
    wide = (2 * lon_cols, 2 * lon_cols)
    source, target = iota(wide, 0), iota(wide, 1)
    within, which = source & (lon_half - 1), (source >> (log_lon - 1)) & 1
    column_at = jnp.where(source < lon_cols, within - lon_half, within + lon_cols)
    apart = column_at - (target & (lon_cols - 1))
    value = jnp.where(which == (target >> log_lon), tap_value(apart.astype(jnp.float32), lon_half), 0.0)
    high, low = halves(value)
    edge_ref[0] = high
    edge_ref[1] = low

    def spread(c, carry):
        std_row_ref[pl.ds(pl.multiple_of(c * lat_rows, lat_rows), lat_rows), :] = jnp.full(
            (lat_rows, lon_cols), std_ref[c], jnp.float32
        )
        return carry

    lax.fori_loop(0, width, spread, 0)

    def lat_product(ref, first, second):
        def pair(ref):
            return jnp.concatenate([ref[first, :], ref[second, :]], axis=1)

        field = pair(ref)
        field_high, field_low = halves(field)
        swapped, far = pair(swap_ref), pair(far_ref)
        stacked = jnp.concatenate([field_high, field_low, field_high, swapped, swapped, far, far], axis=0)
        return matmul(band_ref[...], stacked)

    def lat_then_send(k):
        base = pl.multiple_of(k * CHUNK, CHUNK)
        first, second = pl.ds(base, GROUP), pl.ds(base + GROUP, GROUP)
        result = lat_product(ctrl_ref, first, second)
        top, bottom = result[:, :lon_cols], result[:, lon_cols:]
        g_ref[first, :] = top
        g_ref[second, :] = bottom
        pack(top, bottom, half_of(k))

    def lat_last(k):
        base = pl.multiple_of(k * CHUNK, CHUNK)
        first, second = pl.ds(base, GROUP), pl.ds(base + GROUP, GROUP)
        result = lat_product(g_ref, first, second)
        inc_ref[first, :] = result[:, :lon_cols] * std_row_ref[first, :]
        inc_ref[second, :] = result[:, lon_cols:] * std_row_ref[second, :]

    def lat_rest():
        result = lat_product(g_ref, pl.ds(rows - CHUNK, GROUP), pl.ds(rows - GROUP, GROUP))
        kept = jnp.concatenate([result[:, :lon_cols], result[:, lon_cols:]], axis=0)[CHUNK - rest:]
        inc_ref[last, :] = kept * std_row_ref[last, :]

    def lon_product(ref, start, count, part):
        half = count // 2
        both = jnp.concatenate([from_left_ref[part, :], from_right_ref[part, :]], axis=1)
        sides = matmul(both, edge_ref[0]) + matmul(both, edge_ref[1])
        high, low = halves(ref[pl.ds(start, count), :])
        own = matmul(high, mid_ref[...])
        own = own[:, :lon_cols] + own[:, lon_cols:] + matmul(low, mid_ref[:, :lon_cols])
        return own[:half] + sides[:, :lon_cols], own[half:] + sides[:, lon_cols:]

    def lon_last(k):
        base = pl.multiple_of(k * CHUNK, CHUNK)
        first, second = pl.ds(base, GROUP), pl.ds(base + GROUP, GROUP)
        top, bottom = lon_product(g_ref, base, CHUNK, half_of(k))
        inc_ref[first, :] = top * std_row_ref[first, :]
        inc_ref[second, :] = bottom * std_row_ref[second, :]

    def lon_first(start, count, part):
        first, second = pl.ds(start, count // 2), pl.ds(start + count // 2, count // 2)
        top, bottom = lon_product(ctrl_ref, start, count, part)
        g_ref[first, :] = top
        g_ref[second, :] = bottom
        own_ref[first, :] = top.astype(jnp.bfloat16)
        own_ref[second, :] = bottom.astype(jnp.bfloat16)

    def pick(start, count, group):
        values = inc_ref[pl.ds(start, count), :].astype(jnp.bfloat16)
        found = across(cell_ref[...], values)
        mine = (iota(row_ref.shape, 1) & (lat_rows - 1)) == row_ref[...]
        parts = []
        for at in range(0, count, lon_cols):
            piece = found[:, at:at + lon_cols]
            parts.append(jnp.where(mine[:, : piece.shape[1]], piece, 0.0).astype(jnp.bfloat16))
        masked = jnp.concatenate(parts, axis=1)
        gather = (iota((count, lon_cols), 0) >> log_lat) == iota((count, lon_cols), 1)
        result = matmul(masked, jnp.where(gather, 1.0, 0.0).astype(jnp.bfloat16))
        result = result.reshape(devices, 8, lon_cols)[:, :slots_each, :]
        pick_ref[:, :, pl.ds(pl.multiple_of(group * lon_cols, lon_cols), lon_cols)] = result.astype(jnp.bfloat16)

    def send_back(group):
        def give(d, carry):
            back((me + d) % devices, group).start()
            return carry

        lax.fori_loop(1, devices, give, 0)

    def learn():
        def hear(d, carry):
            other = (me + d) % devices
            asked = request(other, other, other, other)
            asked.wait_send()
            asked.wait_recv()
            return carry

        lax.fori_loop(1, devices, hear, 0)
        listed = jnp.broadcast_to(table_ref[...].astype(jnp.float32), (devices, 8, table_ref.shape[2]))
        wants = iota(listed.shape, 2) == iota(listed.shape, 1) + me * slots_each
        cell = jnp.sum(jnp.where(wants, listed, 0.0), axis=2, keepdims=True).astype(jnp.int32)
        cell = jnp.broadcast_to(cell, (devices, 8, lon_cols)).reshape(devices * 8, lon_cols)
        row_ref[...] = cell >> log_lon
        cell_ref[...] = jnp.where((cell & (lon_cols - 1)) == iota(cell.shape, 1), 1.0, 0.0).astype(jnp.bfloat16)

    each = -(-(lon // 2) // 4)
    rounds = -(-(lon // 2) // each)

    def stage(k, carry):
        def arrive(k, part):
            swap(k, part).wait_recv()

            @pl.when(onward)
            def _():
                forward(k, part).start()

        def await_far(k, part):
            @pl.when(comes)
            def _():
                forward(k, part).wait_recv()

        @pl.when(k < full)
        def _():
            arrive(k, chunk_of(k))

        @pl.when(k == full)
        def _():
            arrive(full, last)

        @pl.when(k < rounds)
        def _():
            def step(n, carry):
                pl.semaphore_wait(token_sem.at[0], 1)
                pl.semaphore_wait(token_sem.at[1], 1)

                @pl.when(k * each + n + 1 < rounds * each)
                def _():
                    pass_tokens()

                return carry

            lax.fori_loop(0, each, step, 0)

        @pl.when(k == rounds - 1)
        def _():
            lax.fori_loop(1, devices, ask, 0)

        def await_lon(k, part):
            to_right(k, part).wait_recv()
            to_left(k, part).wait_recv()

        ahead, behind, done = k + early, k - 2, k - 4

        @pl.when(ahead < full)
        def _():
            await_lon(ahead, half_of(ahead))
            lon_first(pl.multiple_of(ahead * CHUNK, CHUNK), CHUNK, half_of(ahead))
            swap(ahead, chunk_of(ahead)).start()

        @pl.when(ahead == full)
        def _():
            await_lon(full, last_half)
            lon_first(full * CHUNK, rest, last_half)
            swap(full, last).start()

        @pl.when(jnp.logical_and(behind >= 0, behind < early))
        def _():
            await_far(behind, chunk_of(behind))
            lat_then_send(behind)

        @pl.when(jnp.logical_and(done >= 0, done < early))
        def _():
            await_lon(done, half_of(done))
            lon_last(done)

        @pl.when(jnp.logical_and(behind >= 0, behind < early))
        def _():
            send_lon(behind, half_of(behind))

        @pl.when(jnp.logical_and(behind >= early, behind < full))
        def _():
            await_far(behind, chunk_of(behind))
            lat_last(behind)

        @pl.when(k == 5)
        def _():
            learn()

        def give(group):
            pick(pl.multiple_of(group * 2 * CHUNK, 2 * CHUNK), 2 * CHUNK, group)
            send_back(group)

        @pl.when(jnp.logical_and(jnp.logical_and(done >= 0, done < early), done % 2 == 1))
        def _():
            give(done // 2)

        @pl.when(jnp.logical_and(jnp.logical_and(behind >= early, behind < full), behind % 2 == 1))
        def _():
            give(behind // 2)

        @pl.when(behind == full)
        def _():
            await_far(full, last)
            lat_rest()
            pick(full * CHUNK, rest, full // 2)
            send_back(full // 2)

        return carry

    lax.fori_loop(0, full + 3, stage, 0)
    got_ref[me] = pick_ref[me]

    def finish(k, part, half):
        swap(k, part).wait_send()

        @pl.when(onward)
        def _():
            forward(k, part).wait_send()

        to_right(k, half).wait_send()
        to_left(k, half).wait_send()

    def finish_full(k, carry):
        finish(k, chunk_of(k), half_of(k))
        return carry

    lax.fori_loop(0, full, finish_full, 0)
    finish(full, last, last_half)

    def collect(d, carry):
        other = (me + d) % devices
        whole = remote(
            pick_ref.at[other], got_ref.at[other], col_send.at[other], col_recv.at[other], place(other)
        )
        whole.wait_send()
        whole.wait_recv()
        return carry

    lax.fori_loop(1, devices, collect, 0)


def dense_step(control, col_dev, col_cell, std_dev, slots_each):
    lat, lon = lax.axis_size("lat"), lax.axis_size("lon")
    width, lat_rows, lon_cols = control.shape
    devices, rows = lat * lon, width * lat_rows
    pieces = rows // CHUNK + 1
    lanes = lane_tiles(width) * lon_cols
    listed = (1, lane_tiles(devices * slots_each) * 128)
    vmem, hbm = pl.BlockSpec(memory_space=pltpu.VMEM), pl.BlockSpec(memory_space=pltpu.HBM)
    dma = pltpu.SemaphoreType.DMA
    bf16, f32 = jnp.bfloat16, jnp.float32
    return pl.pallas_call(
        functools.partial(dense_kernel, lat, lon, lat_rows, slots_each),
        in_specs=[hbm] * 4,
        out_specs=[vmem, vmem, vmem],
        out_shape=[
            jax.ShapeDtypeStruct((rows, lon_cols), f32),
            jax.ShapeDtypeStruct((devices, *listed), jnp.int32),
            jax.ShapeDtypeStruct((devices, slots_each, lanes), bf16),
        ],
        scratch_shapes=[
            pltpu.VMEM((rows, lon_cols), f32),
            pltpu.VMEM((1, col_cell.shape[0]), jnp.int32),
            pltpu.VMEM((1, col_cell.shape[0]), jnp.int32),
            pltpu.SMEM(std_dev.shape, f32),
            pltpu.VMEM((1, *listed), jnp.int32),
            pltpu.VMEM((rows, lon_cols), bf16),
            pltpu.VMEM((rows, lon_cols), bf16),
            pltpu.VMEM((rows, lon_cols), bf16),
            pltpu.VMEM((rows, lon_cols), f32),
            *[pltpu.VMEM((rows // 2, lon_cols), bf16)] * 4,
            pltpu.VMEM((GROUP, 7 * GROUP), bf16),
            pltpu.VMEM((lon_cols, 2 * lon_cols), bf16),
            pltpu.VMEM((2, 2 * lon_cols, 2 * lon_cols), bf16),
            pltpu.VMEM((rows, lon_cols), f32),
            pltpu.VMEM((devices * 8, lon_cols), bf16),
            pltpu.VMEM((devices * 8, lon_cols), jnp.int32),
            pltpu.VMEM((devices, slots_each, lanes), bf16),
            *[dma((pieces,))] * 4,
            *[dma((2, pieces))] * 2,
            *[dma((devices,))] * 4,
            dma((pieces,)),
            dma((3,)),
            pltpu.SemaphoreType.REGULAR((2,)),
        ],
        compiler_params=pltpu.CompilerParams(collective_id=0, has_side_effects=True, vmem_limit_bytes=DENSE_VMEM),
        name="dense",
    )(control.reshape(rows, lon_cols), col_dev.reshape(1, -1), col_cell[None, :], std_dev)


def lane_tiles(count):
    return -(-count // 128)


PIECE = 16


def piece_slot(index, slots_each, piece, kind):
    device, row = index >> 4, index & (PIECE - 1)
    spare = PIECE - 2 * slots_each
    if kind < 2:
        number = row - kind * slots_each
        valid = jnp.logical_and(number >= 0, number < slots_each)
    else:
        number = row - 2 * slots_each + piece * spare
        valid = jnp.logical_and(row >= 2 * slots_each, number < slots_each)
    return jnp.where(valid, device * 8 + number, -1)


def sounding_part(
    slots_each, step,
    jac_hbm, got_ref, dev_ref, innov_ref, inv_ref, dep_ref, out_ref,
    jac_ref, apart_ref, col_ref, tail_ref, weight_ref, grad_ref, jac_sem,
):
    channels, count, width = jac_ref.shape
    steps = channels // step
    devices, lanes = got_ref.shape[0], got_ref.shape[2]
    most = width // 128 * 128
    iota = lambda shape, axis: lax.broadcasted_iota(jnp.int32, shape, axis)

    def load(b):
        part = pl.ds(b * step, step)
        return pltpu.make_async_copy(jac_hbm.at[part], jac_ref.at[part], jac_sem.at[b])

    def begin(b, carry):
        load(b).start()
        return carry

    lax.fori_loop(0, steps, begin, 0)
    apart_ref[...] = jnp.zeros_like(apart_ref)
    apart_ref[:, :slots_each, :] = got_ref[...].astype(jnp.float32)
    onehot, _, slot = slots_of(dev_ref, dev_ref, 8, devices * 8)
    onehot = jnp.where(onehot, 1.0, 0.0).astype(jnp.bfloat16)
    columns = matmul(onehot, apart_ref[...].reshape(devices * 8, lanes).astype(jnp.bfloat16))
    col_ref[...] = columns.astype(jnp.bfloat16)
    tail_ref[...] = columns[:, most:]
    grad_ref[...] = jnp.zeros_like(grad_ref)
    square = (count, count)

    def product(b):
        block = jac_ref[pl.ds(b * step, step), :, :most]
        return across(block.reshape(step * count, most), col_ref[:, :most])

    def depart(b, found):
        mine = iota(square, 0) == iota(square, 1)
        for k in range(step):
            channel = b * step + k
            own = jnp.where(mine, found[k * count:(k + 1) * count] - innov_ref[pl.ds(channel, 1), :], 0.0)
            if width > most:
                tail = jac_ref[channel, :, most:].astype(jnp.float32) * tail_ref[:, : width - most]
                own = own + jnp.concatenate([tail, jnp.zeros((count, count - (width - most)), jnp.float32)], axis=1)
            departure = jnp.sum(own, axis=1, keepdims=True)
            dep_ref[pl.ds(channel, 1), :] = jnp.sum(jnp.where(mine, departure, 0.0), axis=0, keepdims=True)
            weight = (departure * inv_ref[channel]).astype(jnp.bfloat16).astype(jnp.float32)
            weight_ref[k] = jnp.broadcast_to(weight, (count, 128))

    def gradient(b):
        for group in range(0, count, 16):
            part = slice(group, group + 16)
            for lane in range(0, width, 128):
                end = min(lane + 128, width)
                total = grad_ref[part, lane:end]
                for k in range(step):
                    values = jac_ref[b * step + k, part, lane:end].astype(jnp.float32)
                    total = total + values * weight_ref[k, part, : end - lane]
                grad_ref[part, lane:end] = total

    load(0).wait()
    depart(0, product(0))

    def body(b, carry):
        load(b).wait()
        found = product(b)
        gradient(b - 1)
        depart(b, found)
        return carry

    lax.fori_loop(1, steps, body, 0)
    gradient(steps - 1)
    grads = grad_ref[...].astype(jnp.bfloat16)
    for piece in range(2):
        packed = jnp.zeros((devices * PIECE, 128), jnp.float32)
        for kind in range(3):
            held = piece_slot(iota((devices * PIECE, count), 0), slots_each, piece, kind)
            onehot = jnp.where(held == slot, 1.0, 0.0).astype(jnp.bfloat16)
            tile = (2 * piece + kind if kind < 2 else 4) * 128
            packed = packed + matmul(onehot, grads[:, tile:tile + 128])
        out_ref[piece] = packed.astype(out_ref.dtype)


def adjoint_kernel(
    lat, lon, lat_rows, slots_each, cuts, step,
    jac_hbm, got_ref, dev_ref, innov_ref, inv_ref, table_ref, std_ref,
    dep_ref, out_ref,
    jac_ref, apart_ref, col_ref, tail_ref, scale_ref, grad_ref, jac_sem,
    give_ref, arrived_ref, compact_ref, grads_ref, weight_ref, std_row_ref,
    give_send, give_recv, swap_send, swap_recv, far_send, far_recv, lon_send, lon_recv,
):
    devices = lat * lon
    slots = devices * slots_each
    rows, lon_cols = out_ref.shape
    log_lon = lon_cols.bit_length() - 1
    row, column = lax.axis_index("lat"), lax.axis_index("lon")
    me = row * lon + column
    odd = row % 2
    near = 1 - 2 * odd
    partner, stride = row + near, 2 * near
    onward = jnp.logical_and(row + stride >= 0, row + stride < lat)
    comes = jnp.logical_and(row - stride >= 0, row - stride < lat)
    place = lambda other: (other // lon, other % lon)
    iota = lambda shape, axis: lax.broadcasted_iota(jnp.int32, shape, axis)
    chunks = range(len(cuts) - 1)
    part = [pl.ds(cuts[j], cuts[j + 1] - cuts[j]) for j in chunks]

    @pl.when(jnp.logical_not(comes))
    def _():
        grads_ref[2] = jnp.zeros_like(grads_ref[2])

    barrier = pltpu.get_barrier_semaphore()

    def greet(d, carry):
        pl.semaphore_signal(barrier, inc=1, device_id=place((me + d) % devices), device_id_type=MESH)
        return carry

    lax.fori_loop(1, devices, greet, 0)
    sounding_part(
        slots_each, step, jac_hbm, got_ref, dev_ref, innov_ref, inv_ref, dep_ref, give_ref,
        jac_ref, apart_ref, col_ref, tail_ref, scale_ref, grad_ref, jac_sem,
    )
    std_row_ref[...] = jnp.zeros_like(std_row_ref)
    std_row_ref[:, : std_ref.shape[0]] = std_ref[...].reshape(1, -1)

    def piece_of(d):
        return pl.ds(pl.multiple_of(d * PIECE, PIECE), PIECE)

    arrived_ref[:, piece_of(me), :] = give_ref[:, piece_of(me), :]
    pl.semaphore_wait(barrier, devices - 1)

    def remote(source, target, send, recv, device):
        return pltpu.make_async_remote_copy(
            src_ref=source, dst_ref=target, send_sem=send, recv_sem=recv, device_id=device, device_id_type=MESH
        )

    def hand(j, other, source):
        return remote(
            give_ref.at[j, piece_of(other)], arrived_ref.at[j, piece_of(source)],
            give_send.at[j, other], give_recv.at[j, source], place(other),
        )

    for j in range(2):

        def give(d, carry):
            hand(j, (me + d) % devices, me).start()
            return carry

        lax.fori_loop(1, devices, give, 0)

    total = 9 * slots
    flat = (1, total)
    at = iota(flat, 1).astype(jnp.float32)
    block = jnp.floor((at + 0.5) / slots)
    within = at - block * slots
    source = jnp.floor((within + 0.5) / slots_each)
    order = within - source * slots_each
    up = jnp.floor((block + 0.5) / 3.0)
    along = block - 3.0 * up
    lat_shift = jnp.where(up == 0.0, 0.0, jnp.where(up == 1.0, 1.0, -1.0)) * near.astype(jnp.float32)
    lon_shift = jnp.where(along == 0.0, 0.0, jnp.where(along == 1.0, -1.0, 1.0))
    owner_row = jnp.clip(row.astype(jnp.float32) + lat_shift, 0.0, lat - 1.0)
    owner_col = column.astype(jnp.float32) + lon_shift
    owner_col = jnp.where(owner_col < 0.0, owner_col + lon, jnp.where(owner_col >= lon, owner_col - lon, owner_col))
    wanted = ((owner_row * lon + owner_col) * slots_each + order).astype(jnp.int32)
    listed = table_ref[...].reshape(devices, table_ref.shape[2])
    chosen = jnp.where(iota((listed.shape[1], total), 0) == wanted, 1.0, 0.0).astype(jnp.bfloat16)
    mine = iota((devices, total), 0) == source.astype(jnp.int32)

    def position(values):
        found = matmul(values.astype(jnp.bfloat16), chosen)
        return jnp.sum(jnp.where(mine, found, 0.0), axis=0, keepdims=True)

    slot_row = position(listed >> log_lon) + lat_shift * lat_rows
    slot_col = position(listed & (lon_cols - 1)) + lon_shift * lon_cols
    down = iota((lon_cols, total), 0).astype(jnp.float32)
    col_weight = tap_value(slot_col - down, lon_cols // 2)
    for i in range(0, lat_rows, 2):
        for k in range(2):
            value = col_weight * tap_value(slot_row - (i + k), LHALF)
            high, low = halves(value)
            weight_ref[i // 2, k * lon_cols:(k + 1) * lon_cols, :] = high
            weight_ref[i // 2, (k + 2) * lon_cols:(k + 3) * lon_cols, :] = low

    spread = (slots, devices * PIECE)
    for at, (piece, kind) in enumerate(((0, 0), (0, 1), (0, 2), (1, 2))):
        held = piece_slot(iota(spread, 1), slots_each, piece, kind)
        wanted = jnp.where(held < 0, -1, (held >> 3) * slots_each + (held & 7))
        compact_ref[at] = jnp.where(wanted == iota(spread, 0), 1.0, 0.0).astype(jnp.bfloat16)

    def receive(j):
        def wait(d, carry):
            other = (me + d) % devices
            hand(j, other, other).wait_send()
            hand(j, other, other).wait_recv()
            return carry

        lax.fori_loop(1, devices, wait, 0)
        for kind in range(2):
            tile = (2 * j + kind) * 128
            grads_ref[0, 0, :, tile:tile + 128] = matmul(compact_ref[kind], arrived_ref[j]).astype(jnp.bfloat16)

    def receive_rest():
        rest = matmul(compact_ref[2], arrived_ref[0]) + matmul(compact_ref[3], arrived_ref[1])
        grads_ref[0, 0, :, part[2]] = rest.astype(jnp.bfloat16)

    def swap(j, b):
        return remote(
            grads_ref.at[0, b, :, part[j]], grads_ref.at[1, b, :, part[j]],
            swap_send.at[j, b], swap_recv.at[j, b], (partner, column),
        )

    def forward(j, b):
        return remote(
            grads_ref.at[1, b, :, part[j]], grads_ref.at[2, b, :, part[j]],
            far_send.at[j, b], far_recv.at[j, b], (row + stride, column),
        )

    def to_right(j, a):
        return remote(
            grads_ref.at[a, 0, :, part[j]], grads_ref.at[a, 1, :, part[j]],
            lon_send.at[0, j, a], lon_recv.at[0, j, a], (row, (column + 1) % lon),
        )

    def to_left(j, a):
        return remote(
            grads_ref.at[a, 0, :, part[j]], grads_ref.at[a, 2, :, part[j]],
            lon_send.at[1, j, a], lon_recv.at[1, j, a], (row, (column + lon - 1) % lon),
        )

    def send_lon(j, a):
        to_right(j, a).start()
        to_left(j, a).start()

    def await_lon(j, a):
        to_right(j, a).wait_recv()
        to_left(j, a).wait_recv()

    def pass_on(j, b):
        swap(j, b).wait_recv()

        @pl.when(onward)
        def _():
            forward(j, b).start()

    def await_far(j, b):
        @pl.when(comes)
        def _():
            forward(j, b).wait_recv()

    def compute(j):
        count = cuts[j + 1] - cuts[j]
        kept = min(count, rows // lat_rows - cuts[j])
        grads = grads_ref[:, :, :, part[j]].reshape(total, count)

        def two(i, carry):
            result = matmul(weight_ref[i], grads)
            result = (result[: 2 * lon_cols] + result[2 * lon_cols:]) * std_row_ref[:, part[j]]
            for k in range(2):
                piece = result[k * lon_cols:(k + 1) * lon_cols].T
                out_ref[pl.ds(cuts[j] * lat_rows + 2 * i + k, kept, stride=lat_rows), :] = piece[:kept]
            return carry

        lax.fori_loop(0, lat_rows // 2, two, 0)

    lon_first = (0, 2)
    receive(0)
    send_lon(0, 0)
    swap(0, 0).start()
    receive(1)
    swap(1, 0).start()
    receive_rest()
    send_lon(2, 0)
    swap(2, 0).start()
    pass_on(0, 0)
    await_lon(0, 0)
    swap(0, 1).start()
    swap(0, 2).start()
    pass_on(1, 0)
    send_lon(1, 0)
    send_lon(1, 1)
    pass_on(2, 0)
    await_lon(2, 0)
    swap(2, 1).start()
    swap(2, 2).start()
    await_far(1, 0)
    send_lon(1, 2)
    for j in lon_first:
        pass_on(j, 1)
        pass_on(j, 2)
    for j in chunks:
        if j in lon_first:
            for b in range(3):
                await_far(j, b)
        else:
            for a in range(3):
                await_lon(j, a)
        compute(j)
    for j in chunks:
        for b in range(3) if j in lon_first else (0,):
            swap(j, b).wait_send()

            @pl.when(onward)
            def _():
                forward(j, b).wait_send()

        for a in (0,) if j in lon_first else range(3):
            to_right(j, a).wait_send()
            to_left(j, a).wait_send()


def analysis_step(jacobian, got, table, col_dev, innovation, inv_error, std_dev, lat_rows, lon_cols):
    lat, lon = lax.axis_size("lat"), lax.axis_size("lon")
    count, channels, width = jacobian.shape
    devices, slots_each, lanes = got.shape
    slots, rows = devices * slots_each, width * lat_rows
    cuts = [0, 256, 512, lanes]
    pieces = len(cuts) - 1
    step = next(n for n in (10, 8, 6, 5, 4, 3, 2, 1) if channels % n == 0)
    vmem, hbm = pl.BlockSpec(memory_space=pltpu.VMEM), pl.BlockSpec(memory_space=pl.ANY)
    dma = pltpu.SemaphoreType.DMA
    bf16, f32 = jnp.bfloat16, jnp.float32
    departures, adjoint = pl.pallas_call(
        functools.partial(adjoint_kernel, lat, lon, lat_rows, slots_each, cuts, step),
        in_specs=[hbm, vmem, vmem, vmem, pl.BlockSpec(memory_space=pltpu.SMEM), vmem, vmem],
        out_specs=[vmem, vmem],
        out_shape=[
            jax.ShapeDtypeStruct((channels, count), f32),
            jax.ShapeDtypeStruct((rows, lon_cols), f32),
        ],
        scratch_shapes=[
            pltpu.VMEM((channels, count, width), bf16),
            pltpu.VMEM((devices, 8, lanes), f32),
            pltpu.VMEM((count, lanes), bf16),
            pltpu.VMEM((count, 128), f32),
            pltpu.VMEM((step, count, 128), f32),
            pltpu.VMEM((count, lanes), f32),
            dma((channels // step,)),
            pltpu.VMEM((2, devices * PIECE, 128), bf16),
            pltpu.VMEM((2, devices * PIECE, 128), bf16),
            pltpu.VMEM((4, slots, devices * PIECE), bf16),
            pltpu.VMEM((3, 3, slots, lanes), bf16),
            pltpu.VMEM((lat_rows // 2, 4 * lon_cols, 9 * slots), bf16),
            pltpu.VMEM((1, lanes), f32),
            *[dma((2, devices))] * 2,
            *[dma((pieces, 3))] * 4,
            *[dma((2, pieces, 3))] * 2,
        ],
        compiler_params=pltpu.CompilerParams(collective_id=1, has_side_effects=True, vmem_limit_bytes=VMEM),
        name="analysis",
    )(jnp.transpose(jacobian, (1, 0, 2)), got, col_dev.reshape(1, -1), innovation.T, inv_error, table, std_dev)
    return departures, adjoint


def local(control, std_dev, col_dev, col_cell, jacobian, innovation, inv_error):
    width, lat_rows, lon_cols = control.shape
    devices = lax.axis_size("lat") * lax.axis_size("lon")
    slots_each = max(2, 2 * col_cell.shape[0] // devices)
    increment, table, got = dense_step(control, col_dev, col_cell, std_dev, slots_each)
    departures, adjoint = analysis_step(
        jacobian, got, table, col_dev, innovation, inv_error, std_dev, lat_rows, lon_cols
    )
    return departures.T, increment.reshape(control.shape), adjoint.reshape(control.shape)


def solution(mesh):
    placed = (
        P(None, "lat", "lon"),
        P(),
        P(("lat", "lon"), None),
        P(("lat", "lon")),
        P(("lat", "lon"), None, None),
        P(("lat", "lon"), None),
        P(),
    )
    return jax.shard_map(
        local,
        mesh=mesh,
        in_specs=placed,
        out_specs=(P(("lat", "lon"), None), P(None, "lat", "lon"), P(None, "lat", "lon")),
        check_vma=False,
    )
```

```python
import functools
import math

import jax
import jax.numpy as jnp
from jax import lax
from jax.experimental import pallas as pl
from jax.experimental.pallas import tpu as pltpu
from jax.sharding import PartitionSpec as P

LHALF = 8
MESH = pl.DeviceIdType.MESH
VMEM = 48 << 20
DENSE_VMEM = 64300000


def tap_weights(offset, half_width):
    spread = 2.0 * half_width / 3.0
    taps = jnp.arange(-half_width, half_width + 1, dtype=jnp.int32).astype(jnp.float32)
    norm_total = jnp.sqrt(jnp.sum(jnp.exp(-taps * taps / (spread * spread))))
    weights = jnp.exp(-offset * offset / (2.0 * spread * spread)) / norm_total
    return jnp.where(jnp.abs(offset) <= half_width, weights, jnp.zeros_like(weights))


def halves(weights):
    high = weights.astype(jnp.bfloat16)
    return high, (weights - high.astype(jnp.float32)).astype(jnp.bfloat16)


def tap_value(offset, half_width):
    spread = 2.0 * half_width / 3.0
    norm_total = math.sqrt(sum(math.exp(-e * e / (spread * spread)) for e in range(-half_width, half_width + 1)))
    weights = jnp.exp(-offset * offset / (2.0 * spread * spread)) / norm_total
    return jnp.where(jnp.abs(offset) <= half_width, weights, 0.0)


GROUP = 256
CHUNK = 2 * GROUP


def matmul(left, right):
    return jnp.dot(left, right, preferred_element_type=jnp.float32)


def across(left, right):
    return lax.dot_general(left, right, (((1,), (1,)), ((), ())), preferred_element_type=jnp.float32)


def slots_of(dev_ref, cell_ref, slots_each, count):
    sound_count = dev_ref.shape[1]
    square = (sound_count, sound_count)
    iota = lambda shape, axis: lax.broadcasted_iota(jnp.int32, shape, axis)
    before = iota(square, 0) - iota(square, 1)
    across_lanes = jnp.broadcast_to(dev_ref[...].astype(jnp.float32), square)
    upright = lambda spread: jnp.sum(jnp.where(before == 0, spread, 0.0), axis=1, keepdims=True)
    down = upright(across_lanes)
    alike = across_lanes == down
    order = jnp.sum(jnp.where(jnp.logical_and(alike, before > 0), 1.0, 0.0), axis=1, keepdims=True)
    slot = down * slots_each + order
    onehot = slot.astype(jnp.int32) == iota((sound_count, count), 1)
    cell = upright(jnp.broadcast_to(cell_ref[...].astype(jnp.float32), square))
    order = jnp.sum(jnp.where(jnp.logical_and(alike, before < 0), 1.0, 0.0), axis=0, keepdims=True)
    return onehot, cell, (dev_ref[...].astype(jnp.float32) * slots_each + order).astype(jnp.int32)


def dense_kernel(
    lat, lon, lat_rows, slots_each,
    ctrl_hbm, dev_hbm, ask_hbm, std_hbm,
    inc_ref, table_ref, got_ref,
    ctrl_ref, dev_ref, ask_ref, std_ref, wanted_ref, own_ref, swap_ref, far_ref, g_ref, to_right_ref, to_left_ref, from_left_ref, from_right_ref,
    band_ref, mid_ref, edge_ref, std_row_ref, cell_ref, row_ref, pick_ref,
    swap_send, swap_recv, far_send, far_recv, lon_send, lon_recv,
    want_send, want_recv, col_send, col_recv, load_sem, small_sem, token_sem,
):
    rows, lon_cols = ctrl_ref.shape
    width = rows // lat_rows
    full, rest = rows // CHUNK, rows % CHUNK
    early = 2
    log_lat, log_lon = lat_rows.bit_length() - 1, lon_cols.bit_length() - 1
    lon_half = lon_cols // 2
    row, column = lax.axis_index("lat"), lax.axis_index("lon")
    devices, me = lat * lon, row * lon + column
    odd = row % 2
    partner, step = row + 1 - 2 * odd, 2 - 4 * odd
    onward = jnp.logical_and(row + step >= 0, row + step < lat)
    comes = jnp.logical_and(row - step >= 0, row - step < lat)
    place = lambda other: (other // lon, other % lon)
    iota = lambda shape, axis: lax.broadcasted_iota(jnp.int32, shape, axis)

    barrier = pltpu.get_barrier_semaphore()

    right, left = (row, (column + 1) % lon), (row, (column + lon - 1) % lon)

    def tell(semaphore, device):
        pl.semaphore_signal(semaphore, inc=1, device_id=device, device_id_type=MESH)

    for d in range(1, lat):
        tell(barrier, ((row + d) % lat, column))
    tell(barrier, right)
    tell(barrier, left)

    def chunk_of(k):
        return pl.ds(pl.multiple_of(k * CHUNK, CHUNK), CHUNK)

    def half_of(k):
        return pl.ds(pl.multiple_of(k * GROUP, GROUP), GROUP)

    last, last_half = pl.ds(full * CHUNK, rest), pl.ds(full * GROUP, rest // 2)

    def remote(source, target, send, recv, device):
        return pltpu.make_async_remote_copy(
            src_ref=source, dst_ref=target, send_sem=send, recv_sem=recv, device_id=device, device_id_type=MESH
        )

    def request(dst, send, recv, other):
        return remote(wanted_ref.at[0], table_ref.at[dst], want_send.at[send], want_recv.at[recv], place(other))

    def swap(k, part):
        return remote(own_ref.at[part], swap_ref.at[part], swap_send.at[k], swap_recv.at[k], (partner, column))

    def forward(k, part):
        return remote(swap_ref.at[part], far_ref.at[part], far_send.at[k], far_recv.at[k], (row + step, column))

    def to_right(k, part):
        return remote(
            to_right_ref.at[part], from_left_ref.at[part], lon_send.at[0, k], lon_recv.at[0, k],
            (row, (column + 1) % lon),
        )

    def to_left(k, part):
        return remote(
            to_left_ref.at[part], from_right_ref.at[part], lon_send.at[1, k], lon_recv.at[1, k],
            (row, (column + lon - 1) % lon),
        )

    def back(d, group):
        part = pl.ds(pl.multiple_of(group * lon_cols, lon_cols), lon_cols)
        return remote(
            pick_ref.at[d, :, part], got_ref.at[me, :, part], col_send.at[d], col_recv.at[me], place(d)
        )

    def round_own(part):
        own_ref[part, :] = ctrl_ref[part, :].astype(jnp.bfloat16)

    def load(k, part):
        return pltpu.make_async_copy(ctrl_hbm.at[part], ctrl_ref.at[part], load_sem.at[k])

    def begin(k, carry):
        load(k, chunk_of(k)).start()
        return carry

    small = [
        pltpu.make_async_copy(source, target, small_sem.at[at])
        for at, (source, target) in enumerate(((dev_hbm, dev_ref), (ask_hbm, ask_ref), (std_hbm, std_ref)))
    ]
    for copy in small:
        copy.start()
    lax.fori_loop(0, full, begin, 0)
    load(full, last).start()
    for copy in small:
        copy.wait()
    onehot, cell_at, _ = slots_of(dev_ref, ask_ref, slots_each, wanted_ref.shape[2])
    wanted_ref[0] = jnp.sum(jnp.where(onehot, cell_at, 0.0), axis=0, keepdims=True).astype(jnp.int32)

    @pl.when(jnp.logical_not(comes))
    def _():
        far_ref[...] = jnp.zeros_like(far_ref)

    load(0, chunk_of(0)).wait()
    round_own(chunk_of(0))
    pl.semaphore_wait(barrier, lat + 1)

    def pass_tokens():
        tell(token_sem.at[0], right)
        tell(token_sem.at[1], left)

    pass_tokens()

    def ask(d, carry):
        request(me, (me + d) % devices, me, (me + d) % devices).start()
        return carry


    def send_own(k, carry):
        load(k + 1, chunk_of(k + 1)).wait()

        @pl.when(k + 1 < early)
        def _():
            round_own(chunk_of(k + 1))

        swap(k, chunk_of(k)).start()
        return carry

    lax.fori_loop(0, early, send_own, 0)
    lane = iota((1, lon_cols), 1)

    def pack(first, second, part):
        right = jnp.where(lane < lon_half, pltpu.roll(first, lon_half, 1), second)
        left = jnp.where(lane < lon_half, first, pltpu.roll(second, lon_half, 1))
        to_right_ref[part, :] = right.astype(jnp.bfloat16)
        to_left_ref[part, :] = left.astype(jnp.bfloat16)

    def send_lon(k, part):
        to_right(k, part).start()
        to_left(k, part).start()

    def pack_own(k, carry):
        base = pl.multiple_of(k * CHUNK, CHUNK)
        pack(ctrl_ref[pl.ds(base, GROUP), :], ctrl_ref[pl.ds(base + GROUP, GROUP), :], half_of(k))

        @pl.when(k + 1 < full)
        def _():
            load(k + 1, chunk_of(k + 1)).wait()

        send_lon(k, half_of(k))
        return carry

    lax.fori_loop(early, full, pack_own, 0)
    load(full, last).wait()
    middle = full * CHUNK + rest // 2
    pack(ctrl_ref[full * CHUNK:middle, :], ctrl_ref[middle:, :], last_half)
    table_ref[me] = wanted_ref[0]
    send_lon(full, last_half)

    square = (GROUP, GROUP)
    same = (iota(square, 0) >> log_lat) == (iota(square, 1) >> log_lat)
    apart = (iota(square, 1) & (lat_rows - 1)) - (iota(square, 0) & (lat_rows - 1))

    def lat_band(shift):
        return halves(jnp.where(same, tap_value((apart + shift).astype(jnp.float32), LHALF), 0.0))

    high, low = lat_band(0)
    swap_high, swap_low = lat_band(lat_rows - 2 * lat_rows * odd)
    far_high, far_low = lat_band(2 * lat_rows * odd - lat_rows)
    for at, block in enumerate((high, high, low, swap_high, swap_low, far_high, far_low)):
        band_ref[:, at * GROUP:(at + 1) * GROUP] = block
    along = iota((lon_cols, lon_cols), 0) - iota((lon_cols, lon_cols), 1)
    high, low = halves(tap_value(along.astype(jnp.float32), lon_half))
    mid_ref[:, :lon_cols] = high
    mid_ref[:, lon_cols:] = low
    wide = (2 * lon_cols, 2 * lon_cols)
    source, target = iota(wide, 0), iota(wide, 1)
    within, which = source & (lon_half - 1), (source >> (log_lon - 1)) & 1
    column_at = jnp.where(source < lon_cols, within - lon_half, within + lon_cols)
    apart = column_at - (target & (lon_cols - 1))
    value = jnp.where(which == (target >> log_lon), tap_value(apart.astype(jnp.float32), lon_half), 0.0)
    high, low = halves(value)
    edge_ref[0] = high
    edge_ref[1] = low

    def spread(c, carry):
        std_row_ref[pl.ds(pl.multiple_of(c * lat_rows, lat_rows), lat_rows), :] = jnp.full(
            (lat_rows, lon_cols), std_ref[c], jnp.float32
        )
        return carry

    lax.fori_loop(0, width, spread, 0)

    def lat_product(ref, first, second):
        def pair(ref):
            return jnp.concatenate([ref[first, :], ref[second, :]], axis=1)

        field = pair(ref)
        field_high, field_low = halves(field)
        swapped, far = pair(swap_ref), pair(far_ref)
        stacked = jnp.concatenate([field_high, field_low, field_high, swapped, swapped, far, far], axis=0)
        return matmul(band_ref[...], stacked)

    def lat_then_send(k):
        base = pl.multiple_of(k * CHUNK, CHUNK)
        first, second = pl.ds(base, GROUP), pl.ds(base + GROUP, GROUP)
        result = lat_product(ctrl_ref, first, second)
        top, bottom = result[:, :lon_cols], result[:, lon_cols:]
        g_ref[first, :] = top
        g_ref[second, :] = bottom
        pack(top, bottom, half_of(k))

    def lat_last(k):
        base = pl.multiple_of(k * CHUNK, CHUNK)
        first, second = pl.ds(base, GROUP), pl.ds(base + GROUP, GROUP)
        result = lat_product(g_ref, first, second)
        inc_ref[first, :] = result[:, :lon_cols] * std_row_ref[first, :]
        inc_ref[second, :] = result[:, lon_cols:] * std_row_ref[second, :]

    def lat_rest():
        result = lat_product(g_ref, pl.ds(rows - CHUNK, GROUP), pl.ds(rows - GROUP, GROUP))
        kept = jnp.concatenate([result[:, :lon_cols], result[:, lon_cols:]], axis=0)[CHUNK - rest:]
        inc_ref[last, :] = kept * std_row_ref[last, :]

    def lon_product(ref, start, count, part):
        half = count // 2
        both = jnp.concatenate([from_left_ref[part, :], from_right_ref[part, :]], axis=1)
        sides = matmul(both, edge_ref[0]) + matmul(both, edge_ref[1])
        high, low = halves(ref[pl.ds(start, count), :])
        own = matmul(high, mid_ref[...])
        own = own[:, :lon_cols] + own[:, lon_cols:] + matmul(low, mid_ref[:, :lon_cols])
        return own[:half] + sides[:, :lon_cols], own[half:] + sides[:, lon_cols:]

    def lon_last(k):
        base = pl.multiple_of(k * CHUNK, CHUNK)
        first, second = pl.ds(base, GROUP), pl.ds(base + GROUP, GROUP)
        top, bottom = lon_product(g_ref, base, CHUNK, half_of(k))
        inc_ref[first, :] = top * std_row_ref[first, :]
        inc_ref[second, :] = bottom * std_row_ref[second, :]

    def lon_first(start, count, part):
        first, second = pl.ds(start, count // 2), pl.ds(start + count // 2, count // 2)
        top, bottom = lon_product(ctrl_ref, start, count, part)
        g_ref[first, :] = top
        g_ref[second, :] = bottom
        own_ref[first, :] = top.astype(jnp.bfloat16)
        own_ref[second, :] = bottom.astype(jnp.bfloat16)

    def pick(start, count, group):
        values = inc_ref[pl.ds(start, count), :].astype(jnp.bfloat16)
        found = across(cell_ref[...], values)
        mine = (iota(row_ref.shape, 1) & (lat_rows - 1)) == row_ref[...]
        parts = []
        for at in range(0, count, lon_cols):
            piece = found[:, at:at + lon_cols]
            parts.append(jnp.where(mine[:, : piece.shape[1]], piece, 0.0).astype(jnp.bfloat16))
        masked = jnp.concatenate(parts, axis=1)
        gather = (iota((count, lon_cols), 0) >> log_lat) == iota((count, lon_cols), 1)
        result = matmul(masked, jnp.where(gather, 1.0, 0.0).astype(jnp.bfloat16))
        result = result.reshape(devices, 8, lon_cols)[:, :slots_each, :]
        pick_ref[:, :, pl.ds(pl.multiple_of(group * lon_cols, lon_cols), lon_cols)] = result.astype(jnp.bfloat16)

    def send_back(group):
        def give(d, carry):
            back((me + d) % devices, group).start()
            return carry

        lax.fori_loop(1, devices, give, 0)

    def learn():
        def hear(d, carry):
            other = (me + d) % devices
            asked = request(other, other, other, other)
            asked.wait_send()
            asked.wait_recv()
            return carry

        lax.fori_loop(1, devices, hear, 0)
        listed = jnp.broadcast_to(table_ref[...].astype(jnp.float32), (devices, 8, table_ref.shape[2]))
        wants = iota(listed.shape, 2) == iota(listed.shape, 1) + me * slots_each
        cell = jnp.sum(jnp.where(wants, listed, 0.0), axis=2, keepdims=True).astype(jnp.int32)
        cell = jnp.broadcast_to(cell, (devices, 8, lon_cols)).reshape(devices * 8, lon_cols)
        row_ref[...] = cell >> log_lon
        cell_ref[...] = jnp.where((cell & (lon_cols - 1)) == iota(cell.shape, 1), 1.0, 0.0).astype(jnp.bfloat16)

    each = -(-(lon // 2) // 4)
    rounds = -(-(lon // 2) // each)

    def stage(k, carry):
        def arrive(k, part):
            swap(k, part).wait_recv()

            @pl.when(onward)
            def _():
                forward(k, part).start()

        def await_far(k, part):
            @pl.when(comes)
            def _():
                forward(k, part).wait_recv()

        @pl.when(k < full)
        def _():
            arrive(k, chunk_of(k))

        @pl.when(k == full)
        def _():
            arrive(full, last)

        @pl.when(k < rounds)
        def _():
            def step(n, carry):
                pl.semaphore_wait(token_sem.at[0], 1)
                pl.semaphore_wait(token_sem.at[1], 1)

                @pl.when(k * each + n + 1 < rounds * each)
                def _():
                    pass_tokens()

                return carry

            lax.fori_loop(0, each, step, 0)

        @pl.when(k == rounds - 1)
        def _():
            lax.fori_loop(1, devices, ask, 0)

        def await_lon(k, part):
            to_right(k, part).wait_recv()
            to_left(k, part).wait_recv()

        ahead, behind, done = k + early, k - 2, k - 4

        @pl.when(ahead < full)
        def _():
            await_lon(ahead, half_of(ahead))
            lon_first(pl.multiple_of(ahead * CHUNK, CHUNK), CHUNK, half_of(ahead))
            swap(ahead, chunk_of(ahead)).start()

        @pl.when(ahead == full)
        def _():
            await_lon(full, last_half)
            lon_first(full * CHUNK, rest, last_half)
            swap(full, last).start()

        @pl.when(jnp.logical_and(behind >= 0, behind < early))
        def _():
            await_far(behind, chunk_of(behind))
            lat_then_send(behind)

        @pl.when(jnp.logical_and(done >= 0, done < early))
        def _():
            await_lon(done, half_of(done))
            lon_last(done)

        @pl.when(jnp.logical_and(behind >= 0, behind < early))
        def _():
            send_lon(behind, half_of(behind))

        @pl.when(jnp.logical_and(behind >= early, behind < full))
        def _():
            await_far(behind, chunk_of(behind))
            lat_last(behind)

        @pl.when(k == 5)
        def _():
            learn()

        def give(group):
            pick(pl.multiple_of(group * 2 * CHUNK, 2 * CHUNK), 2 * CHUNK, group)
            send_back(group)

        @pl.when(jnp.logical_and(jnp.logical_and(done >= 0, done < early), done % 2 == 1))
        def _():
            give(done // 2)

        @pl.when(jnp.logical_and(jnp.logical_and(behind >= early, behind < full), behind % 2 == 1))
        def _():
            give(behind // 2)

        @pl.when(behind == full)
        def _():
            await_far(full, last)
            lat_rest()
            pick(full * CHUNK, rest, full // 2)
            send_back(full // 2)

        return carry

    lax.fori_loop(0, full + 3, stage, 0)
    got_ref[me] = pick_ref[me]

    def finish(k, part, half):
        swap(k, part).wait_send()

        @pl.when(onward)
        def _():
            forward(k, part).wait_send()

        to_right(k, half).wait_send()
        to_left(k, half).wait_send()

    def finish_full(k, carry):
        finish(k, chunk_of(k), half_of(k))
        return carry

    lax.fori_loop(0, full, finish_full, 0)
    finish(full, last, last_half)

    def collect(d, carry):
        other = (me + d) % devices
        whole = remote(
            pick_ref.at[other], got_ref.at[other], col_send.at[other], col_recv.at[other], place(other)
        )
        whole.wait_send()
        whole.wait_recv()
        return carry

    lax.fori_loop(1, devices, collect, 0)


def dense_step(control, col_dev, col_cell, std_dev, slots_each):
    lat, lon = lax.axis_size("lat"), lax.axis_size("lon")
    width, lat_rows, lon_cols = control.shape
    devices, rows = lat * lon, width * lat_rows
    pieces = rows // CHUNK + 1
    lanes = lane_tiles(width) * lon_cols
    listed = (1, lane_tiles(devices * slots_each) * 128)
    vmem, hbm = pl.BlockSpec(memory_space=pltpu.VMEM), pl.BlockSpec(memory_space=pltpu.HBM)
    dma = pltpu.SemaphoreType.DMA
    bf16, f32 = jnp.bfloat16, jnp.float32
    return pl.pallas_call(
        functools.partial(dense_kernel, lat, lon, lat_rows, slots_each),
        in_specs=[hbm] * 4,
        out_specs=[vmem, vmem, vmem],
        out_shape=[
            jax.ShapeDtypeStruct((rows, lon_cols), f32),
            jax.ShapeDtypeStruct((devices, *listed), jnp.int32),
            jax.ShapeDtypeStruct((devices, slots_each, lanes), bf16),
        ],
        scratch_shapes=[
            pltpu.VMEM((rows, lon_cols), f32),
            pltpu.VMEM((1, col_cell.shape[0]), jnp.int32),
            pltpu.VMEM((1, col_cell.shape[0]), jnp.int32),
            pltpu.SMEM(std_dev.shape, f32),
            pltpu.VMEM((1, *listed), jnp.int32),
            pltpu.VMEM((rows, lon_cols), bf16),
            pltpu.VMEM((rows, lon_cols), bf16),
            pltpu.VMEM((rows, lon_cols), bf16),
            pltpu.VMEM((rows, lon_cols), f32),
            *[pltpu.VMEM((rows // 2, lon_cols), bf16)] * 4,
            pltpu.VMEM((GROUP, 7 * GROUP), bf16),
            pltpu.VMEM((lon_cols, 2 * lon_cols), bf16),
            pltpu.VMEM((2, 2 * lon_cols, 2 * lon_cols), bf16),
            pltpu.VMEM((rows, lon_cols), f32),
            pltpu.VMEM((devices * 8, lon_cols), bf16),
            pltpu.VMEM((devices * 8, lon_cols), jnp.int32),
            pltpu.VMEM((devices, slots_each, lanes), bf16),
            *[dma((pieces,))] * 4,
            *[dma((2, pieces))] * 2,
            *[dma((devices,))] * 4,
            dma((pieces,)),
            dma((3,)),
            pltpu.SemaphoreType.REGULAR((2,)),
        ],
        compiler_params=pltpu.CompilerParams(collective_id=0, has_side_effects=True, vmem_limit_bytes=DENSE_VMEM),
        name="dense",
    )(control.reshape(rows, lon_cols), col_dev.reshape(1, -1), col_cell[None, :], std_dev)


def lane_tiles(count):
    return -(-count // 128)


PIECE = 16


def piece_slot(index, slots_each, piece, kind):
    device, row = index >> 4, index & (PIECE - 1)
    spare = PIECE - 2 * slots_each
    if kind < 2:
        number = row - kind * slots_each
        valid = jnp.logical_and(number >= 0, number < slots_each)
    else:
        number = row - 2 * slots_each + piece * spare
        valid = jnp.logical_and(row >= 2 * slots_each, number < slots_each)
    return jnp.where(valid, device * 8 + number, -1)


def sounding_part(
    slots_each, step,
    jac_hbm, got_ref, dev_ref, innov_ref, inv_ref, dep_ref, out_ref,
    jac_ref, apart_ref, col_ref, tail_ref, weight_ref, grad_ref, jac_sem,
):
    channels, count, width = jac_ref.shape
    steps = channels // step
    devices, lanes = got_ref.shape[0], got_ref.shape[2]
    most = width // 128 * 128
    iota = lambda shape, axis: lax.broadcasted_iota(jnp.int32, shape, axis)

    def load(b):
        part = pl.ds(b * step, step)
        return pltpu.make_async_copy(jac_hbm.at[part], jac_ref.at[part], jac_sem.at[b])

    def begin(b, carry):
        load(b).start()
        return carry

    lax.fori_loop(0, steps, begin, 0)
    apart_ref[...] = jnp.zeros_like(apart_ref)
    apart_ref[:, :slots_each, :] = got_ref[...].astype(jnp.float32)
    onehot, _, slot = slots_of(dev_ref, dev_ref, 8, devices * 8)
    onehot = jnp.where(onehot, 1.0, 0.0).astype(jnp.bfloat16)
    columns = matmul(onehot, apart_ref[...].reshape(devices * 8, lanes).astype(jnp.bfloat16))
    col_ref[...] = columns.astype(jnp.bfloat16)
    tail_ref[...] = columns[:, most:]
    grad_ref[...] = jnp.zeros_like(grad_ref)
    square = (count, count)

    def product(b):
        block = jac_ref[pl.ds(b * step, step), :, :most]
        return across(block.reshape(step * count, most), col_ref[:, :most])

    def depart(b, found):
        mine = iota(square, 0) == iota(square, 1)
        for k in range(step):
            channel = b * step + k
            own = jnp.where(mine, found[k * count:(k + 1) * count] - innov_ref[pl.ds(channel, 1), :], 0.0)
            if width > most:
                tail = jac_ref[channel, :, most:].astype(jnp.float32) * tail_ref[:, : width - most]
                own = own + jnp.concatenate([tail, jnp.zeros((count, count - (width - most)), jnp.float32)], axis=1)
            departure = jnp.sum(own, axis=1, keepdims=True)
            dep_ref[pl.ds(channel, 1), :] = jnp.sum(jnp.where(mine, departure, 0.0), axis=0, keepdims=True)
            weight = (departure * inv_ref[channel]).astype(jnp.bfloat16).astype(jnp.float32)
            weight_ref[k] = jnp.broadcast_to(weight, (count, 128))

    def gradient(b):
        for group in range(0, count, 16):
            part = slice(group, group + 16)
            for lane in range(0, width, 128):
                end = min(lane + 128, width)
                total = grad_ref[part, lane:end]
                for k in range(step):
                    values = jac_ref[b * step + k, part, lane:end].astype(jnp.float32)
                    total = total + values * weight_ref[k, part, : end - lane]
                grad_ref[part, lane:end] = total

    load(0).wait()
    depart(0, product(0))

    def body(b, carry):
        load(b).wait()
        found = product(b)
        gradient(b - 1)
        depart(b, found)
        return carry

    lax.fori_loop(1, steps, body, 0)
    gradient(steps - 1)
    grads = grad_ref[...].astype(jnp.bfloat16)
    for piece in range(2):
        packed = jnp.zeros((devices * PIECE, 128), jnp.float32)
        for kind in range(3):
            held = piece_slot(iota((devices * PIECE, count), 0), slots_each, piece, kind)
            onehot = jnp.where(held == slot, 1.0, 0.0).astype(jnp.bfloat16)
            tile = (2 * piece + kind if kind < 2 else 4) * 128
            packed = packed + matmul(onehot, grads[:, tile:tile + 128])
        out_ref[piece] = packed.astype(out_ref.dtype)


def adjoint_kernel(
    lat, lon, lat_rows, slots_each, cuts, step,
    jac_hbm, got_ref, dev_ref, innov_ref, inv_ref, table_ref, std_ref,
    dep_ref, out_ref,
    jac_ref, apart_ref, col_ref, tail_ref, scale_ref, grad_ref, jac_sem,
    give_ref, arrived_ref, compact_ref, grads_ref, weight_ref, std_row_ref,
    give_send, give_recv, swap_send, swap_recv, far_send, far_recv, lon_send, lon_recv,
):
    devices = lat * lon
    slots = devices * slots_each
    rows, lon_cols = out_ref.shape
    log_lon = lon_cols.bit_length() - 1
    row, column = lax.axis_index("lat"), lax.axis_index("lon")
    me = row * lon + column
    odd = row % 2
    near = 1 - 2 * odd
    partner, stride = row + near, 2 * near
    onward = jnp.logical_and(row + stride >= 0, row + stride < lat)
    comes = jnp.logical_and(row - stride >= 0, row - stride < lat)
    place = lambda other: (other // lon, other % lon)
    iota = lambda shape, axis: lax.broadcasted_iota(jnp.int32, shape, axis)
    chunks = range(len(cuts) - 1)
    part = [pl.ds(cuts[j], cuts[j + 1] - cuts[j]) for j in chunks]

    @pl.when(jnp.logical_not(comes))
    def _():
        grads_ref[2] = jnp.zeros_like(grads_ref[2])

    barrier = pltpu.get_barrier_semaphore()

    def greet(d, carry):
        pl.semaphore_signal(barrier, inc=1, device_id=place((me + d) % devices), device_id_type=MESH)
        return carry

    lax.fori_loop(1, devices, greet, 0)
    sounding_part(
        slots_each, step, jac_hbm, got_ref, dev_ref, innov_ref, inv_ref, dep_ref, give_ref,
        jac_ref, apart_ref, col_ref, tail_ref, scale_ref, grad_ref, jac_sem,
    )
    std_row_ref[...] = jnp.zeros_like(std_row_ref)
    std_row_ref[:, : std_ref.shape[0]] = std_ref[...].reshape(1, -1)

    def piece_of(d):
        return pl.ds(pl.multiple_of(d * PIECE, PIECE), PIECE)

    arrived_ref[:, piece_of(me), :] = give_ref[:, piece_of(me), :]
    pl.semaphore_wait(barrier, devices - 1)

    def remote(source, target, send, recv, device):
        return pltpu.make_async_remote_copy(
            src_ref=source, dst_ref=target, send_sem=send, recv_sem=recv, device_id=device, device_id_type=MESH
        )

    def hand(j, other, source):
        return remote(
            give_ref.at[j, piece_of(other)], arrived_ref.at[j, piece_of(source)],
            give_send.at[j, other], give_recv.at[j, source], place(other),
        )

    for j in range(2):

        def give(d, carry):
            hand(j, (me + d) % devices, me).start()
            return carry

        lax.fori_loop(1, devices, give, 0)

    total = 9 * slots
    flat = (1, total)
    at = iota(flat, 1).astype(jnp.float32)
    block = jnp.floor((at + 0.5) / slots)
    within = at - block * slots
    source = jnp.floor((within + 0.5) / slots_each)
    order = within - source * slots_each
    up = jnp.floor((block + 0.5) / 3.0)
    along = block - 3.0 * up
    lat_shift = jnp.where(up == 0.0, 0.0, jnp.where(up == 1.0, 1.0, -1.0)) * near.astype(jnp.float32)
    lon_shift = jnp.where(along == 0.0, 0.0, jnp.where(along == 1.0, -1.0, 1.0))
    owner_row = jnp.clip(row.astype(jnp.float32) + lat_shift, 0.0, lat - 1.0)
    owner_col = column.astype(jnp.float32) + lon_shift
    owner_col = jnp.where(owner_col < 0.0, owner_col + lon, jnp.where(owner_col >= lon, owner_col - lon, owner_col))
    wanted = ((owner_row * lon + owner_col) * slots_each + order).astype(jnp.int32)
    listed = table_ref[...].reshape(devices, table_ref.shape[2])
    chosen = jnp.where(iota((listed.shape[1], total), 0) == wanted, 1.0, 0.0).astype(jnp.bfloat16)
    mine = iota((devices, total), 0) == source.astype(jnp.int32)

    def position(values):
        found = matmul(values.astype(jnp.bfloat16), chosen)
        return jnp.sum(jnp.where(mine, found, 0.0), axis=0, keepdims=True)

    slot_row = position(listed >> log_lon) + lat_shift * lat_rows
    slot_col = position(listed & (lon_cols - 1)) + lon_shift * lon_cols
    down = iota((lon_cols, total), 0).astype(jnp.float32)
    col_weight = tap_value(slot_col - down, lon_cols // 2)
    for i in range(0, lat_rows, 2):
        for k in range(2):
            value = col_weight * tap_value(slot_row - (i + k), LHALF)
            high, low = halves(value)
            weight_ref[i // 2, k * lon_cols:(k + 1) * lon_cols, :] = high
            weight_ref[i // 2, (k + 2) * lon_cols:(k + 3) * lon_cols, :] = low

    spread = (slots, devices * PIECE)
    for at, (piece, kind) in enumerate(((0, 0), (0, 1), (0, 2), (1, 2))):
        held = piece_slot(iota(spread, 1), slots_each, piece, kind)
        wanted = jnp.where(held < 0, -1, (held >> 3) * slots_each + (held & 7))
        compact_ref[at] = jnp.where(wanted == iota(spread, 0), 1.0, 0.0).astype(jnp.bfloat16)

    def receive(j):
        def wait(d, carry):
            other = (me + d) % devices
            hand(j, other, other).wait_send()
            hand(j, other, other).wait_recv()
            return carry

        lax.fori_loop(1, devices, wait, 0)
        for kind in range(2):
            tile = (2 * j + kind) * 128
            grads_ref[0, 0, :, tile:tile + 128] = matmul(compact_ref[kind], arrived_ref[j]).astype(jnp.bfloat16)

    def receive_rest():
        rest = matmul(compact_ref[2], arrived_ref[0]) + matmul(compact_ref[3], arrived_ref[1])
        grads_ref[0, 0, :, part[2]] = rest.astype(jnp.bfloat16)

    def swap(j, b):
        return remote(
            grads_ref.at[0, b, :, part[j]], grads_ref.at[1, b, :, part[j]],
            swap_send.at[j, b], swap_recv.at[j, b], (partner, column),
        )

    def forward(j, b):
        return remote(
            grads_ref.at[1, b, :, part[j]], grads_ref.at[2, b, :, part[j]],
            far_send.at[j, b], far_recv.at[j, b], (row + stride, column),
        )

    def to_right(j, a):
        return remote(
            grads_ref.at[a, 0, :, part[j]], grads_ref.at[a, 1, :, part[j]],
            lon_send.at[0, j, a], lon_recv.at[0, j, a], (row, (column + 1) % lon),
        )

    def to_left(j, a):
        return remote(
            grads_ref.at[a, 0, :, part[j]], grads_ref.at[a, 2, :, part[j]],
            lon_send.at[1, j, a], lon_recv.at[1, j, a], (row, (column + lon - 1) % lon),
        )

    def send_lon(j, a):
        to_right(j, a).start()
        to_left(j, a).start()

    def await_lon(j, a):
        to_right(j, a).wait_recv()
        to_left(j, a).wait_recv()

    def pass_on(j, b):
        swap(j, b).wait_recv()

        @pl.when(onward)
        def _():
            forward(j, b).start()

    def await_far(j, b):
        @pl.when(comes)
        def _():
            forward(j, b).wait_recv()

    def compute(j):
        count = cuts[j + 1] - cuts[j]
        kept = min(count, rows // lat_rows - cuts[j])
        grads = grads_ref[:, :, :, part[j]].reshape(total, count)

        def two(i, carry):
            result = matmul(weight_ref[i], grads)
            result = (result[: 2 * lon_cols] + result[2 * lon_cols:]) * std_row_ref[:, part[j]]
            for k in range(2):
                piece = result[k * lon_cols:(k + 1) * lon_cols].T
                out_ref[pl.ds(cuts[j] * lat_rows + 2 * i + k, kept, stride=lat_rows), :] = piece[:kept]
            return carry

        lax.fori_loop(0, lat_rows // 2, two, 0)

    lon_first = (0, 2)
    receive(0)
    send_lon(0, 0)
    swap(0, 0).start()
    receive(1)
    swap(1, 0).start()
    receive_rest()
    send_lon(2, 0)
    swap(2, 0).start()
    pass_on(0, 0)
    await_lon(0, 0)
    swap(0, 1).start()
    swap(0, 2).start()
    pass_on(1, 0)
    send_lon(1, 0)
    send_lon(1, 1)
    pass_on(2, 0)
    await_lon(2, 0)
    swap(2, 1).start()
    swap(2, 2).start()
    await_far(1, 0)
    send_lon(1, 2)
    for j in lon_first:
        pass_on(j, 1)
        pass_on(j, 2)
    for j in chunks:
        if j in lon_first:
            for b in range(3):
                await_far(j, b)
        else:
            for a in range(3):
                await_lon(j, a)
        compute(j)
    for j in chunks:
        for b in range(3) if j in lon_first else (0,):
            swap(j, b).wait_send()

            @pl.when(onward)
            def _():
                forward(j, b).wait_send()

        for a in (0,) if j in lon_first else range(3):
            to_right(j, a).wait_send()
            to_left(j, a).wait_send()


def analysis_step(jacobian, got, table, col_dev, innovation, inv_error, std_dev, lat_rows, lon_cols):
    lat, lon = lax.axis_size("lat"), lax.axis_size("lon")
    count, channels, width = jacobian.shape
    devices, slots_each, lanes = got.shape
    slots, rows = devices * slots_each, width * lat_rows
    cuts = [0, 256, 512, lanes]
    pieces = len(cuts) - 1
    step = next(n for n in (10, 8, 6, 5, 4, 3, 2, 1) if channels % n == 0)
    vmem, hbm = pl.BlockSpec(memory_space=pltpu.VMEM), pl.BlockSpec(memory_space=pl.ANY)
    dma = pltpu.SemaphoreType.DMA
    bf16, f32 = jnp.bfloat16, jnp.float32
    departures, adjoint = pl.pallas_call(
        functools.partial(adjoint_kernel, lat, lon, lat_rows, slots_each, cuts, step),
        in_specs=[hbm, vmem, vmem, vmem, pl.BlockSpec(memory_space=pltpu.SMEM), vmem, vmem],
        out_specs=[vmem, vmem],
        out_shape=[
            jax.ShapeDtypeStruct((channels, count), f32),
            jax.ShapeDtypeStruct((rows, lon_cols), f32),
        ],
        scratch_shapes=[
            pltpu.VMEM((channels, count, width), bf16),
            pltpu.VMEM((devices, 8, lanes), f32),
            pltpu.VMEM((count, lanes), bf16),
            pltpu.VMEM((count, 128), f32),
            pltpu.VMEM((step, count, 128), f32),
            pltpu.VMEM((count, lanes), f32),
            dma((channels // step,)),
            pltpu.VMEM((2, devices * PIECE, 128), bf16),
            pltpu.VMEM((2, devices * PIECE, 128), bf16),
            pltpu.VMEM((4, slots, devices * PIECE), bf16),
            pltpu.VMEM((3, 3, slots, lanes), bf16),
            pltpu.VMEM((lat_rows // 2, 4 * lon_cols, 9 * slots), bf16),
            pltpu.VMEM((1, lanes), f32),
            *[dma((2, devices))] * 2,
            *[dma((pieces, 3))] * 4,
            *[dma((2, pieces, 3))] * 2,
        ],
        compiler_params=pltpu.CompilerParams(collective_id=1, has_side_effects=True, vmem_limit_bytes=VMEM),
        name="analysis",
    )(jnp.transpose(jacobian, (1, 0, 2)), got, col_dev.reshape(1, -1), innovation.T, inv_error, table, std_dev)
    return departures, adjoint


def local(control, std_dev, col_dev, col_cell, jacobian, innovation, inv_error):
    width, lat_rows, lon_cols = control.shape
    devices = lax.axis_size("lat") * lax.axis_size("lon")
    slots_each = max(2, 2 * col_cell.shape[0] // devices)
    increment, table, got = dense_step(control, col_dev, col_cell, std_dev, slots_each)
    departures, adjoint = analysis_step(
        jacobian, got, table, col_dev, innovation, inv_error, std_dev, lat_rows, lon_cols
    )
    return departures.T, increment.reshape(control.shape), adjoint.reshape(control.shape)


def solution(mesh):
    placed = (
        P(None, "lat", "lon"),
        P(),
        P(("lat", "lon"), None),
        P(("lat", "lon")),
        P(("lat", "lon"), None, None),
        P(("lat", "lon"), None),
        P(),
    )
    return jax.shard_map(
        local,
        mesh=mesh,
        in_specs=placed,
        out_specs=(P(("lat", "lon"), None), P(None, "lat", "lon"), P(None, "lat", "lon")),
        check_vma=False,
    )
```

```python
import functools
import math

import jax
import jax.numpy as jnp
from jax import lax
from jax.experimental import pallas as pl
from jax.experimental.pallas import tpu as pltpu
from jax.sharding import PartitionSpec as P

LHALF = 8
MESH = pl.DeviceIdType.MESH
VMEM = 48 << 20
DENSE_VMEM = 64300000


def tap_weights(offset, half_width):
    spread = 2.0 * half_width / 3.0
    taps = jnp.arange(-half_width, half_width + 1, dtype=jnp.int32).astype(jnp.float32)
    norm_total = jnp.sqrt(jnp.sum(jnp.exp(-taps * taps / (spread * spread))))
    weights = jnp.exp(-offset * offset / (2.0 * spread * spread)) / norm_total
    return jnp.where(jnp.abs(offset) <= half_width, weights, jnp.zeros_like(weights))


def halves(weights):
    high = weights.astype(jnp.bfloat16)
    return high, (weights - high.astype(jnp.float32)).astype(jnp.bfloat16)


def tap_value(offset, half_width):
    spread = 2.0 * half_width / 3.0
    norm_total = math.sqrt(sum(math.exp(-e * e / (spread * spread)) for e in range(-half_width, half_width + 1)))
    weights = jnp.exp(-offset * offset / (2.0 * spread * spread)) / norm_total
    return jnp.where(jnp.abs(offset) <= half_width, weights, 0.0)


GROUP = 256
CHUNK = 2 * GROUP


def matmul(left, right):
    return jnp.dot(left, right, preferred_element_type=jnp.float32)


def across(left, right):
    return lax.dot_general(left, right, (((1,), (1,)), ((), ())), preferred_element_type=jnp.float32)


def slots_of(dev_ref, cell_ref, slots_each, count):
    sound_count = dev_ref.shape[1]
    square = (sound_count, sound_count)
    iota = lambda shape, axis: lax.broadcasted_iota(jnp.int32, shape, axis)
    before = iota(square, 0) - iota(square, 1)
    across_lanes = jnp.broadcast_to(dev_ref[...].astype(jnp.float32), square)
    upright = lambda spread: jnp.sum(jnp.where(before == 0, spread, 0.0), axis=1, keepdims=True)
    down = upright(across_lanes)
    alike = across_lanes == down
    order = jnp.sum(jnp.where(jnp.logical_and(alike, before > 0), 1.0, 0.0), axis=1, keepdims=True)
    slot = down * slots_each + order
    onehot = slot.astype(jnp.int32) == iota((sound_count, count), 1)
    cell = upright(jnp.broadcast_to(cell_ref[...].astype(jnp.float32), square))
    order = jnp.sum(jnp.where(jnp.logical_and(alike, before < 0), 1.0, 0.0), axis=0, keepdims=True)
    return onehot, cell, (dev_ref[...].astype(jnp.float32) * slots_each + order).astype(jnp.int32)


def dense_kernel(
    lat, lon, lat_rows, slots_each,
    ctrl_hbm, dev_hbm, ask_hbm, std_hbm,
    inc_ref, table_ref, got_ref,
    ctrl_ref, dev_ref, ask_ref, std_ref, wanted_ref, own_ref, swap_ref, far_ref, g_ref, to_right_ref, to_left_ref, from_left_ref, from_right_ref,
    band_ref, mid_ref, edge_ref, std_row_ref, cell_ref, row_ref, pick_ref,
    swap_send, swap_recv, far_send, far_recv, lon_send, lon_recv,
    want_send, want_recv, col_send, col_recv, load_sem, small_sem, token_sem,
):
    rows, lon_cols = ctrl_ref.shape
    width = rows // lat_rows
    full, rest = rows // CHUNK, rows % CHUNK
    early = 2
    log_lat, log_lon = lat_rows.bit_length() - 1, lon_cols.bit_length() - 1
    lon_half = lon_cols // 2
    row, column = lax.axis_index("lat"), lax.axis_index("lon")
    devices, me = lat * lon, row * lon + column
    odd = row % 2
    partner, step = row + 1 - 2 * odd, 2 - 4 * odd
    onward = jnp.logical_and(row + step >= 0, row + step < lat)
    comes = jnp.logical_and(row - step >= 0, row - step < lat)
    place = lambda other: (other // lon, other % lon)
    iota = lambda shape, axis: lax.broadcasted_iota(jnp.int32, shape, axis)

    barrier = pltpu.get_barrier_semaphore()

    right, left = (row, (column + 1) % lon), (row, (column + lon - 1) % lon)

    def tell(semaphore, device):
        pl.semaphore_signal(semaphore, inc=1, device_id=device, device_id_type=MESH)

    for d in range(1, lat):
        tell(barrier, ((row + d) % lat, column))
    tell(barrier, right)
    tell(barrier, left)

    def chunk_of(k):
        return pl.ds(pl.multiple_of(k * CHUNK, CHUNK), CHUNK)

    def half_of(k):
        return pl.ds(pl.multiple_of(k * GROUP, GROUP), GROUP)

    last, last_half = pl.ds(full * CHUNK, rest), pl.ds(full * GROUP, rest // 2)

    def remote(source, target, send, recv, device):
        return pltpu.make_async_remote_copy(
            src_ref=source, dst_ref=target, send_sem=send, recv_sem=recv, device_id=device, device_id_type=MESH
        )

    def request(dst, send, recv, other):
        return remote(wanted_ref.at[0], table_ref.at[dst], want_send.at[send], want_recv.at[recv], place(other))

    def swap(k, part):
        return remote(own_ref.at[part], swap_ref.at[part], swap_send.at[k], swap_recv.at[k], (partner, column))

    def forward(k, part):
        return remote(swap_ref.at[part], far_ref.at[part], far_send.at[k], far_recv.at[k], (row + step, column))

    def to_right(k, part):
        return remote(
            to_right_ref.at[part], from_left_ref.at[part], lon_send.at[0, k], lon_recv.at[0, k],
            (row, (column + 1) % lon),
        )

    def to_left(k, part):
        return remote(
            to_left_ref.at[part], from_right_ref.at[part], lon_send.at[1, k], lon_recv.at[1, k],
            (row, (column + lon - 1) % lon),
        )

    def back(d, group):
        part = pl.ds(pl.multiple_of(group * lon_cols, lon_cols), lon_cols)
        return remote(
            pick_ref.at[d, :, part], got_ref.at[me, :, part], col_send.at[d], col_recv.at[me], place(d)
        )

    def round_own(part):
        own_ref[part, :] = ctrl_ref[part, :].astype(jnp.bfloat16)

    def load(k, part):
        return pltpu.make_async_copy(ctrl_hbm.at[part], ctrl_ref.at[part], load_sem.at[k])

    def begin(k, carry):
        load(k, chunk_of(k)).start()
        return carry

    small = [
        pltpu.make_async_copy(source, target, small_sem.at[at])
        for at, (source, target) in enumerate(((dev_hbm, dev_ref), (ask_hbm, ask_ref), (std_hbm, std_ref)))
    ]
    for copy in small:
        copy.start()
    lax.fori_loop(0, full, begin, 0)
    load(full, last).start()
    for copy in small:
        copy.wait()
    onehot, cell_at, _ = slots_of(dev_ref, ask_ref, slots_each, wanted_ref.shape[2])
    wanted_ref[0] = jnp.sum(jnp.where(onehot, cell_at, 0.0), axis=0, keepdims=True).astype(jnp.int32)

    @pl.when(jnp.logical_not(comes))
    def _():
        far_ref[...] = jnp.zeros_like(far_ref)

    load(0, chunk_of(0)).wait()
    round_own(chunk_of(0))
    pl.semaphore_wait(barrier, lat + 1)

    def pass_tokens():
        tell(token_sem.at[0], right)
        tell(token_sem.at[1], left)

    pass_tokens()

    def ask(d, carry):
        request(me, (me + d) % devices, me, (me + d) % devices).start()
        return carry


    def send_own(k, carry):
        load(k + 1, chunk_of(k + 1)).wait()

        @pl.when(k + 1 < early)
        def _():
            round_own(chunk_of(k + 1))

        swap(k, chunk_of(k)).start()
        return carry

    lax.fori_loop(0, early, send_own, 0)
    lane = iota((1, lon_cols), 1)

    def pack(first, second, part):
        right = jnp.where(lane < lon_half, pltpu.roll(first, lon_half, 1), second)
        left = jnp.where(lane < lon_half, first, pltpu.roll(second, lon_half, 1))
        to_right_ref[part, :] = right.astype(jnp.bfloat16)
        to_left_ref[part, :] = left.astype(jnp.bfloat16)

    def send_lon(k, part):
        to_right(k, part).start()
        to_left(k, part).start()

    def pack_own(k, carry):
        base = pl.multiple_of(k * CHUNK, CHUNK)
        pack(ctrl_ref[pl.ds(base, GROUP), :], ctrl_ref[pl.ds(base + GROUP, GROUP), :], half_of(k))

        @pl.when(k + 1 < full)
        def _():
            load(k + 1, chunk_of(k + 1)).wait()

        send_lon(k, half_of(k))
        return carry

    lax.fori_loop(early, full, pack_own, 0)
    load(full, last).wait()
    middle = full * CHUNK + rest // 2
    pack(ctrl_ref[full * CHUNK:middle, :], ctrl_ref[middle:, :], last_half)
    table_ref[me] = wanted_ref[0]
    send_lon(full, last_half)

    square = (GROUP, GROUP)
    same = (iota(square, 0) >> log_lat) == (iota(square, 1) >> log_lat)
    apart = (iota(square, 1) & (lat_rows - 1)) - (iota(square, 0) & (lat_rows - 1))

    def lat_band(shift):
        return halves(jnp.where(same, tap_value((apart + shift).astype(jnp.float32), LHALF), 0.0))

    high, low = lat_band(0)
    swap_high, swap_low = lat_band(lat_rows - 2 * lat_rows * odd)
    far_high, far_low = lat_band(2 * lat_rows * odd - lat_rows)
    for at, block in enumerate((high, high, low, swap_high, swap_low, far_high, far_low)):
        band_ref[:, at * GROUP:(at + 1) * GROUP] = block
    along = iota((lon_cols, lon_cols), 0) - iota((lon_cols, lon_cols), 1)
    high, low = halves(tap_value(along.astype(jnp.float32), lon_half))
    mid_ref[:, :lon_cols] = high
    mid_ref[:, lon_cols:] = low
    wide = (2 * lon_cols, 2 * lon_cols)
    source, target = iota(wide, 0), iota(wide, 1)
    within, which = source & (lon_half - 1), (source >> (log_lon - 1)) & 1
    column_at = jnp.where(source < lon_cols, within - lon_half, within + lon_cols)
    apart = column_at - (target & (lon_cols - 1))
    value = jnp.where(which == (target >> log_lon), tap_value(apart.astype(jnp.float32), lon_half), 0.0)
    high, low = halves(value)
    edge_ref[0] = high
    edge_ref[1] = low

    def spread(c, carry):
        std_row_ref[pl.ds(pl.multiple_of(c * lat_rows, lat_rows), lat_rows), :] = jnp.full(
            (lat_rows, lon_cols), std_ref[c], jnp.float32
        )
        return carry

    lax.fori_loop(0, width, spread, 0)

    def lat_product(ref, first, second):
        def pair(ref):
            return jnp.concatenate([ref[first, :], ref[second, :]], axis=1)

        field = pair(ref)
        field_high, field_low = halves(field)
        swapped, far = pair(swap_ref), pair(far_ref)
        stacked = jnp.concatenate([field_high, field_low, field_high, swapped, swapped, far, far], axis=0)
        return matmul(band_ref[...], stacked)

    def lat_then_send(k):
        base = pl.multiple_of(k * CHUNK, CHUNK)
        first, second = pl.ds(base, GROUP), pl.ds(base + GROUP, GROUP)
        result = lat_product(ctrl_ref, first, second)
        top, bottom = result[:, :lon_cols], result[:, lon_cols:]
        g_ref[first, :] = top
        g_ref[second, :] = bottom
        pack(top, bottom, half_of(k))

    def lat_last(k):
        base = pl.multiple_of(k * CHUNK, CHUNK)
        first, second = pl.ds(base, GROUP), pl.ds(base + GROUP, GROUP)
        result = lat_product(g_ref, first, second)
        inc_ref[first, :] = result[:, :lon_cols] * std_row_ref[first, :]
        inc_ref[second, :] = result[:, lon_cols:] * std_row_ref[second, :]

    def lat_rest():
        result = lat_product(g_ref, pl.ds(rows - CHUNK, GROUP), pl.ds(rows - GROUP, GROUP))
        kept = jnp.concatenate([result[:, :lon_cols], result[:, lon_cols:]], axis=0)[CHUNK - rest:]
        inc_ref[last, :] = kept * std_row_ref[last, :]

    def lon_product(ref, start, count, part):
        half = count // 2
        both = jnp.concatenate([from_left_ref[part, :], from_right_ref[part, :]], axis=1)
        sides = matmul(both, edge_ref[0]) + matmul(both, edge_ref[1])
        high, low = halves(ref[pl.ds(start, count), :])
        own = matmul(high, mid_ref[...])
        own = own[:, :lon_cols] + own[:, lon_cols:] + matmul(low, mid_ref[:, :lon_cols])
        return own[:half] + sides[:, :lon_cols], own[half:] + sides[:, lon_cols:]

    def lon_last(k):
        base = pl.multiple_of(k * CHUNK, CHUNK)
        first, second = pl.ds(base, GROUP), pl.ds(base + GROUP, GROUP)
        top, bottom = lon_product(g_ref, base, CHUNK, half_of(k))
        inc_ref[first, :] = top * std_row_ref[first, :]
        inc_ref[second, :] = bottom * std_row_ref[second, :]

    def lon_first(start, count, part):
        first, second = pl.ds(start, count // 2), pl.ds(start + count // 2, count // 2)
        top, bottom = lon_product(ctrl_ref, start, count, part)
        g_ref[first, :] = top
        g_ref[second, :] = bottom
        own_ref[first, :] = top.astype(jnp.bfloat16)
        own_ref[second, :] = bottom.astype(jnp.bfloat16)

    def pick(start, count, group):
        values = inc_ref[pl.ds(start, count), :].astype(jnp.bfloat16)
        found = across(cell_ref[...], values)
        mine = (iota(row_ref.shape, 1) & (lat_rows - 1)) == row_ref[...]
        parts = []
        for at in range(0, count, lon_cols):
            piece = found[:, at:at + lon_cols]
            parts.append(jnp.where(mine[:, : piece.shape[1]], piece, 0.0).astype(jnp.bfloat16))
        masked = jnp.concatenate(parts, axis=1)
        gather = (iota((count, lon_cols), 0) >> log_lat) == iota((count, lon_cols), 1)
        result = matmul(masked, jnp.where(gather, 1.0, 0.0).astype(jnp.bfloat16))
        result = result.reshape(devices, 8, lon_cols)[:, :slots_each, :]
        pick_ref[:, :, pl.ds(pl.multiple_of(group * lon_cols, lon_cols), lon_cols)] = result.astype(jnp.bfloat16)

    def send_back(group):
        def give(d, carry):
            back((me + d) % devices, group).start()
            return carry

        lax.fori_loop(1, devices, give, 0)

    def learn():
        def hear(d, carry):
            other = (me + d) % devices
            asked = request(other, other, other, other)
            asked.wait_send()
            asked.wait_recv()
            return carry

        lax.fori_loop(1, devices, hear, 0)
        listed = jnp.broadcast_to(table_ref[...].astype(jnp.float32), (devices, 8, table_ref.shape[2]))
        wants = iota(listed.shape, 2) == iota(listed.shape, 1) + me * slots_each
        cell = jnp.sum(jnp.where(wants, listed, 0.0), axis=2, keepdims=True).astype(jnp.int32)
        cell = jnp.broadcast_to(cell, (devices, 8, lon_cols)).reshape(devices * 8, lon_cols)
        row_ref[...] = cell >> log_lon
        cell_ref[...] = jnp.where((cell & (lon_cols - 1)) == iota(cell.shape, 1), 1.0, 0.0).astype(jnp.bfloat16)

    each = -(-(lon // 2) // 4)
    rounds = -(-(lon // 2) // each)

    def stage(k, carry):
        def arrive(k, part):
            swap(k, part).wait_recv()

            @pl.when(onward)
            def _():
                forward(k, part).start()

        def await_far(k, part):
            @pl.when(comes)
            def _():
                forward(k, part).wait_recv()

        @pl.when(k < full)
        def _():
            arrive(k, chunk_of(k))

        @pl.when(k == full)
        def _():
            arrive(full, last)

        @pl.when(k < rounds)
        def _():
            def step(n, carry):
                pl.semaphore_wait(token_sem.at[0], 1)
                pl.semaphore_wait(token_sem.at[1], 1)

                @pl.when(k * each + n + 1 < rounds * each)
                def _():
                    pass_tokens()

                return carry

            lax.fori_loop(0, each, step, 0)

        @pl.when(k == rounds - 1)
        def _():
            lax.fori_loop(1, devices, ask, 0)

        def await_lon(k, part):
            to_right(k, part).wait_recv()
            to_left(k, part).wait_recv()

        ahead, behind, done = k + early, k - 2, k - 4

        @pl.when(ahead < full)
        def _():
            await_lon(ahead, half_of(ahead))
            lon_first(pl.multiple_of(ahead * CHUNK, CHUNK), CHUNK, half_of(ahead))
            swap(ahead, chunk_of(ahead)).start()

        @pl.when(ahead == full)
        def _():
            await_lon(full, last_half)
            lon_first(full * CHUNK, rest, last_half)
            swap(full, last).start()

        @pl.when(jnp.logical_and(behind >= 0, behind < early))
        def _():
            await_far(behind, chunk_of(behind))
            lat_then_send(behind)

        @pl.when(jnp.logical_and(done >= 0, done < early))
        def _():
            await_lon(done, half_of(done))
            lon_last(done)

        @pl.when(jnp.logical_and(behind >= 0, behind < early))
        def _():
            send_lon(behind, half_of(behind))

        @pl.when(jnp.logical_and(behind >= early, behind < full))
        def _():
            await_far(behind, chunk_of(behind))
            lat_last(behind)

        @pl.when(k == 5)
        def _():
            learn()

        def give(group):
            pick(pl.multiple_of(group * 2 * CHUNK, 2 * CHUNK), 2 * CHUNK, group)
            send_back(group)

        @pl.when(jnp.logical_and(jnp.logical_and(done >= 0, done < early), done % 2 == 1))
        def _():
            give(done // 2)

        @pl.when(jnp.logical_and(jnp.logical_and(behind >= early, behind < full), behind % 2 == 1))
        def _():
            give(behind // 2)

        @pl.when(behind == full)
        def _():
            await_far(full, last)
            lat_rest()
            pick(full * CHUNK, rest, full // 2)
            send_back(full // 2)

        return carry

    lax.fori_loop(0, full + 3, stage, 0)
    got_ref[me] = pick_ref[me]

    def finish(k, part, half):
        swap(k, part).wait_send()

        @pl.when(onward)
        def _():
            forward(k, part).wait_send()

        to_right(k, half).wait_send()
        to_left(k, half).wait_send()

    def finish_full(k, carry):
        finish(k, chunk_of(k), half_of(k))
        return carry

    lax.fori_loop(0, full, finish_full, 0)
    finish(full, last, last_half)

    def collect(d, carry):
        other = (me + d) % devices
        whole = remote(
            pick_ref.at[other], got_ref.at[other], col_send.at[other], col_recv.at[other], place(other)
        )
        whole.wait_send()
        whole.wait_recv()
        return carry

    lax.fori_loop(1, devices, collect, 0)


def dense_step(control, col_dev, col_cell, std_dev, slots_each):
    lat, lon = lax.axis_size("lat"), lax.axis_size("lon")
    width, lat_rows, lon_cols = control.shape
    devices, rows = lat * lon, width * lat_rows
    pieces = rows // CHUNK + 1
    lanes = lane_tiles(width) * lon_cols
    listed = (1, lane_tiles(devices * slots_each) * 128)
    vmem, hbm = pl.BlockSpec(memory_space=pltpu.VMEM), pl.BlockSpec(memory_space=pltpu.HBM)
    dma = pltpu.SemaphoreType.DMA
    bf16, f32 = jnp.bfloat16, jnp.float32
    return pl.pallas_call(
        functools.partial(dense_kernel, lat, lon, lat_rows, slots_each),
        in_specs=[hbm] * 4,
        out_specs=[vmem, vmem, vmem],
        out_shape=[
            jax.ShapeDtypeStruct((rows, lon_cols), f32),
            jax.ShapeDtypeStruct((devices, *listed), jnp.int32),
            jax.ShapeDtypeStruct((devices, slots_each, lanes), bf16),
        ],
        scratch_shapes=[
            pltpu.VMEM((rows, lon_cols), f32),
            pltpu.VMEM((1, col_cell.shape[0]), jnp.int32),
            pltpu.VMEM((1, col_cell.shape[0]), jnp.int32),
            pltpu.SMEM(std_dev.shape, f32),
            pltpu.VMEM((1, *listed), jnp.int32),
            pltpu.VMEM((rows, lon_cols), bf16),
            pltpu.VMEM((rows, lon_cols), bf16),
            pltpu.VMEM((rows, lon_cols), bf16),
            pltpu.VMEM((rows, lon_cols), f32),
            *[pltpu.VMEM((rows // 2, lon_cols), bf16)] * 4,
            pltpu.VMEM((GROUP, 7 * GROUP), bf16),
            pltpu.VMEM((lon_cols, 2 * lon_cols), bf16),
            pltpu.VMEM((2, 2 * lon_cols, 2 * lon_cols), bf16),
            pltpu.VMEM((rows, lon_cols), f32),
            pltpu.VMEM((devices * 8, lon_cols), bf16),
            pltpu.VMEM((devices * 8, lon_cols), jnp.int32),
            pltpu.VMEM((devices, slots_each, lanes), bf16),
            *[dma((pieces,))] * 4,
            *[dma((2, pieces))] * 2,
            *[dma((devices,))] * 4,
            dma((pieces,)),
            dma((3,)),
            pltpu.SemaphoreType.REGULAR((2,)),
        ],
        compiler_params=pltpu.CompilerParams(collective_id=0, has_side_effects=True, vmem_limit_bytes=DENSE_VMEM),
        name="dense",
    )(control.reshape(rows, lon_cols), col_dev.reshape(1, -1), col_cell[None, :], std_dev)


def lane_tiles(count):
    return -(-count // 128)


PIECE = 16


def piece_slot(index, slots_each, piece, kind):
    device, row = index >> 4, index & (PIECE - 1)
    spare = PIECE - 2 * slots_each
    if kind < 2:
        number = row - kind * slots_each
        valid = jnp.logical_and(number >= 0, number < slots_each)
    else:
        number = row - 2 * slots_each + piece * spare
        valid = jnp.logical_and(row >= 2 * slots_each, number < slots_each)
    return jnp.where(valid, device * 8 + number, -1)


def sounding_part(
    slots_each, step,
    jac_hbm, got_ref, dev_ref, innov_ref, inv_ref, dep_ref, out_ref,
    jac_ref, apart_ref, col_ref, tail_ref, weight_ref, grad_ref, jac_sem,
):
    channels, count, width = jac_ref.shape
    steps = channels // step
    devices, lanes = got_ref.shape[0], got_ref.shape[2]
    most = width // 128 * 128
    iota = lambda shape, axis: lax.broadcasted_iota(jnp.int32, shape, axis)

    def load(b):
        part = pl.ds(b * step, step)
        return pltpu.make_async_copy(jac_hbm.at[part], jac_ref.at[part], jac_sem.at[b])

    def begin(b, carry):
        load(b).start()
        return carry

    lax.fori_loop(0, steps, begin, 0)
    apart_ref[...] = jnp.zeros_like(apart_ref)
    apart_ref[:, :slots_each, :] = got_ref[...].astype(jnp.float32)
    onehot, _, slot = slots_of(dev_ref, dev_ref, 8, devices * 8)
    onehot = jnp.where(onehot, 1.0, 0.0).astype(jnp.bfloat16)
    columns = matmul(onehot, apart_ref[...].reshape(devices * 8, lanes).astype(jnp.bfloat16))
    col_ref[...] = columns.astype(jnp.bfloat16)
    tail_ref[...] = columns[:, most:]
    grad_ref[...] = jnp.zeros_like(grad_ref)
    square = (count, count)

    def product(b):
        block = jac_ref[pl.ds(b * step, step), :, :most]
        return across(block.reshape(step * count, most), col_ref[:, :most])

    def depart(b, found):
        mine = iota(square, 0) == iota(square, 1)
        for k in range(step):
            channel = b * step + k
            own = jnp.where(mine, found[k * count:(k + 1) * count] - innov_ref[pl.ds(channel, 1), :], 0.0)
            if width > most:
                tail = jac_ref[channel, :, most:].astype(jnp.float32) * tail_ref[:, : width - most]
                own = own + jnp.concatenate([tail, jnp.zeros((count, count - (width - most)), jnp.float32)], axis=1)
            departure = jnp.sum(own, axis=1, keepdims=True)
            dep_ref[pl.ds(channel, 1), :] = jnp.sum(jnp.where(mine, departure, 0.0), axis=0, keepdims=True)
            weight = (departure * inv_ref[channel]).astype(jnp.bfloat16).astype(jnp.float32)
            weight_ref[k] = jnp.broadcast_to(weight, (count, 128))

    def gradient(b):
        for group in range(0, count, 16):
            part = slice(group, group + 16)
            for lane in range(0, width, 128):
                end = min(lane + 128, width)
                total = grad_ref[part, lane:end]
                for k in range(step):
                    values = jac_ref[b * step + k, part, lane:end].astype(jnp.float32)
                    total = total + values * weight_ref[k, part, : end - lane]
                grad_ref[part, lane:end] = total

    load(0).wait()
    depart(0, product(0))

    def body(b, carry):
        load(b).wait()
        found = product(b)
        gradient(b - 1)
        depart(b, found)
        return carry

    lax.fori_loop(1, steps, body, 0)
    gradient(steps - 1)
    grads = grad_ref[...].astype(jnp.bfloat16)
    for piece in range(2):
        packed = jnp.zeros((devices * PIECE, 128), jnp.float32)
        for kind in range(3):
            held = piece_slot(iota((devices * PIECE, count), 0), slots_each, piece, kind)
            onehot = jnp.where(held == slot, 1.0, 0.0).astype(jnp.bfloat16)
            tile = (2 * piece + kind if kind < 2 else 4) * 128
            packed = packed + matmul(onehot, grads[:, tile:tile + 128])
        out_ref[piece] = packed.astype(out_ref.dtype)


def adjoint_kernel(
    lat, lon, lat_rows, slots_each, cuts, step,
    jac_hbm, got_ref, dev_ref, innov_ref, inv_ref, table_ref, std_ref,
    dep_ref, out_ref,
    jac_ref, apart_ref, col_ref, tail_ref, scale_ref, grad_ref, jac_sem,
    give_ref, arrived_ref, compact_ref, grads_ref, weight_ref, std_row_ref,
    give_send, give_recv, swap_send, swap_recv, far_send, far_recv, lon_send, lon_recv,
):
    devices = lat * lon
    slots = devices * slots_each
    rows, lon_cols = out_ref.shape
    log_lon = lon_cols.bit_length() - 1
    row, column = lax.axis_index("lat"), lax.axis_index("lon")
    me = row * lon + column
    odd = row % 2
    near = 1 - 2 * odd
    partner, stride = row + near, 2 * near
    onward = jnp.logical_and(row + stride >= 0, row + stride < lat)
    comes = jnp.logical_and(row - stride >= 0, row - stride < lat)
    place = lambda other: (other // lon, other % lon)
    iota = lambda shape, axis: lax.broadcasted_iota(jnp.int32, shape, axis)
    chunks = range(len(cuts) - 1)
    part = [pl.ds(cuts[j], cuts[j + 1] - cuts[j]) for j in chunks]

    @pl.when(jnp.logical_not(comes))
    def _():
        grads_ref[2] = jnp.zeros_like(grads_ref[2])

    barrier = pltpu.get_barrier_semaphore()

    def greet(d, carry):
        pl.semaphore_signal(barrier, inc=1, device_id=place((me + d) % devices), device_id_type=MESH)
        return carry

    lax.fori_loop(1, devices, greet, 0)
    sounding_part(
        slots_each, step, jac_hbm, got_ref, dev_ref, innov_ref, inv_ref, dep_ref, give_ref,
        jac_ref, apart_ref, col_ref, tail_ref, scale_ref, grad_ref, jac_sem,
    )
    std_row_ref[...] = jnp.zeros_like(std_row_ref)
    std_row_ref[:, : std_ref.shape[0]] = std_ref[...].reshape(1, -1)

    def piece_of(d):
        return pl.ds(pl.multiple_of(d * PIECE, PIECE), PIECE)

    arrived_ref[:, piece_of(me), :] = give_ref[:, piece_of(me), :]
    pl.semaphore_wait(barrier, devices - 1)

    def remote(source, target, send, recv, device):
        return pltpu.make_async_remote_copy(
            src_ref=source, dst_ref=target, send_sem=send, recv_sem=recv, device_id=device, device_id_type=MESH
        )

    def hand(j, other, source):
        return remote(
            give_ref.at[j, piece_of(other)], arrived_ref.at[j, piece_of(source)],
            give_send.at[j, other], give_recv.at[j, source], place(other),
        )

    for j in range(2):

        def give(d, carry):
            hand(j, (me + d) % devices, me).start()
            return carry

        lax.fori_loop(1, devices, give, 0)

    total = 9 * slots
    flat = (1, total)
    at = iota(flat, 1).astype(jnp.float32)
    block = jnp.floor((at + 0.5) / slots)
    within = at - block * slots
    source = jnp.floor((within + 0.5) / slots_each)
    order = within - source * slots_each
    up = jnp.floor((block + 0.5) / 3.0)
    along = block - 3.0 * up
    lat_shift = jnp.where(up == 0.0, 0.0, jnp.where(up == 1.0, 1.0, -1.0)) * near.astype(jnp.float32)
    lon_shift = jnp.where(along == 0.0, 0.0, jnp.where(along == 1.0, -1.0, 1.0))
    owner_row = jnp.clip(row.astype(jnp.float32) + lat_shift, 0.0, lat - 1.0)
    owner_col = column.astype(jnp.float32) + lon_shift
    owner_col = jnp.where(owner_col < 0.0, owner_col + lon, jnp.where(owner_col >= lon, owner_col - lon, owner_col))
    wanted = ((owner_row * lon + owner_col) * slots_each + order).astype(jnp.int32)
    listed = table_ref[...].reshape(devices, table_ref.shape[2])
    chosen = jnp.where(iota((listed.shape[1], total), 0) == wanted, 1.0, 0.0).astype(jnp.bfloat16)
    mine = iota((devices, total), 0) == source.astype(jnp.int32)

    def position(values):
        found = matmul(values.astype(jnp.bfloat16), chosen)
        return jnp.sum(jnp.where(mine, found, 0.0), axis=0, keepdims=True)

    slot_row = position(listed >> log_lon) + lat_shift * lat_rows
    slot_col = position(listed & (lon_cols - 1)) + lon_shift * lon_cols
    down = iota((lon_cols, total), 0).astype(jnp.float32)
    col_weight = tap_value(slot_col - down, lon_cols // 2)
    for i in range(0, lat_rows, 2):
        for k in range(2):
            value = col_weight * tap_value(slot_row - (i + k), LHALF)
            high, low = halves(value)
            weight_ref[i // 2, k * lon_cols:(k + 1) * lon_cols, :] = high
            weight_ref[i // 2, (k + 2) * lon_cols:(k + 3) * lon_cols, :] = low

    spread = (slots, devices * PIECE)
    for at, (piece, kind) in enumerate(((0, 0), (0, 1), (0, 2), (1, 2))):
        held = piece_slot(iota(spread, 1), slots_each, piece, kind)
        wanted = jnp.where(held < 0, -1, (held >> 3) * slots_each + (held & 7))
        compact_ref[at] = jnp.where(wanted == iota(spread, 0), 1.0, 0.0).astype(jnp.bfloat16)

    def receive(j):
        def wait(d, carry):
            other = (me + d) % devices
            hand(j, other, other).wait_send()
            hand(j, other, other).wait_recv()
            return carry

        lax.fori_loop(1, devices, wait, 0)
        for kind in range(2):
            tile = (2 * j + kind) * 128
            grads_ref[0, 0, :, tile:tile + 128] = matmul(compact_ref[kind], arrived_ref[j]).astype(jnp.bfloat16)

    def receive_rest():
        rest = matmul(compact_ref[2], arrived_ref[0]) + matmul(compact_ref[3], arrived_ref[1])
        grads_ref[0, 0, :, part[2]] = rest.astype(jnp.bfloat16)

    def swap(j, b):
        return remote(
            grads_ref.at[0, b, :, part[j]], grads_ref.at[1, b, :, part[j]],
            swap_send.at[j, b], swap_recv.at[j, b], (partner, column),
        )

    def forward(j, b):
        return remote(
            grads_ref.at[1, b, :, part[j]], grads_ref.at[2, b, :, part[j]],
            far_send.at[j, b], far_recv.at[j, b], (row + stride, column),
        )

    def to_right(j, a):
        return remote(
            grads_ref.at[a, 0, :, part[j]], grads_ref.at[a, 1, :, part[j]],
            lon_send.at[0, j, a], lon_recv.at[0, j, a], (row, (column + 1) % lon),
        )

    def to_left(j, a):
        return remote(
            grads_ref.at[a, 0, :, part[j]], grads_ref.at[a, 2, :, part[j]],
            lon_send.at[1, j, a], lon_recv.at[1, j, a], (row, (column + lon - 1) % lon),
        )

    def send_lon(j, a):
        to_right(j, a).start()
        to_left(j, a).start()

    def await_lon(j, a):
        to_right(j, a).wait_recv()
        to_left(j, a).wait_recv()

    def pass_on(j, b):
        swap(j, b).wait_recv()

        @pl.when(onward)
        def _():
            forward(j, b).start()

    def await_far(j, b):
        @pl.when(comes)
        def _():
            forward(j, b).wait_recv()

    def compute(j):
        count = cuts[j + 1] - cuts[j]
        kept = min(count, rows // lat_rows - cuts[j])
        grads = grads_ref[:, :, :, part[j]].reshape(total, count)

        def two(i, carry):
            result = matmul(weight_ref[i], grads)
            result = (result[: 2 * lon_cols] + result[2 * lon_cols:]) * std_row_ref[:, part[j]]
            for k in range(2):
                piece = result[k * lon_cols:(k + 1) * lon_cols].T
                out_ref[pl.ds(cuts[j] * lat_rows + 2 * i + k, kept, stride=lat_rows), :] = piece[:kept]
            return carry

        lax.fori_loop(0, lat_rows // 2, two, 0)

    lon_first = (0, 2)
    receive(0)
    send_lon(0, 0)
    swap(0, 0).start()
    receive(1)
    swap(1, 0).start()
    receive_rest()
    send_lon(2, 0)
    pass_on(0, 0)
    await_lon(0, 0)
    swap(0, 1).start()
    swap(0, 2).start()
    pass_on(1, 0)
    send_lon(1, 0)
    send_lon(1, 1)
    swap(2, 0).start()
    await_lon(2, 0)
    swap(2, 1).start()
    swap(2, 2).start()
    await_far(1, 0)
    send_lon(1, 2)
    for j, b in ((0, 1), (0, 2), (2, 0), (2, 1), (2, 2)):
        pass_on(j, b)
    for b in range(3):
        await_far(0, b)
    compute(0)
    for b in range(3):
        await_far(2, b)
    compute(2)
    for a in range(3):
        await_lon(1, a)
    compute(1)
    for j in chunks:
        for b in range(3) if j in lon_first else (0,):
            swap(j, b).wait_send()

            @pl.when(onward)
            def _():
                forward(j, b).wait_send()

        for a in (0,) if j in lon_first else range(3):
            to_right(j, a).wait_send()
            to_left(j, a).wait_send()


def analysis_step(jacobian, got, table, col_dev, innovation, inv_error, std_dev, lat_rows, lon_cols):
    lat, lon = lax.axis_size("lat"), lax.axis_size("lon")
    count, channels, width = jacobian.shape
    devices, slots_each, lanes = got.shape
    slots, rows = devices * slots_each, width * lat_rows
    cuts = [0, 256, 512, lanes]
    pieces = len(cuts) - 1
    step = next(n for n in (10, 8, 6, 5, 4, 3, 2, 1) if channels % n == 0)
    vmem, hbm = pl.BlockSpec(memory_space=pltpu.VMEM), pl.BlockSpec(memory_space=pl.ANY)
    dma = pltpu.SemaphoreType.DMA
    bf16, f32 = jnp.bfloat16, jnp.float32
    departures, adjoint = pl.pallas_call(
        functools.partial(adjoint_kernel, lat, lon, lat_rows, slots_each, cuts, step),
        in_specs=[hbm, vmem, vmem, vmem, pl.BlockSpec(memory_space=pltpu.SMEM), vmem, vmem],
        out_specs=[vmem, vmem],
        out_shape=[
            jax.ShapeDtypeStruct((channels, count), f32),
            jax.ShapeDtypeStruct((rows, lon_cols), f32),
        ],
        scratch_shapes=[
            pltpu.VMEM((channels, count, width), bf16),
            pltpu.VMEM((devices, 8, lanes), f32),
            pltpu.VMEM((count, lanes), bf16),
            pltpu.VMEM((count, 128), f32),
            pltpu.VMEM((step, count, 128), f32),
            pltpu.VMEM((count, lanes), f32),
            dma((channels // step,)),
            pltpu.VMEM((2, devices * PIECE, 128), bf16),
            pltpu.VMEM((2, devices * PIECE, 128), bf16),
            pltpu.VMEM((4, slots, devices * PIECE), bf16),
            pltpu.VMEM((3, 3, slots, lanes), bf16),
            pltpu.VMEM((lat_rows // 2, 4 * lon_cols, 9 * slots), bf16),
            pltpu.VMEM((1, lanes), f32),
            *[dma((2, devices))] * 2,
            *[dma((pieces, 3))] * 4,
            *[dma((2, pieces, 3))] * 2,
        ],
        compiler_params=pltpu.CompilerParams(collective_id=1, has_side_effects=True, vmem_limit_bytes=VMEM),
        name="analysis",
    )(jnp.transpose(jacobian, (1, 0, 2)), got, col_dev.reshape(1, -1), innovation.T, inv_error, table, std_dev)
    return departures, adjoint


def local(control, std_dev, col_dev, col_cell, jacobian, innovation, inv_error):
    width, lat_rows, lon_cols = control.shape
    devices = lax.axis_size("lat") * lax.axis_size("lon")
    slots_each = max(2, 2 * col_cell.shape[0] // devices)
    increment, table, got = dense_step(control, col_dev, col_cell, std_dev, slots_each)
    departures, adjoint = analysis_step(
        jacobian, got, table, col_dev, innovation, inv_error, std_dev, lat_rows, lon_cols
    )
    return departures.T, increment.reshape(control.shape), adjoint.reshape(control.shape)


def solution(mesh):
    placed = (
        P(None, "lat", "lon"),
        P(),
        P(("lat", "lon"), None),
        P(("lat", "lon")),
        P(("lat", "lon"), None, None),
        P(("lat", "lon"), None),
        P(),
    )
    return jax.shard_map(
        local,
        mesh=mesh,
        in_specs=placed,
        out_specs=(P(("lat", "lon"), None), P(None, "lat", "lon"), P(None, "lat", "lon")),
        check_vma=False,
    )
```
